256 devices in a mesh: space: 32 (over z, y_lo, core), mem: 8 (over x, y_hi).
Axes of the slice: x: 4, y: 4 (y_hi: 2, y_lo: 2; y = y_hi * 2 + y_lo), z: 8, core: 2. Of those that a mesh axis runs over, the one named last changes fastest.
Arguments:
- members: bfloat16 [1024, 768, 2, 384], P(('space', 'mem')), may hold values from -24 to 24
- state: float32 [768, 2, 384], P('space'), may hold values from -6 to 6
- cotangent: float32 [768, 2, 384], P('space'), may hold values from -6 to 6
- conv_in: float32 [3, 3, 128, 2], replicated, may hold values from -1.5 to 1.5
- conv_out: float32 [3, 3, 2, 128], replicated, may hold values from -0.1875 to 0.1875
- bias: float32 [128], replicated, may hold values from -3 to 3
Outputs:
- increment: float32 [768, 2, 384], P('space')
- response: float32 [768, 2, 384], P('space')
The draws below stay inside these ranges and needn't reach their ends.
All inputs are finite; a program needn't handle non-finite values.
Results may differ from the reference program's by a relative error of at most 0.0045.
Values may be sent and summed in bfloat16 or wider, within the bound.
No kernel may reach another device: no remote copies, remote signals or barrier semaphores. Data moves between devices by JAX's collectives and lax.ppermute only.
A program may use at most 64 MiB of HBM per device.

```python
import jax
import jax.numpy as jnp
from jax import lax

LAT = 384
HID = 128
VARS = 2
HALF = 16
LON = 768
MEMBERS = 1024


def strengthened(drawn, own_key, source, target, shards_of, factor):
    owner, partner = [(jnp.arange(drawn.shape[axis_at]) // (drawn.shape[axis_at] // shards_of)).reshape([-1 if axis == axis_at else 1 for axis in range(drawn.ndim)]) for axis_at in (source, target)]
    chosen = jax.random.permutation(own_key, shards_of)[partner]
    strong = (owner == chosen) | (owner == (partner + shards_of // 2) % shards_of)
    return jnp.where(strong, factor * drawn, drawn)


def block_scale(rng, shape, shards, low, largest):
    level = 1.0
    for dim, parts in shards:
        steps = jax.random.uniform(jax.random.fold_in(jax.random.fold_in(rng, 6), dim), (parts,), jnp.float32, low / len(shards), largest / len(shards))
        level = level * jnp.repeat(jnp.exp(steps), shape[dim] // parts).reshape((-1,) + (1,) * (len(shape) - 1 - dim))
    return level


def centred(rng, shape, scale, limit, shards=(), kind=jnp.bfloat16):
    result = scale * jax.random.normal(rng, shape, jnp.float32)
    if shards:
        result = result * block_scale(rng, shape, shards, -0.22, 0.18)
    return jnp.clip(result, -limit, limit).astype(kind)


def gaussian_with(stream_key, shape, scale, reach, pieces, heavy, dtype=jnp.bfloat16):
    drawn = scale * jax.random.normal(stream_key, shape, jnp.float32)
    if pieces:
        drawn = drawn * block_scale(stream_key, shape, pieces, -0.22, 0.18)
    return jnp.clip(strengthened(drawn, jax.random.fold_in(stream_key, 3), *heavy), -reach, reach).astype(dtype)


def setup_inputs(seed: int = 0) -> dict:
    splits = jax.random.split(jax.random.key(seed), 7)
    return {
        "members": gaussian_with(splits[0], (MEMBERS, LON, VARS, LAT), 1.0, 24.0, ((0, 256),), (0, 1, 256, 6.0)),
        "state": centred(splits[1], (LON, VARS, LAT), 1.0, 6.0, ((0, 32),), jnp.float32),
        "cotangent": centred(splits[2], (LON, VARS, LAT), 1.0, 6.0, ((0, 32),), jnp.float32),
        "conv_in": centred(splits[3], (3, 3, HID, VARS), (9 * VARS) ** -0.5, 1.5, (), jnp.float32),
        "conv_out": centred(splits[4], (3, 3, VARS, HID), (9 * HID) ** -0.5, 0.1875, (), jnp.float32),
        "bias": centred(splits[5], (HID,), 0.5, 3.0, (), jnp.float32),
    }


def wrap_lon(field):
    return jnp.concatenate([field[-1:], field, field[:1]], axis=0)


def convolve(field, weight):
    padded = jnp.pad(wrap_lon(field), ((0, 0), (0, 0), (1, 1)))
    row_count = field.shape[0]
    lat_count = field.shape[2]
    summed = jnp.zeros((row_count, weight.shape[2], lat_count), jnp.float32)
    for step_lon in range(3):
        for step_lat in range(3):
            window = padded[step_lon:step_lon + row_count, :, step_lat:step_lat + lat_count]
            summed = summed + jnp.einsum("oc,xcy->xoy", weight[step_lon, step_lat], window, precision=lax.Precision.HIGHEST)
    return summed


def flipped(weight):
    return jnp.transpose(weight[::-1, ::-1], (0, 1, 3, 2))


def band_matrix(count, wrap):
    row_index = jnp.arange(count)[:, None]
    col_index = jnp.arange(count)[None, :]
    distance = jnp.abs(row_index - col_index)
    if wrap:
        distance = jnp.minimum(distance, count - distance)
    ratio = distance.astype(jnp.float32) / (HALF + 1.0)
    return jnp.where(distance <= HALF, 1.0 - ratio * ratio, 0.0).astype(jnp.bfloat16)


def reference(members, state, cotangent, conv_in, conv_out, bias):
    activity = jnp.tanh(convolve(state, conv_in) + bias[None, :, None])
    slopes = 1.0 - activity * activity
    backward = slopes * convolve(cotangent, flipped(conv_out))
    gradient = (cotangent + convolve(backward, flipped(conv_in))).astype(jnp.bfloat16)
    lat_loc = band_matrix(LAT, False).astype(jnp.float32)
    lon_loc = band_matrix(LON, True).astype(jnp.float32)
    grad_wide = gradient.astype(jnp.float32)

    def member_step(carry, member):
        member_wide = member.astype(jnp.float32)
        product = (member_wide * grad_wide).astype(jnp.bfloat16).astype(jnp.float32)
        banded = jnp.einsum("xcy,yz->xcz", product, lat_loc, precision=lax.Precision.HIGHEST).astype(jnp.bfloat16).astype(jnp.float32)
        spread = jnp.einsum("zx,xcy->zcy", lon_loc, banded, precision=lax.Precision.HIGHEST)
        return carry + member_wide * spread, None

    start_sum = jnp.zeros(state.shape, jnp.float32)
    summed, unused = lax.scan(member_step, start_sum, members)
    increment = summed / (MEMBERS - 1.0)
    tangent_hidden = slopes * convolve(increment, conv_in)
    response = increment + convolve(tangent_hidden, conv_out)
    return increment, response
```

```python
import jax
import jax.numpy as jnp
from jax import lax
from jax.sharding import PartitionSpec as P

HALF = 16


def convolve(padded, weight):
    row_count = padded.shape[0] - 2
    lat_count = padded.shape[2]
    out_count = weight.shape[2]
    in_count = weight.shape[3]
    if out_count <= in_count:
        flattened = weight.reshape(9 * out_count, in_count)
        product = jnp.einsum(
            "kc,xcy->xky",
            flattened,
            padded,
            precision=lax.Precision.HIGHEST,
            preferred_element_type=jnp.float32,
        )
        product = jnp.pad(product, ((0, 0), (0, 0), (1, 1)))
        summed = jnp.zeros((row_count, out_count, lat_count), jnp.float32)
        for step_lon in range(3):
            for step_lat in range(3):
                tap_index = step_lon * 3 + step_lat
                summed = (
                    summed
                    + product[
                        step_lon : step_lon + row_count,
                        tap_index * out_count : (tap_index + 1) * out_count,
                        step_lat : step_lat + lat_count,
                    ]
                )
        return summed
    lat_padded = jnp.pad(padded, ((0, 0), (0, 0), (1, 1)))
    stacked = jnp.concatenate(
        [
            lat_padded[step_lon : step_lon + row_count, :, step_lat : step_lat + lat_count]
            for step_lon in range(3)
            for step_lat in range(3)
        ],
        axis=1,
    )
    flattened = jnp.transpose(weight, (2, 0, 1, 3)).reshape(out_count, 9 * in_count)
    return jnp.einsum(
        "ok,xky->xoy",
        flattened,
        stacked,
        precision=lax.Precision.HIGHEST,
        preferred_element_type=jnp.float32,
    )


def flipped(weight):
    return jnp.transpose(weight[::-1, ::-1], (0, 1, 3, 2))


def band_matrix(count, wrap):
    row_index = jnp.arange(count)[:, None]
    col_index = jnp.arange(count)[None, :]
    distance = jnp.abs(row_index - col_index)
    if wrap:
        distance = jnp.minimum(distance, count - distance)
    ratio = distance.astype(jnp.float32) / (HALF + 1.0)
    return jnp.where(distance <= HALF, 1.0 - ratio * ratio, 0.0).astype(jnp.bfloat16)


def per_device(members, state, cotangent, conv_in, conv_out, bias):
    blocks = lax.axis_size("space")
    groups = lax.axis_size("mem")
    rows, var_count, lats = state.shape
    core = lax.axis_index("space") % 2
    joined = jnp.concatenate([state, cotangent], axis=1)
    right = [(i, (i + 1) % blocks) for i in range(blocks)]
    left = [((i + 1) % blocks, i) for i in range(blocks)]
    before = lax.ppermute(joined[-2:], "space", right)
    after = lax.ppermute(joined[:2], "space", left)
    padded = jnp.concatenate([before, joined, after], axis=0)
    state_pad = padded[:, :var_count]
    cot_pad = padded[:, var_count:]
    activity = jnp.tanh(convolve(state_pad, conv_in) + bias[None, :, None])
    slopes = 1.0 - activity * activity
    backward = slopes * convolve(cot_pad, flipped(conv_out))
    gradient = cotangent + convolve(backward, flipped(conv_in))
    planes = jnp.transpose(gradient, (1, 0, 2)).astype(jnp.bfloat16)
    outgoing = jnp.broadcast_to(planes[None], (blocks // 2, 2, rows, lats))
    gathered = lax.all_to_all(
        outgoing.reshape(blocks, rows, lats), "space", 0, 0, tiled=True
    )
    field = gathered.reshape(blocks * rows, lats).astype(jnp.float32)

    kept = lax.dynamic_index_in_dim(members, core, 2, False)
    given = lax.dynamic_index_in_dim(members, 1 - core, 2, False)
    swap = [(i, i ^ 1) for i in range(blocks)]
    taken = lax.ppermute(given, "space", swap)
    plane = jnp.concatenate([kept, taken], axis=0)
    wide = plane.astype(jnp.float32)
    product = (wide * field[None]).astype(jnp.bfloat16)
    banded = jnp.einsum(
        "mxy,yz->mxz", product, band_matrix(lats, False), preferred_element_type=jnp.float32
    ).astype(jnp.bfloat16)
    lon_loc = band_matrix(blocks * rows, True)
    spread = jnp.einsum("zx,mxy->mzy", lon_loc, banded, preferred_element_type=jnp.float32)
    contrib = jnp.sum(wide * spread, axis=0).astype(jnp.bfloat16)
    tiles = contrib.reshape(blocks, rows, lats)
    parts = jnp.concatenate(
        [jnp.roll(tiles[:, -2:], 1, 0), tiles, jnp.roll(tiles[:, :2], -1, 0)], axis=1
    )
    arrived = lax.all_to_all(parts, "space", 0, 0, tiled=True)
    block = jnp.sum(
        arrived.reshape(blocks // 2, 2, rows + 4, lats).astype(jnp.float32), axis=0
    ).astype(jnp.bfloat16)
    copies = lax.all_to_all(
        jnp.broadcast_to(block[None], (groups, 2, rows + 4, lats)), "mem", 0, 0, tiled=True
    )
    member_count = members.shape[0] * blocks * groups
    total = jnp.sum(copies.astype(jnp.float32), axis=0) / (member_count - 1.0)
    incr_pad = jnp.transpose(total, (1, 0, 2))
    increment = incr_pad[2:-2]
    tangent_hidden = slopes * convolve(incr_pad, conv_in)
    response = increment + convolve(tangent_hidden, conv_out)
    return (increment, response)


def solution(mesh):
    in_specs = (
        P(("space", "mem"), None, None, None),
        P("space", None, None),
        P("space", None, None),
        P(),
        P(),
        P(),
    )
    out_specs = (P("space", None, None), P("space", None, None))
    return jax.shard_map(
        per_device, mesh=mesh, in_specs=in_specs, out_specs=out_specs, check_vma=False
    )
```

```python
import functools

import jax
import jax.numpy as jnp
import ml_dtypes
import numpy as np
from jax import lax
from jax.experimental import pallas as pl
from jax.experimental.pallas import tpu as pltpu
from jax.sharding import PartitionSpec as P

HALF = 16
GROUP = 32
BF = jnp.bfloat16
F32 = jnp.float32


def taps(distance):
    ratio = distance.astype(np.float32) / np.float32(HALF + 1.0)
    value = np.float32(1.0) - ratio * ratio
    return np.where(distance <= HALF, value, np.float32(0.0)).astype(ml_dtypes.bfloat16)


def shifted(value, step):
    if step == 1:
        return value
    lats = value.shape[-1]
    lane = lax.broadcasted_iota(jnp.int32, value.shape, value.ndim - 1)
    if step == 0:
        return jnp.where(lane == 0, 0.0, pltpu.roll(value, 1, value.ndim - 1))
    return jnp.where(lane == lats - 1, 0.0, pltpu.roll(value, lats - 1, value.ndim - 1))


def split_high_low(value):
    high = value.astype(BF)
    low = (value - high.astype(F32)).astype(BF)
    return high, low


def stack_taps(wide_ref, tap_ref):
    for tile in range(wide_ref.shape[0]):
        value = wide_ref[tile]
        rows = value.shape[0] // 8
        high = value.astype(BF).astype(F32)
        low = value - high
        high = high.reshape(rows, 1, 8, 128)
        low = low.reshape(rows, 1, 8, 128)
        both = jnp.concatenate([high, low, high, low], axis=1).reshape(rows * GROUP, 128)
        tap_ref[:, tile * 128 : (tile + 1) * 128] = both.astype(BF)


def put_taps(wide_ref, plane, first_row, var):
    rows = plane.shape[0]
    for step in range(3):
        moved = shifted(plane, step)
        for tile in range(wide_ref.shape[0]):
            start = first_row * 8 + 2 * step + var
            wide_ref[tile, pl.ds(start, rows, stride=8), :] = moved[:, tile * 128 : (tile + 1) * 128]


def put_ones(wide_ref, value):
    rows = wide_ref.shape[1] // 8
    for tile in range(wide_ref.shape[0]):
        wide_ref[tile, pl.ds(6, rows, stride=8), :] = jnp.full((rows, 128), value, F32)
        wide_ref[tile, pl.ds(7, rows, stride=8), :] = jnp.zeros((rows, 128), F32)


def fold_hidden(hidden, back_weight, fold_ref, row):
    high, low = split_high_low(hidden)
    product = jnp.dot(
        back_weight, jnp.concatenate([high, low], axis=0), preferred_element_type=F32
    )
    product = product[:24] + product[24:]
    total = product[8:16] + shifted(product[0:8], 0) + shifted(product[16:24], 2)
    for tile in range(fold_ref.shape[0]):
        fold_ref[tile, pl.ds(pl.multiple_of(row * 8, 8), 8), :] = total[:, tile * 128 : (tile + 1) * 128]


def folded(fold_ref, rows, var):
    tiles = []
    for tile in range(fold_ref.shape[0]):
        tiles.append(
            sum(
                fold_ref[tile, pl.ds(10 * step + var, rows, stride=8), :] for step in range(3)
            )
        )
    return jnp.concatenate(tiles, axis=1)


def fill_padded(main_ref, before_ref, after_ref, var_from, wide_ref):
    rows = main_ref.shape[0]
    for var in range(2):
        put_taps(wide_ref, main_ref[:, var, :], 2, var)
        for row in range(2):
            line = var_from + var
            put_taps(wide_ref, before_ref[row, line : line + 1, :], row, var)
            put_taps(wide_ref, after_ref[row, line : line + 1, :], rows + 2 + row, var)


def gradient_kernel(
    state_ref, cot_ref, before_ref, after_ref, front_ref, back_ref, out_ref, wide, state_taps, cot_taps, fold
):
    rows = state_ref.shape[0]
    put_ones(wide, 1.0)
    fill_padded(state_ref, before_ref, after_ref, 0, wide)
    stack_taps(wide, state_taps)
    fill_padded(cot_ref, before_ref, after_ref, 2, wide)
    stack_taps(wide, cot_taps)

    def step(row, carry):
        window = pl.ds(pl.multiple_of(row * GROUP, GROUP), 3 * GROUP)
        activity = jnp.tanh(jnp.dot(front_ref[0], state_taps[window, :], preferred_element_type=F32))
        slopes = 1.0 - activity * activity
        hidden = slopes * jnp.dot(front_ref[1], cot_taps[window, :], preferred_element_type=F32)
        fold_hidden(hidden, back_ref[0], fold, row)
        return carry

    lax.fori_loop(0, rows + 2, step, 0, unroll=2)
    for var in range(2):
        plane = (cot_ref[:, var, :] + folded(fold, rows, var)).astype(BF)
        for pair in range(out_ref.shape[0] // 2):
            out_ref[2 * pair + var] = plane


def slopes_kernel(state_ref, before_ref, after_ref, front_ref, out_ref, wide, state_taps):
    rows = state_ref.shape[0]
    put_ones(wide, 1.0)
    fill_padded(state_ref, before_ref, after_ref, 0, wide)
    stack_taps(wide, state_taps)

    def step(row, carry):
        window = pl.ds(pl.multiple_of(row * GROUP, GROUP), 3 * GROUP)
        activity = jnp.tanh(jnp.dot(front_ref[0], state_taps[window, :], preferred_element_type=F32))
        out_ref[row] = 1.0 - activity * activity
        return carry

    lax.fori_loop(0, rows + 2, step, 0, unroll=2)


def response_kernel(
    scale, copies_ref, slopes_ref, front_ref, back_ref, incr_out, resp_out, wide, incr_taps, fold
):
    rows = incr_out.shape[0]
    planes = []
    put_ones(wide, 0.0)
    for var in range(2):
        window = pl.ds(var * (rows + 4), rows + 4)
        plane = copies_ref[0, window, :].astype(F32)
        for group in range(1, copies_ref.shape[0]):
            plane = plane + copies_ref[group, window, :].astype(F32)
        plane = plane * scale
        planes.append(plane)
        put_taps(wide, plane, 0, var)
    stack_taps(wide, incr_taps)

    def step(row, carry):
        window = pl.ds(pl.multiple_of(row * GROUP, GROUP), 3 * GROUP)
        hidden = slopes_ref[row] * jnp.dot(
            front_ref[0], incr_taps[window, :], preferred_element_type=F32
        )
        fold_hidden(hidden, back_ref[1], fold, row)
        return carry

    lax.fori_loop(0, rows + 2, step, 0, unroll=2)
    for var in range(2):
        increment = planes[var][2 : 2 + rows]
        incr_out[:, var, :] = increment
        resp_out[:, var, :] = increment + folded(fold, rows, var)


def planes_kernel(core_ref, members_ref, keep_ref, give_ref, lines):
    core = core_ref[0]
    rows = members_ref.shape[1]
    lines[...] = members_ref.reshape(rows * 2, 128)[...].astype(F32)
    keep_ref[0] = lines[pl.ds(core, rows, stride=2), :].astype(BF)
    give_ref[0] = lines[pl.ds(1 - core, rows, stride=2), :].astype(BF)


def member_kernel(
    span, keep_ref, take_ref, field_ref, lat_ref, lon_ref, out_ref, field, banded, total
):
    step = pl.program_id(0)
    lons = field_ref.shape[0]
    blocks = out_ref.shape[0]
    rows = lons // blocks

    @pl.when(step == 0)
    def _():
        field[...] = field_ref[...].astype(F32)
        total[...] = jnp.zeros_like(total)

    for member_ref in (keep_ref, take_ref):
        for start in range(0, lons, span):
            window = pl.ds(start, span)
            product = (member_ref[0, window, :].astype(F32) * field[window, :]).astype(BF)
            banded[pl.ds(HALF + start, span), :] = jnp.dot(
                product, lat_ref[...], preferred_element_type=F32
            ).astype(BF)
        banded[pl.ds(0, HALF), :] = banded[pl.ds(lons, HALF), :]
        banded[pl.ds(HALF + lons, HALF), :] = banded[pl.ds(HALF, HALF), :]
        for start in range(0, lons, span):
            spread = jnp.dot(
                lon_ref[...], banded[pl.ds(start, span + 2 * HALF), :], preferred_element_type=F32
            )
            window = pl.ds(8 + start, span)
            total[window, :] += member_ref[0, pl.ds(start, span), :].astype(F32) * spread

    @pl.when(step == pl.num_programs(0) - 1)
    def _():
        total[pl.ds(0, 8), :] = total[pl.ds(lons, 8), :]
        total[pl.ds(lons + 8, 8), :] = total[pl.ds(8, 8), :]
        for block in range(blocks):
            out_ref[block] = total[pl.ds(6 + block * rows, rows + 4), :].astype(BF)


def sum_kernel(parts_ref, out_ref):
    for var in range(2):
        plane = parts_ref[var].astype(F32)
        for pair in range(1, parts_ref.shape[0] // 2):
            plane = plane + parts_ref[2 * pair + var].astype(F32)
        plane = plane.astype(BF)
        for group in range(out_ref.shape[0]):
            out_ref[group, pl.ds(var * plane.shape[0], plane.shape[0]), :] = plane


def weight_stacks(conv_in, conv_out, bias):
    first = jnp.transpose(conv_in, (0, 1, 3, 2))
    hidden = first.shape[-1]
    front = jnp.stack([first, conv_out[::-1, ::-1]]).reshape(2, 3, 6, hidden)
    ones = jnp.zeros((2, 3, 2, hidden), F32).at[0, 1, 0].set(bias)
    front = jnp.concatenate([front, ones], axis=2)
    back = jnp.stack([first[::-1, ::-1], conv_out])
    back = jnp.transpose(back, (0, 2, 1, 3, 4)).reshape(2, 3, 6, hidden)
    back = jnp.pad(back, ((0, 0), (0, 0), (0, 2), (0, 0))).reshape(2, 24, hidden)
    high = lax.reduce_precision(front, 8, 7)
    low = front - high
    front = jnp.stack([high, high, low, low], axis=2).reshape(2, 3 * GROUP, hidden)
    front = jnp.transpose(front, (0, 2, 1)).astype(BF)
    high = lax.reduce_precision(back, 8, 7)
    low = back - high
    back = jnp.concatenate([high, low], axis=1)
    back = jnp.concatenate([back, back], axis=2).astype(BF)
    return front, back


def per_device(members, state, cotangent, conv_in, conv_out, bias):
    blocks = lax.axis_size("space")
    groups = lax.axis_size("mem")
    held, lons, var_count, lats = members.shape
    rows = state.shape[0]
    tiles = lats // 128
    core = lax.axis_index("space") % 2
    right = [(i, (i + 1) % blocks) for i in range(blocks)]
    left = [((i + 1) % blocks, i) for i in range(blocks)]
    swap = [(i, i ^ 1) for i in range(blocks)]
    tail = jnp.concatenate([state[-2:], cotangent[-2:]], axis=1)
    head = jnp.concatenate([state[:2], cotangent[:2]], axis=1)
    before = lax.ppermute(tail, "space", right)
    after = lax.ppermute(head, "space", left)
    front, back = weight_stacks(conv_in, conv_out, bias)

    wide = pltpu.VMEM((tiles, (rows + 4) * 8, 128), F32)
    tap = pltpu.VMEM(((rows + 4) * GROUP, lats), BF)
    fold = pltpu.VMEM((tiles, (rows + 2) * 8, 128), F32)
    big = pltpu.CompilerParams(vmem_limit_bytes=48 << 20)
    outgoing = pl.pallas_call(
        gradient_kernel,
        out_shape=jax.ShapeDtypeStruct((blocks, rows, lats), BF),
        scratch_shapes=[wide, tap, tap, fold],
        compiler_params=big,
        cost_estimate=pl.CostEstimate(flops=2_000_000_000, bytes_accessed=1_500_000, transcendentals=1_200_000),
        name="gradient",
    )(state, cotangent, before, after, front, back)
    members, outgoing = lax.optimization_barrier((members, outgoing))
    gathered = lax.all_to_all(outgoing, "space", 0, 0, tiled=True)
    whole = pl.BlockSpec((1, lons, var_count, 128), lambda i, j, c: (i, 0, 0, j))
    plane_spec = pl.BlockSpec((1, lons, 128), lambda i, j, c: (i, 0, j))
    kept, given = pl.pallas_call(
        planes_kernel,
        grid_spec=pltpu.PrefetchScalarGridSpec(
            num_scalar_prefetch=1,
            grid=(held, tiles),
            in_specs=[whole],
            out_specs=[plane_spec, plane_spec],
            scratch_shapes=[pltpu.VMEM((lons * 2, 128), F32)],
        ),
        out_shape=[jax.ShapeDtypeStruct((held, lons, lats), BF)] * 2,
        compiler_params=big,
        cost_estimate=pl.CostEstimate(flops=0, bytes_accessed=20_000_000, transcendentals=0),
        name="planes",
    )(core.reshape(1), members)
    taken = lax.ppermute(given, "space", swap)
    slopes = pl.pallas_call(
        slopes_kernel,
        out_shape=jax.ShapeDtypeStruct((rows + 2, conv_in.shape[2], lats), F32),
        scratch_shapes=[wide, tap],
        compiler_params=big,
        cost_estimate=pl.CostEstimate(flops=1_000_000_000, bytes_accessed=6_000_000, transcendentals=1_200_000),
        name="slopes",
    )(state, before, after, front)

    span = 192
    offsets = np.arange(lats)
    lat_loc = jnp.asarray(taps(np.abs(offsets[:, None] - offsets[None, :])))
    lon_loc = jnp.asarray(
        taps(np.abs(np.arange(span)[:, None] + HALF - np.arange(span + 2 * HALF)[None, :]))
    )
    one = pl.BlockSpec((1, lons, lats), lambda i: (i, 0, 0))
    fixed = lambda *shape: pl.BlockSpec(shape, lambda i: (0,) * len(shape))
    parts = pl.pallas_call(
        functools.partial(member_kernel, span),
        grid=(held,),
        in_specs=[one, one, fixed(lons, lats), fixed(lats, lats), fixed(span, span + 2 * HALF)],
        out_specs=fixed(blocks, rows + 4, lats),
        out_shape=jax.ShapeDtypeStruct((blocks, rows + 4, lats), BF),
        scratch_shapes=[
            pltpu.VMEM((lons, lats), F32),
            pltpu.VMEM((lons + 2 * HALF, lats), BF),
            pltpu.VMEM((lons + 16, lats), F32),
        ],
        compiler_params=big,
        cost_estimate=pl.CostEstimate(flops=4_000_000_000, bytes_accessed=6_000_000, transcendentals=0),
        name="members",
    )(kept, taken, gathered.reshape(lons, lats), lat_loc, lon_loc)
    arrived = lax.all_to_all(parts, "space", 0, 0, tiled=True)
    spread = pl.pallas_call(
        sum_kernel,
        out_shape=jax.ShapeDtypeStruct((groups, 2 * (rows + 4), lats), BF),
        compiler_params=big,
        name="block_sum",
    )(arrived)
    copies = lax.all_to_all(spread, "mem", 0, 0, tiled=True)
    member_count = held * blocks * groups
    field = jax.ShapeDtypeStruct(state.shape, F32)
    increment, response = pl.pallas_call(
        functools.partial(response_kernel, 1.0 / (member_count - 1.0)),
        out_shape=[field, field],
        scratch_shapes=[wide, tap, fold],
        compiler_params=big,
        name="response",
    )(copies, slopes, front, back)
    return (increment, response)


def solution(mesh):
    in_specs = (
        P(("space", "mem"), None, None, None),
        P("space", None, None),
        P("space", None, None),
        P(),
        P(),
        P(),
    )
    out_specs = (P("space", None, None), P("space", None, None))
    return jax.shard_map(
        per_device, mesh=mesh, in_specs=in_specs, out_specs=out_specs, check_vma=False
    )
```

```python
import functools

import jax
import jax.numpy as jnp
import ml_dtypes
import numpy as np
from jax import lax
from jax.experimental import pallas as pl
from jax.experimental.pallas import tpu as pltpu
from jax.sharding import PartitionSpec as P

HALF = 16
GROUP = 32
UNROLL = 2
BF = jnp.bfloat16
F32 = jnp.float32


def taps(distance):
    ratio = distance.astype(np.float32) / np.float32(HALF + 1.0)
    value = np.float32(1.0) - ratio * ratio
    return np.where(distance <= HALF, value, np.float32(0.0)).astype(ml_dtypes.bfloat16)


def shifted(value, step):
    if step == 1:
        return value
    lats = value.shape[-1]
    lane = lax.broadcasted_iota(jnp.int32, value.shape, value.ndim - 1)
    if step == 0:
        return jnp.where(lane == 0, 0.0, pltpu.roll(value, 1, value.ndim - 1))
    return jnp.where(lane == lats - 1, 0.0, pltpu.roll(value, lats - 1, value.ndim - 1))


def split_high_low(value):
    high = value.astype(BF)
    low = (value - high.astype(F32)).astype(BF)
    return high, low


def stack_taps(wide_ref, tap_ref):
    for tile in range(wide_ref.shape[0]):
        value = wide_ref[tile]
        rows = value.shape[0] // 8
        high = value.astype(BF).astype(F32)
        low = value - high
        high = high.reshape(rows, 1, 8, 128)
        low = low.reshape(rows, 1, 8, 128)
        both = jnp.concatenate([high, low, high, low], axis=1).reshape(rows * GROUP, 128)
        tap_ref[:, tile * 128 : (tile + 1) * 128] = both.astype(BF)


def put_taps(wide_ref, plane, first_row, var):
    rows = plane.shape[0]
    for step in range(3):
        moved = shifted(plane, step)
        for tile in range(wide_ref.shape[0]):
            start = first_row * 8 + 2 * step + var
            wide_ref[tile, pl.ds(start, rows, stride=8), :] = moved[:, tile * 128 : (tile + 1) * 128]


def put_ones(wide_ref, value):
    rows = wide_ref.shape[1] // 8
    for tile in range(wide_ref.shape[0]):
        wide_ref[tile, pl.ds(6, rows, stride=8), :] = jnp.full((rows, 128), value, F32)
        wide_ref[tile, pl.ds(7, rows, stride=8), :] = jnp.zeros((rows, 128), F32)


def fold_hidden(hidden, back_weight, product_ref, row):
    high, low = split_high_low(hidden)
    product = jnp.dot(
        back_weight, jnp.concatenate([high, low], axis=0), preferred_element_type=F32
    )
    product = product[:24] + product[24:]
    for step in range(3):
        product_ref[step, pl.ds(pl.multiple_of(row * 8, 8), 8), :] = product[8 * step : 8 * step + 8]


def fold_lats(product_ref, fold_ref, first, count):
    window = pl.ds(first * 8, count * 8)
    total = (
        product_ref[1, window, :]
        + shifted(product_ref[0, window, :], 0)
        + shifted(product_ref[2, window, :], 2)
    )
    for tile in range(fold_ref.shape[0]):
        fold_ref[tile, window, :] = total[:, tile * 128 : (tile + 1) * 128]


def folded(fold_ref, rows, var):
    tiles = []
    for tile in range(fold_ref.shape[0]):
        tiles.append(
            sum(
                fold_ref[tile, pl.ds(10 * step + var, rows, stride=8), :] for step in range(3)
            )
        )
    return jnp.concatenate(tiles, axis=1)


def fill_edges(before_ref, after_ref, var_from, wide_ref):
    for var in range(2):
        line = var_from + var
        for row in range(2):
            put_taps(wide_ref, before_ref[row, line : line + 1, :], row, var)
            put_taps(wide_ref, after_ref[row, line : line + 1, :], 2 + row, var)


def tap_window(row):
    return pl.ds(pl.multiple_of(row * GROUP, GROUP), 3 * GROUP)


def bands(tap_ref, edge_ref, frame_ref):
    half = 2 * GROUP
    last = tap_ref.shape[0] - half
    frame_ref[0:half, :] = edge_ref[0:half, :]
    frame_ref[half : 2 * half, :] = tap_ref[0:half, :]
    frame_ref[2 * half : 3 * half, :] = tap_ref[last : last + half, :]
    frame_ref[3 * half : 4 * half, :] = edge_ref[half : 2 * half, :]


def front_stack(rows_ref):
    value = rows_ref[...]
    high = value.astype(BF).astype(F32)
    low = value - high
    high = high.reshape(3, 1, 8, 128)
    low = low.reshape(3, 1, 8, 128)
    both = jnp.concatenate([high, high, low, low], axis=1).reshape(3 * GROUP, 128)
    return jnp.transpose(both).astype(BF)


def back_stack(rows_ref):
    value = rows_ref[...]
    high = value.astype(BF).astype(F32)
    both = jnp.concatenate([high, value - high], axis=0)
    return jnp.concatenate([both, both], axis=1).astype(BF)


def fetch(pairs, semaphores):
    copies = [
        pltpu.make_async_copy(source, target, semaphores.at[index])
        for index, (source, target) in enumerate(pairs)
    ]
    for copy in copies:
        copy.start()
    return copies


def prepare_kernel(
    state_far,
    cot_far,
    first_far,
    second_far,
    bias_far,
    front_ref,
    back_ref,
    state_taps,
    cot_taps,
    fold,
    cot_planes,
    wide,
    lines,
    product,
    state_ref,
    cot_ref,
    first_ref,
    second_ref,
    bias_ref,
    semaphores,
):
    rows = state_ref.shape[0]
    near = (first_ref, second_ref, bias_ref, state_ref, cot_ref)
    far = (first_far, second_far, bias_far, state_far, cot_far)
    copies = fetch(zip(far, near), semaphores)
    for copy in copies[:3]:
        copy.wait()
    for which in range(2):
        lines[...] = jnp.zeros_like(lines)
        for lon in range(3):
            for lat in range(3):
                start = 8 * lon + 2 * lat
                if which == 0:
                    lines[start : start + 2, :] = first_ref[lon, lat]
                else:
                    lines[start : start + 2, :] = second_ref[2 - lon, 2 - lat]
        if which == 0:
            lines[14:15, :] = bias_ref[...]
        front_ref[which] = front_stack(lines)
        lines[...] = jnp.zeros_like(lines)
        for lon in range(3):
            for lat in range(3):
                start = 8 * lat + 2 * lon
                if which == 0:
                    lines[start : start + 2, :] = first_ref[2 - lon, 2 - lat]
                else:
                    lines[start : start + 2, :] = second_ref[lon, lat]
        back_ref[which] = back_stack(lines)

    put_ones(wide, 1.0)
    for copy in copies[3:]:
        copy.wait()
    for main_ref, tap_ref in ((state_ref, state_taps), (cot_ref, cot_taps)):
        for var in range(2):
            plane = main_ref[:, var, :]
            if main_ref is cot_ref:
                cot_planes[var] = plane
            put_taps(wide, plane, 0, var)
        stack_taps(wide, tap_ref)

    def step(row, carry):
        activity = jnp.tanh(
            jnp.dot(front_ref[0], state_taps[tap_window(row), :], preferred_element_type=F32)
        )
        slopes = 1.0 - activity * activity
        hidden = slopes * jnp.dot(
            front_ref[1], cot_taps[tap_window(row), :], preferred_element_type=F32
        )
        fold_hidden(hidden, back_ref[0], product, row + 2)
        return carry

    lax.fori_loop(0, rows - 2, step, 0, unroll=UNROLL)
    fold_lats(product, fold, 2, rows - 2)


def gradient_kernel(
    cot_planes,
    before_ref,
    after_ref,
    front_ref,
    back_ref,
    state_taps,
    cot_taps,
    fold_ref,
    out_ref,
    wide,
    edge,
    state_frame,
    cot_frame,
    product,
    fold,
):
    rows = cot_planes.shape[1]
    put_ones(wide, 1.0)
    for var_from, tap_ref, frame_ref in ((0, state_taps, state_frame), (2, cot_taps, cot_frame)):
        fill_edges(before_ref, after_ref, var_from, wide)
        stack_taps(wide, edge)
        bands(tap_ref, edge, frame_ref)
    fold[...] = fold_ref[...]
    for start, row in ((0, 0), (1, 1), (4, rows), (5, rows + 1)):
        window = pl.ds(start * GROUP, 3 * GROUP)
        activity = jnp.tanh(
            jnp.dot(front_ref[0], state_frame[window, :], preferred_element_type=F32)
        )
        slopes = 1.0 - activity * activity
        hidden = slopes * jnp.dot(
            front_ref[1], cot_frame[window, :], preferred_element_type=F32
        )
        fold_hidden(hidden, back_ref[0], product, row)
    fold_lats(product, fold, 0, 2)
    fold_lats(product, fold, rows, 2)
    for var in range(2):
        plane = (cot_planes[var] + folded(fold, rows, var)).astype(BF)
        for pair in range(out_ref.shape[0] // 2):
            out_ref[2 * pair + var] = plane


def slopes_kernel(
    before_ref, after_ref, front_ref, state_taps, out_ref, wide, edge, frame
):
    rows = out_ref.shape[0] - 2
    put_ones(wide, 1.0)
    fill_edges(before_ref, after_ref, 0, wide)
    stack_taps(wide, edge)
    bands(state_taps, edge, frame)

    def slopes(window):
        activity = jnp.tanh(jnp.dot(front_ref[0], window, preferred_element_type=F32))
        return 1.0 - activity * activity

    for start, row in ((0, 0), (1, 1), (4, rows), (5, rows + 1)):
        out_ref[row] = slopes(frame[pl.ds(start * GROUP, 3 * GROUP), :])

    def step(row, carry):
        out_ref[row + 2] = slopes(state_taps[tap_window(row), :])
        return carry

    lax.fori_loop(0, rows - 2, step, 0, unroll=2)


def response_kernel(
    scale,
    copies_ref,
    slopes_far,
    front_ref,
    back_ref,
    incr_out,
    resp_out,
    wide,
    incr_taps,
    product,
    fold,
    slopes_ref,
    semaphores,
):
    rows = incr_out.shape[0]
    half = (rows + 2) // 2
    halves = [pl.ds(0, half), pl.ds(half, half)]
    copies = fetch([(slopes_far.at[part], slopes_ref.at[part]) for part in halves], semaphores)
    planes = []
    put_ones(wide, 0.0)
    for var in range(2):
        window = pl.ds(var * (rows + 4), rows + 4)
        plane = copies_ref[0, window, :].astype(F32)
        for group in range(1, copies_ref.shape[0]):
            plane = plane + copies_ref[group, window, :].astype(F32)
        plane = plane * scale
        planes.append(plane)
        put_taps(wide, plane, 0, var)
    stack_taps(wide, incr_taps)

    def step(row, carry):
        hidden = slopes_ref[row] * jnp.dot(
            front_ref[0], incr_taps[tap_window(row), :], preferred_element_type=F32
        )
        fold_hidden(hidden, back_ref[1], product, row)
        return carry

    copies[0].wait()
    lax.fori_loop(0, half, step, 0, unroll=UNROLL)
    copies[1].wait()
    lax.fori_loop(half, rows + 2, step, 0, unroll=UNROLL)
    fold_lats(product, fold, 0, rows + 2)
    for var in range(2):
        increment = planes[var][2 : 2 + rows]
        incr_out[:, var, :] = increment
        resp_out[:, var, :] = increment + folded(fold, rows, var)


def planes_kernel(core_ref, members_ref, keep_ref, give_ref, lines):
    core = core_ref[0]
    rows = members_ref.shape[1]
    lines[...] = members_ref.reshape(rows * 2, 128)[...].astype(F32)
    keep_ref[...] = lines[pl.ds(core, rows, stride=2), :].astype(BF)
    give_ref[...] = lines[pl.ds(1 - core, rows, stride=2), :].astype(BF)


def member_kernel(span, *refs):
    *far_refs, field_ref, lat_ref, lon_ref, out_ref, field, banded, total, held, semaphores = refs
    lons = field_ref.shape[0]
    member_refs = [held.at[index] for index in range(len(far_refs))]
    copies = fetch(zip(far_refs, member_refs), semaphores)
    blocks = out_ref.shape[0]
    rows = lons // blocks
    field[...] = field_ref[...].astype(F32)
    for index, member_ref in enumerate(member_refs):
        copies[index].wait()
        for start in range(0, lons, span):
            window = pl.ds(start, span)
            product = (member_ref[window, :].astype(F32) * field[window, :]).astype(BF)
            banded[pl.ds(HALF + start, span), :] = jnp.dot(
                product, lat_ref[...], preferred_element_type=F32
            ).astype(BF)
        banded[pl.ds(0, HALF), :] = banded[pl.ds(lons, HALF), :]
        banded[pl.ds(HALF + lons, HALF), :] = banded[pl.ds(HALF, HALF), :]
        for start in range(0, lons, span):
            spread = jnp.dot(
                lon_ref[...], banded[pl.ds(start, span + 2 * HALF), :], preferred_element_type=F32
            )
            window = pl.ds(8 + start, span)
            value = member_ref[pl.ds(start, span), :].astype(F32) * spread
            total[window, :] = value if index == 0 else total[window, :] + value
    total[pl.ds(0, 8), :] = total[pl.ds(lons, 8), :]
    total[pl.ds(lons + 8, 8), :] = total[pl.ds(8, 8), :]
    for block in range(blocks):
        out_ref[block] = total[pl.ds(6 + block * rows, rows + 4), :].astype(BF)


def sum_kernel(parts_ref, out_ref):
    for var in range(2):
        plane = parts_ref[var].astype(F32)
        for pair in range(1, parts_ref.shape[0] // 2):
            plane = plane + parts_ref[2 * pair + var].astype(F32)
        plane = plane.astype(BF)
        for group in range(out_ref.shape[0]):
            out_ref[group, pl.ds(var * plane.shape[0], plane.shape[0]), :] = plane


def per_device(members, state, cotangent, conv_in, conv_out, bias):
    blocks = lax.axis_size("space")
    groups = lax.axis_size("mem")
    held, lons, var_count, lats = members.shape
    rows = state.shape[0]
    tiles = lats // 128
    core = lax.axis_index("space") % 2
    small = pltpu.CompilerParams(vmem_limit_bytes=24 << 20)
    right = [(i, (i + 1) % blocks) for i in range(blocks)]
    left = [((i + 1) % blocks, i) for i in range(blocks)]
    swap = [(i, i ^ 1) for i in range(blocks)]
    tail = jnp.concatenate([state[-2:], cotangent[-2:]], axis=1)
    head = jnp.concatenate([state[:2], cotangent[:2]], axis=1)
    before = lax.ppermute(tail, "space", right)
    after = lax.ppermute(head, "space", left)
    hidden = conv_in.shape[2]
    shape = jax.ShapeDtypeStruct
    padded = lambda count: pltpu.VMEM((tiles, count * 8, 128), F32)
    tap = lambda count: pltpu.VMEM((count * GROUP, lats), BF)
    product = pltpu.VMEM((3, (rows + 2) * 8, lats), F32)
    first = jnp.transpose(conv_in, (0, 1, 3, 2))
    far = pl.BlockSpec(memory_space=pltpu.HBM)
    near = pl.BlockSpec(memory_space=pltpu.VMEM)
    remote = lambda value: pltpu.with_memory_space_constraint(value, pltpu.HBM)
    front, back, state_taps, cot_taps, partial, cot_planes = pl.pallas_call(
        prepare_kernel,
        out_shape=[
            shape((2, hidden, 3 * GROUP), BF),
            shape((2, 48, 2 * hidden), BF),
            shape((rows * GROUP, lats), BF),
            shape((rows * GROUP, lats), BF),
            shape((tiles, (rows + 2) * 8, 128), F32),
            shape((var_count, rows, lats), F32),
        ],
        in_specs=[far] * 5,
        scratch_shapes=[
            padded(rows),
            pltpu.VMEM((24, hidden), F32),
            product,
            pltpu.VMEM(state.shape, F32),
            pltpu.VMEM(state.shape, F32),
            pltpu.VMEM(first.shape, F32),
            pltpu.VMEM(conv_out.shape, F32),
            pltpu.VMEM((1, hidden), F32),
            pltpu.SemaphoreType.DMA((5,)),
        ],
        compiler_params=small,
        cost_estimate=pl.CostEstimate(flops=2_000_000_000, bytes_accessed=3_000_000, transcendentals=1_100_000),
        name="prepare",
    )(*[remote(value) for value in (state, cotangent, first, conv_out, bias.reshape(1, hidden))])
    outgoing = pl.pallas_call(
        gradient_kernel,
        out_shape=shape((blocks, rows, lats), BF),
        scratch_shapes=[
            padded(4), tap(4), tap(8), tap(8), product, padded(rows + 2)
        ],
        compiler_params=small,
        cost_estimate=pl.CostEstimate(flops=400_000_000, bytes_accessed=1_500_000, transcendentals=200_000),
        name="gradient",
    )(cot_planes, before, after, front, back, state_taps, cot_taps, partial)
    members, outgoing = lax.optimization_barrier((members, outgoing))
    gathered = lax.all_to_all(outgoing, "space", 0, 0, tiled=True)
    kept, taken = [], []
    members = remote(members)
    for member in range(held):
        keep, give = pl.pallas_call(
            planes_kernel,
            grid_spec=pltpu.PrefetchScalarGridSpec(
                num_scalar_prefetch=1,
                grid=(tiles,),
                in_specs=[
                    pl.BlockSpec((1, lons, var_count, 128), lambda j, c, member=member: (member, 0, 0, j))
                ],
                out_specs=[pl.BlockSpec((lons, 128), lambda j, c: (0, j))] * 2,
                scratch_shapes=[pltpu.VMEM((lons * 2, 128), F32)],
            ),
            out_shape=[pltpu.HBM((lons, lats), BF)] * 2,
            compiler_params=small,
            cost_estimate=pl.CostEstimate(flops=0, bytes_accessed=10_000_000, transcendentals=0),
            name="planes",
        )(core.reshape(1), members)
        kept.append(keep)
        taken.append(lax.ppermute(give, "space", swap))
    slopes = pl.pallas_call(
        slopes_kernel,
        out_shape=pltpu.HBM((rows + 2, hidden, lats), F32),
        out_specs=near,
        scratch_shapes=[padded(4), tap(4), tap(8)],
        compiler_params=small,
        cost_estimate=pl.CostEstimate(flops=1_000_000_000, bytes_accessed=6_000_000, transcendentals=1_200_000),
        name="slopes",
    )(before, after, front, state_taps)

    span = 192
    offsets = np.arange(lats)
    lat_loc = jnp.asarray(taps(np.abs(offsets[:, None] - offsets[None, :])))
    lon_loc = jnp.asarray(
        taps(np.abs(np.arange(span)[:, None] + HALF - np.arange(span + 2 * HALF)[None, :]))
    )
    parts = pl.pallas_call(
        functools.partial(member_kernel, span),
        in_specs=[far] * (2 * held) + [near] * 3,
        out_shape=jax.ShapeDtypeStruct((blocks, rows + 4, lats), BF),
        scratch_shapes=[
            pltpu.VMEM((lons, lats), F32),
            pltpu.VMEM((lons + 2 * HALF, lats), BF),
            pltpu.VMEM((lons + 16, lats), F32),
            pltpu.VMEM((2 * held, lons, lats), BF),
            pltpu.SemaphoreType.DMA((2 * held,)),
        ],
        compiler_params=small,
        cost_estimate=pl.CostEstimate(flops=4_000_000_000, bytes_accessed=6_000_000, transcendentals=0),
        name="members",
    )(*[remote(value) for value in kept + taken], gathered.reshape(lons, lats), lat_loc, lon_loc)
    arrived = lax.all_to_all(parts, "space", 0, 0, tiled=True)
    spread = pl.pallas_call(
        sum_kernel,
        out_shape=jax.ShapeDtypeStruct((groups, 2 * (rows + 4), lats), BF),
        compiler_params=small,
        name="block_sum",
    )(arrived)
    copies = lax.all_to_all(spread, "mem", 0, 0, tiled=True)
    member_count = held * blocks * groups
    field = jax.ShapeDtypeStruct(state.shape, F32)
    increment, response = pl.pallas_call(
        functools.partial(response_kernel, 1.0 / (member_count - 1.0)),
        out_shape=[field, field],
        in_specs=[near, far, near, near],
        scratch_shapes=[
            padded(rows + 4),
            tap(rows + 4),
            product,
            padded(rows + 2),
            pltpu.VMEM((rows + 2, hidden, lats), F32),
            pltpu.SemaphoreType.DMA((2,)),
        ],
        compiler_params=small,
        name="response",
    )(copies, remote(slopes), front, back)
    return (increment, response)


def solution(mesh):
    in_specs = (
        P(("space", "mem"), None, None, None),
        P("space", None, None),
        P("space", None, None),
        P(),
        P(),
        P(),
    )
    out_specs = (P("space", None, None), P("space", None, None))
    return jax.shard_map(
        per_device, mesh=mesh, in_specs=in_specs, out_specs=out_specs, check_vma=False
    )
```

```python
import functools

import jax
import jax.numpy as jnp
import ml_dtypes
import numpy as np
from jax import lax
from jax.experimental import pallas as pl
from jax.experimental.pallas import tpu as pltpu
from jax.sharding import PartitionSpec as P

HALF = 16
GROUP = 32
UNROLL = True
BF = jnp.bfloat16
F32 = jnp.float32


def taps(distance):
    ratio = distance.astype(np.float32) / np.float32(HALF + 1.0)
    value = np.float32(1.0) - ratio * ratio
    return np.where(distance <= HALF, value, np.float32(0.0)).astype(ml_dtypes.bfloat16)


def shifted(value, step):
    if step == 1:
        return value
    lats = value.shape[-1]
    lane = lax.broadcasted_iota(jnp.int32, value.shape, value.ndim - 1)
    if step == 0:
        return jnp.where(lane == 0, 0.0, pltpu.roll(value, 1, value.ndim - 1))
    return jnp.where(lane == lats - 1, 0.0, pltpu.roll(value, lats - 1, value.ndim - 1))


def split_high_low(value):
    high = value.astype(BF)
    low = (value - high.astype(F32)).astype(BF)
    return high, low


def stack_taps(wide_ref, tap_ref):
    for tile in range(wide_ref.shape[0]):
        value = wide_ref[tile]
        rows = value.shape[0] // 8
        high = value.astype(BF).astype(F32)
        low = value - high
        high = high.reshape(rows, 1, 8, 128)
        low = low.reshape(rows, 1, 8, 128)
        both = jnp.concatenate([high, low, high, low], axis=1).reshape(rows * GROUP, 128)
        tap_ref[:, tile * 128 : (tile + 1) * 128] = both.astype(BF)


def put_taps(wide_ref, plane, first_row, var):
    rows = plane.shape[0]
    for step in range(3):
        moved = shifted(plane, step)
        for tile in range(wide_ref.shape[0]):
            start = first_row * 8 + 2 * step + var
            wide_ref[tile, pl.ds(start, rows, stride=8), :] = moved[:, tile * 128 : (tile + 1) * 128]


def put_ones(wide_ref, value):
    rows = wide_ref.shape[1] // 8
    for tile in range(wide_ref.shape[0]):
        wide_ref[tile, pl.ds(6, rows, stride=8), :] = jnp.full((rows, 128), value, F32)
        wide_ref[tile, pl.ds(7, rows, stride=8), :] = jnp.zeros((rows, 128), F32)


def fold_hidden(hidden, back_weight, product_ref, row):
    high, low = split_high_low(hidden)
    product = jnp.dot(
        back_weight, jnp.concatenate([high, low], axis=0), preferred_element_type=F32
    )
    product = product[:24] + product[24:]
    for step in range(3):
        product_ref[step, pl.ds(pl.multiple_of(row * 8, 8), 8), :] = product[8 * step : 8 * step + 8]


def fold_lats(product_ref, fold_ref, first, count):
    window = pl.ds(first * 8, count * 8)
    total = (
        product_ref[1, window, :]
        + shifted(product_ref[0, window, :], 0)
        + shifted(product_ref[2, window, :], 2)
    )
    for tile in range(fold_ref.shape[0]):
        fold_ref[tile, window, :] = total[:, tile * 128 : (tile + 1) * 128]


def folded(fold_ref, rows, var):
    tiles = []
    for tile in range(fold_ref.shape[0]):
        tiles.append(
            sum(
                fold_ref[tile, pl.ds(10 * step + var, rows, stride=8), :] for step in range(3)
            )
        )
    return jnp.concatenate(tiles, axis=1)


def edges(core_ref, partner_ref, neighbour_ref):
    partner, neighbour = partner_ref[...], neighbour_ref[...]
    first = core_ref[0] == 0
    return jnp.where(first, neighbour, partner), jnp.where(first, partner, neighbour)


def fill_edges(before_ref, after_ref, var_from, wide_ref):
    for var in range(2):
        line = var_from + var
        for row in range(2):
            put_taps(wide_ref, before_ref[row, line : line + 1, :], row, var)
            put_taps(wide_ref, after_ref[row, line : line + 1, :], 2 + row, var)


def tap_window(row):
    return pl.ds(pl.multiple_of(row * GROUP, GROUP), 3 * GROUP)


def bands(tap_ref, edge_ref, frame_ref):
    half = 2 * GROUP
    last = tap_ref.shape[0] - half
    frame_ref[0:half, :] = edge_ref[0:half, :]
    frame_ref[half : 2 * half, :] = tap_ref[0:half, :]
    frame_ref[2 * half : 3 * half, :] = tap_ref[last : last + half, :]
    frame_ref[3 * half : 4 * half, :] = edge_ref[half : 2 * half, :]


def front_stack(rows_ref):
    value = rows_ref[...]
    high = value.astype(BF).astype(F32)
    low = value - high
    high = high.reshape(3, 1, 8, 128)
    low = low.reshape(3, 1, 8, 128)
    both = jnp.concatenate([high, high, low, low], axis=1).reshape(3 * GROUP, 128)
    return jnp.transpose(both).astype(BF)


def back_stack(rows_ref):
    value = rows_ref[...]
    high = value.astype(BF).astype(F32)
    both = jnp.concatenate([high, value - high], axis=0)
    return jnp.concatenate([both, both], axis=1).astype(BF)


def fetch(pairs, semaphores):
    copies = [
        pltpu.make_async_copy(source, target, semaphores.at[index])
        for index, (source, target) in enumerate(pairs)
    ]
    for copy in copies:
        copy.start()
    return copies


def prepare_kernel(
    state_far,
    cot_far,
    first_far,
    second_far,
    bias_far,
    front_ref,
    back_ref,
    state_taps,
    cot_taps,
    fold,
    cot_planes,
    wide,
    lines,
    product,
    state_ref,
    cot_ref,
    first_ref,
    second_ref,
    bias_ref,
    semaphores,
):
    rows = state_ref.shape[0]
    near = (first_ref, second_ref, bias_ref, state_ref, cot_ref)
    far = (first_far, second_far, bias_far, state_far, cot_far)
    copies = fetch(zip(far, near), semaphores)
    for copy in copies[:3]:
        copy.wait()
    for which in range(2):
        lines[...] = jnp.zeros_like(lines)
        for lon in range(3):
            for lat in range(3):
                start = 8 * lon + 2 * lat
                if which == 0:
                    lines[start : start + 2, :] = first_ref[lon, lat]
                else:
                    lines[start : start + 2, :] = second_ref[2 - lon, 2 - lat]
        if which == 0:
            lines[14:15, :] = bias_ref[...]
        front_ref[which] = front_stack(lines)
        lines[...] = jnp.zeros_like(lines)
        for lon in range(3):
            for lat in range(3):
                start = 8 * lat + 2 * lon
                if which == 0:
                    lines[start : start + 2, :] = first_ref[2 - lon, 2 - lat]
                else:
                    lines[start : start + 2, :] = second_ref[lon, lat]
        back_ref[which] = back_stack(lines)

    put_ones(wide, 1.0)
    for copy in copies[3:]:
        copy.wait()
    for main_ref, tap_ref in ((state_ref, state_taps), (cot_ref, cot_taps)):
        for var in range(2):
            plane = main_ref[:, var, :]
            if main_ref is cot_ref:
                cot_planes[var] = plane
            put_taps(wide, plane, 0, var)
        stack_taps(wide, tap_ref)

    def step(row, carry):
        activity = jnp.tanh(
            jnp.dot(front_ref[0], state_taps[tap_window(row), :], preferred_element_type=F32)
        )
        slopes = 1.0 - activity * activity
        hidden = slopes * jnp.dot(
            front_ref[1], cot_taps[tap_window(row), :], preferred_element_type=F32
        )
        fold_hidden(hidden, back_ref[0], product, row + 2)
        return carry

    lax.fori_loop(0, rows - 2, step, 0, unroll=UNROLL)
    fold_lats(product, fold, 2, rows - 2)


def gradient_kernel(
    core_ref,
    cot_planes,
    partner_ref,
    neighbour_ref,
    front_ref,
    back_ref,
    state_taps,
    cot_taps,
    fold_ref,
    out_ref,
    wide,
    edge,
    state_frame,
    cot_frame,
    product,
    fold,
):
    rows = cot_planes.shape[1]
    before_ref, after_ref = edges(core_ref, partner_ref, neighbour_ref)
    put_ones(wide, 1.0)
    for var_from, tap_ref, frame_ref in ((0, state_taps, state_frame), (2, cot_taps, cot_frame)):
        fill_edges(before_ref, after_ref, var_from, wide)
        stack_taps(wide, edge)
        bands(tap_ref, edge, frame_ref)
    fold[...] = fold_ref[...]
    for start, row in ((0, 0), (1, 1), (4, rows), (5, rows + 1)):
        window = pl.ds(start * GROUP, 3 * GROUP)
        activity = jnp.tanh(
            jnp.dot(front_ref[0], state_frame[window, :], preferred_element_type=F32)
        )
        slopes = 1.0 - activity * activity
        hidden = slopes * jnp.dot(
            front_ref[1], cot_frame[window, :], preferred_element_type=F32
        )
        fold_hidden(hidden, back_ref[0], product, row)
    fold_lats(product, fold, 0, 2)
    fold_lats(product, fold, rows, 2)
    for var in range(2):
        plane = (cot_planes[var] + folded(fold, rows, var)).astype(BF)
        for pair in range(out_ref.shape[0] // 2):
            out_ref[2 * pair + var] = plane


def slopes_kernel(
    core_ref, partner_ref, neighbour_ref, front_ref, state_taps, out_ref, wide, edge, frame
):
    rows = out_ref.shape[0] - 2
    before_ref, after_ref = edges(core_ref, partner_ref, neighbour_ref)
    put_ones(wide, 1.0)
    fill_edges(before_ref, after_ref, 0, wide)
    stack_taps(wide, edge)
    bands(state_taps, edge, frame)

    def slopes(window):
        activity = jnp.tanh(jnp.dot(front_ref[0], window, preferred_element_type=F32))
        return 1.0 - activity * activity

    for start, row in ((0, 0), (1, 1), (4, rows), (5, rows + 1)):
        out_ref[row] = slopes(frame[pl.ds(start * GROUP, 3 * GROUP), :])

    def step(row, carry):
        out_ref[row + 2] = slopes(state_taps[tap_window(row), :])
        return carry

    lax.fori_loop(0, rows - 2, step, 0, unroll=2)


def response_kernel(
    scale,
    copies_ref,
    slopes_far,
    front_ref,
    back_ref,
    incr_out,
    resp_out,
    wide,
    incr_taps,
    product,
    fold,
    slopes_ref,
    semaphores,
):
    rows = incr_out.shape[0]
    half = (rows + 2) // 2
    halves = [pl.ds(0, half), pl.ds(half, half)]
    copies = fetch([(slopes_far.at[part], slopes_ref.at[part]) for part in halves], semaphores)
    planes = []
    put_ones(wide, 0.0)
    for var in range(2):
        window = pl.ds(var * (rows + 4), rows + 4)
        plane = copies_ref[0, window, :].astype(F32)
        for group in range(1, copies_ref.shape[0]):
            plane = plane + copies_ref[group, window, :].astype(F32)
        plane = plane * scale
        planes.append(plane)
        put_taps(wide, plane, 0, var)
    stack_taps(wide, incr_taps)

    def step(row, carry):
        hidden = slopes_ref[row] * jnp.dot(
            front_ref[0], incr_taps[tap_window(row), :], preferred_element_type=F32
        )
        fold_hidden(hidden, back_ref[1], product, row)
        return carry

    copies[0].wait()
    lax.fori_loop(0, half, step, 0, unroll=UNROLL)
    copies[1].wait()
    lax.fori_loop(half, rows + 2, step, 0, unroll=UNROLL)
    fold_lats(product, fold, 0, rows + 2)
    for var in range(2):
        increment = planes[var][2 : 2 + rows]
        incr_out[:, var, :] = increment
        resp_out[:, var, :] = increment + folded(fold, rows, var)


def planes_kernel(core_ref, members_far, *refs):
    *outs, near, lines, planes, in_semaphores, out_semaphores = refs
    core = core_ref[0]
    count, tiles, lines_count = near.shape[:3]
    rows = lines_count // 2
    merged = members_far.reshape(count, lines_count, tiles * 128)
    pairs = [
        (merged.at[member, :, pl.ds(tile * 128, 128)], near.at[member, tile])
        for member in range(count)
        for tile in range(tiles)
    ]
    arrivals = fetch(pairs, in_semaphores)
    departures = []
    for member in range(count):
        for tile in range(tiles):
            arrivals[member * tiles + tile].wait()
            lines[...] = near[member, tile].astype(F32)
            window = pl.ds(tile * 128, 128)
            planes[member, :, window] = lines[pl.ds(core, rows, stride=2), :].astype(BF)
            planes[count + member, :, window] = lines[pl.ds(1 - core, rows, stride=2), :].astype(BF)
        for slot in (count + member, member):
            copy = pltpu.make_async_copy(planes.at[slot], outs[slot], out_semaphores.at[slot])
            copy.start()
            departures.append(copy)
    for copy in departures:
        copy.wait()


def member_kernel(span, reaches, *refs):
    *far_refs, field_ref, lat_ref, lon_ref, out_ref, field, banded, total, held, semaphores = refs
    lons = field_ref.shape[0]
    blocks = out_ref.shape[0]
    rows = lons // blocks
    member_refs = [held.at[index] for index in range(len(far_refs))]
    copies = fetch(zip(far_refs, member_refs), semaphores)
    field[...] = field_ref[...].astype(F32)
    for index, member_ref in enumerate(member_refs):
        copies[index].wait()
        for start in range(0, lons, span):
            window = pl.ds(start, span)
            product = (member_ref[window, :].astype(F32) * field[window, :]).astype(BF)
            for (first, last), (low, high) in reaches:
                banded[pl.ds(HALF + start, span), first:last] = jnp.dot(
                    product[:, low:high], lat_ref[low:high, first:last], preferred_element_type=F32
                ).astype(BF)
        banded[pl.ds(0, HALF), :] = banded[pl.ds(lons, HALF), :]
        banded[pl.ds(HALF + lons, HALF), :] = banded[pl.ds(HALF, HALF), :]
        for start in range(0, lons, span):
            spread = jnp.dot(
                lon_ref[...], banded[pl.ds(start, span + 2 * HALF), :], preferred_element_type=F32
            )
            window = pl.ds(8 + start, span)
            value = member_ref[pl.ds(start, span), :].astype(F32) * spread
            total[window, :] = value if index == 0 else total[window, :] + value
    total[pl.ds(0, 8), :] = total[pl.ds(lons, 8), :]
    total[pl.ds(lons + 8, 8), :] = total[pl.ds(8, 8), :]
    for block in range(blocks):
        out_ref[block] = total[pl.ds(6 + block * rows, rows + 4), :].astype(BF)


def sum_kernel(*refs):
    *parts_refs, out_ref = refs
    start = 0
    for parts_ref in parts_refs:
        lines, lats = parts_ref.shape[1:]
        for var in range(2):
            plane = parts_ref[var].astype(F32)
            for pair in range(1, parts_ref.shape[0] // 2):
                plane = plane + parts_ref[2 * pair + var].astype(F32)
            plane = plane.astype(BF)
            for group in range(out_ref.shape[0]):
                out_ref[group, pl.ds(var * lines, lines), pl.ds(start, lats)] = plane
        start += lats


def shape_of(*dims):
    return jax.ShapeDtypeStruct(dims, BF)


def wide_of(*dims):
    return jax.ShapeDtypeStruct(dims, F32)


FAR = pl.BlockSpec(memory_space=pltpu.HBM)
SCALAR = pl.BlockSpec(memory_space=pltpu.SMEM)
NEAR = pl.BlockSpec(memory_space=pltpu.VMEM)
PARAMS = pltpu.CompilerParams(vmem_limit_bytes=24 << 20)


def remote(value):
    return pltpu.with_memory_space_constraint(value, pltpu.HBM)


def padded_scratch(count, lats):
    return pltpu.VMEM((lats // 128, count * 8, 128), F32)


def tap_scratch(count, lats):
    return pltpu.VMEM((count * GROUP, lats), BF)


def prepare(state, cotangent, first, second, bias):
    rows, var_count, lats = state.shape
    hidden = first.shape[-1]
    operands = (state, cotangent, first, second, bias.reshape(1, hidden))
    return pl.pallas_call(
        prepare_kernel,
        out_shape=[
            shape_of(2, hidden, 3 * GROUP),
            shape_of(2, 48, 2 * hidden),
            shape_of(rows * GROUP, lats),
            shape_of(rows * GROUP, lats),
            wide_of(lats // 128, (rows + 2) * 8, 128),
            wide_of(var_count, rows, lats),
        ],
        in_specs=[FAR] * 5,
        scratch_shapes=[
            padded_scratch(rows, lats),
            pltpu.VMEM((24, hidden), F32),
            pltpu.VMEM((3, (rows + 2) * 8, lats), F32),
            pltpu.VMEM(state.shape, F32),
            pltpu.VMEM(state.shape, F32),
            pltpu.VMEM(first.shape, F32),
            pltpu.VMEM(second.shape, F32),
            pltpu.VMEM((1, hidden), F32),
            pltpu.SemaphoreType.DMA((5,)),
        ],
        compiler_params=PARAMS,
        cost_estimate=pl.CostEstimate(
            flops=2_000_000_000, bytes_accessed=3_000_000, transcendentals=1_100_000
        ),
        name="prepare",
    )(*[remote(value) for value in operands])


def gradient_planes(
    blocks, core, cot_planes, partner, neighbour, front, back, state_taps, cot_taps, partial
):
    var_count, rows, lats = cot_planes.shape
    return pl.pallas_call(
        gradient_kernel,
        out_shape=shape_of(blocks, rows, lats),
        in_specs=[SCALAR] + [NEAR] * 8,
        scratch_shapes=[
            padded_scratch(4, lats),
            tap_scratch(4, lats),
            tap_scratch(8, lats),
            tap_scratch(8, lats),
            pltpu.VMEM((3, (rows + 2) * 8, lats), F32),
            padded_scratch(rows + 2, lats),
        ],
        compiler_params=PARAMS,
        cost_estimate=pl.CostEstimate(
            flops=400_000_000, bytes_accessed=1_500_000, transcendentals=200_000
        ),
        name="gradient",
    )(core, cot_planes, partner, neighbour, front, back, state_taps, cot_taps, partial)


def member_planes(core, members):
    count, lons, var_count, lats = members.shape
    results = pl.pallas_call(
        planes_kernel,
        in_specs=[SCALAR, FAR],
        out_specs=[FAR] * (2 * count),
        out_shape=[pltpu.HBM((lons, lats), BF)] * (2 * count),
        scratch_shapes=[
            pltpu.VMEM((count, lats // 128, lons * var_count, 128), BF),
            pltpu.VMEM((lons * 2, 128), F32),
            pltpu.VMEM((2 * count, lons, lats), BF),
            pltpu.SemaphoreType.DMA((count * (lats // 128),)),
            pltpu.SemaphoreType.DMA((2 * count,)),
        ],
        compiler_params=PARAMS,
        cost_estimate=pl.CostEstimate(flops=0, bytes_accessed=10_000_000, transcendentals=0),
        name="planes",
    )(core, remote(members))
    return list(results[:count]), list(results[count:])


def hidden_slopes(core, partner, neighbour, front, state_taps):
    rows = state_taps.shape[0] // GROUP
    hidden, lats = front.shape[1], state_taps.shape[1]
    return pl.pallas_call(
        slopes_kernel,
        out_shape=pltpu.HBM((rows + 2, hidden, lats), F32),
        in_specs=[SCALAR] + [NEAR] * 4,
        out_specs=NEAR,
        scratch_shapes=[padded_scratch(4, lats), tap_scratch(4, lats), tap_scratch(8, lats)],
        compiler_params=PARAMS,
        cost_estimate=pl.CostEstimate(
            flops=1_000_000_000, bytes_accessed=6_000_000, transcendentals=1_200_000
        ),
        name="slopes",
    )(core, partner, neighbour, front, state_taps)


def member_sums(blocks, kept, taken, field):
    lons, lats = field.shape
    rows = lons // blocks
    span = 192
    count = len(kept) + len(taken)
    offsets = np.arange(lats)
    lat_loc = jnp.asarray(taps(np.abs(offsets[:, None] - offsets[None, :])))
    reaches = (((0, 256), (0, 384)), ((256, 384), (128, 384)))
    lon_loc = jnp.asarray(
        taps(np.abs(np.arange(span)[:, None] + HALF - np.arange(span + 2 * HALF)[None, :]))
    )
    return pl.pallas_call(
        functools.partial(member_kernel, span, reaches),
        in_specs=[FAR] * count + [NEAR] * 3,
        out_shape=shape_of(blocks, rows + 4, lats),
        scratch_shapes=[
            pltpu.VMEM((lons, lats), F32),
            pltpu.VMEM((lons + 2 * HALF, lats), BF),
            pltpu.VMEM((lons + 16, lats), F32),
            pltpu.VMEM((count, lons, lats), BF),
            pltpu.SemaphoreType.DMA((count,)),
        ],
        compiler_params=PARAMS,
        cost_estimate=pl.CostEstimate(
            flops=4_000_000_000, bytes_accessed=6_000_000, transcendentals=0
        ),
        name="members",
    )(*[remote(value) for value in kept + taken], field, lat_loc, lon_loc)


def block_sums(groups, arrived):
    lines = arrived[0].shape[1]
    lats = sum(part.shape[2] for part in arrived)
    return pl.pallas_call(
        sum_kernel,
        out_shape=shape_of(groups, 2 * lines, lats),
        compiler_params=PARAMS,
        name="block_sum",
    )(*arrived)


def responses(scale, copies, slopes, front, back):
    rows = copies.shape[1] // 2 - 4
    hidden, lats = slopes.shape[1:]
    return pl.pallas_call(
        functools.partial(response_kernel, scale),
        out_shape=[wide_of(rows, 2, lats)] * 2,
        in_specs=[NEAR, FAR, NEAR, NEAR],
        scratch_shapes=[
            padded_scratch(rows + 4, lats),
            tap_scratch(rows + 4, lats),
            pltpu.VMEM((3, (rows + 2) * 8, lats), F32),
            padded_scratch(rows + 2, lats),
            pltpu.VMEM((rows + 2, hidden, lats), F32),
            pltpu.SemaphoreType.DMA((2,)),
        ],
        compiler_params=PARAMS,
        name="response",
    )(copies, remote(slopes), front, back)


def per_device(members, state, cotangent, conv_in, conv_out, bias):
    blocks = lax.axis_size("space")
    groups = lax.axis_size("mem")
    held, lons, var_count, lats = members.shape
    core = lax.axis_index("space") % 2
    swap = [(i, i ^ 1) for i in range(blocks)]
    chain = [(i, (i + 1 if i % 2 else i - 1) % blocks) for i in range(blocks)]
    tail = jnp.concatenate([state[-2:], cotangent[-2:]], axis=1)
    head = jnp.concatenate([state[:2], cotangent[:2]], axis=1)
    neighbour = lax.ppermute(jnp.where(core == 0, head, tail), "space", chain)
    partner = lax.ppermute(jnp.where(core == 0, tail, head), "space", swap)
    core = core.reshape(1)
    first = jnp.transpose(conv_in, (0, 1, 3, 2))
    front, back, state_taps, cot_taps, partial, cot_planes = prepare(
        state, cotangent, first, conv_out, bias
    )
    outgoing = gradient_planes(
        blocks, core, cot_planes, partner, neighbour, front, back, state_taps, cot_taps, partial
    )
    members, outgoing = lax.optimization_barrier((members, outgoing))
    gathered = lax.all_to_all(outgoing, "space", 0, 0, tiled=True)
    kept, given = member_planes(core, members)
    taken = [lax.ppermute(give, "space", swap) for give in given]
    slopes = hidden_slopes(core, partner, neighbour, front, state_taps)
    parts = member_sums(blocks, kept, taken, gathered.reshape(lons, lats))
    arrived = [lax.all_to_all(parts, "space", 0, 0, tiled=True)]
    spread = block_sums(groups, arrived)
    copies = lax.all_to_all(spread, "mem", 0, 0, tiled=True)
    member_count = held * blocks * groups
    increment, response = responses(1.0 / (member_count - 1.0), copies, slopes, front, back)
    return (increment, response)


def solution(mesh):
    in_specs = (
        P(("space", "mem"), None, None, None),
        P("space", None, None),
        P("space", None, None),
        P(),
        P(),
        P(),
    )
    out_specs = (P("space", None, None), P("space", None, None))
    return jax.shard_map(
        per_device, mesh=mesh, in_specs=in_specs, out_specs=out_specs, check_vma=False
    )
```

```python
import functools

import jax
import jax.numpy as jnp
import ml_dtypes
import numpy as np
from jax import lax
from jax.experimental import pallas as pl
from jax.experimental.pallas import tpu as pltpu
from jax.sharding import PartitionSpec as P

HALF = 16
GROUP = 32
BATCH = 11
BF = jnp.bfloat16
F32 = jnp.float32


def taps(distance):
    ratio = distance.astype(np.float32) / np.float32(HALF + 1.0)
    value = np.float32(1.0) - ratio * ratio
    return np.where(distance <= HALF, value, np.float32(0.0)).astype(ml_dtypes.bfloat16)


def shifted(value, step):
    if step == 1:
        return value
    lats = value.shape[-1]
    lane = lax.broadcasted_iota(jnp.int32, value.shape, value.ndim - 1)
    if step == 0:
        return jnp.where(lane == 0, 0.0, pltpu.roll(value, 1, value.ndim - 1))
    return jnp.where(lane == lats - 1, 0.0, pltpu.roll(value, lats - 1, value.ndim - 1))


def split_high_low(value):
    high = value.astype(BF)
    low = (value - high.astype(F32)).astype(BF)
    return high, low


def stack_taps(wide_ref, tap_ref):
    for tile in range(wide_ref.shape[0]):
        value = wide_ref[tile]
        rows = value.shape[0] // 8
        high = value.astype(BF).astype(F32)
        low = value - high
        high = high.reshape(rows, 1, 8, 128)
        low = low.reshape(rows, 1, 8, 128)
        both = jnp.concatenate([high, low, high, low], axis=1).reshape(rows * GROUP, 128)
        tap_ref[:, tile * 128 : (tile + 1) * 128] = both.astype(BF)


def put_taps(wide_ref, plane, first_row, var):
    rows = plane.shape[0]
    for step in range(3):
        moved = shifted(plane, step)
        for tile in range(wide_ref.shape[0]):
            start = first_row * 8 + 2 * step + var
            wide_ref[tile, pl.ds(start, rows, stride=8), :] = moved[:, tile * 128 : (tile + 1) * 128]


def put_ones(wide_ref, value):
    rows = wide_ref.shape[1] // 8
    for tile in range(wide_ref.shape[0]):
        wide_ref[tile, pl.ds(6, rows, stride=8), :] = jnp.full((rows, 128), value, F32)
        wide_ref[tile, pl.ds(7, rows, stride=8), :] = jnp.zeros((rows, 128), F32)


def fold_rows(hiddens, back_weight, product_ref, rows):
    lats = hiddens[0].shape[1]
    high, low = split_high_low(jnp.concatenate(hiddens, axis=1))
    product = jnp.dot(
        back_weight, jnp.concatenate([high, low], axis=0), preferred_element_type=F32
    )
    product = product[:24] + product[24:]
    for at, row in enumerate(rows):
        for step in range(3):
            product_ref[step, pl.ds(row * 8, 8), :] = product[
                8 * step : 8 * step + 8, at * lats : (at + 1) * lats
            ]


def backward_rows(front_ref, windows):
    activity = [jnp.dot(front_ref[0], state(), preferred_element_type=F32) for state, _ in windows]
    hidden = [jnp.dot(front_ref[1], cot(), preferred_element_type=F32) for _, cot in windows]
    for at in range(len(windows)):
        active = jnp.tanh(activity[at])
        hidden[at] = (1.0 - active * active) * hidden[at]
    return hidden


def window_of(ref, row):
    return lambda: ref[pl.ds(row * GROUP, 3 * GROUP), :]


def fold_lats(product_ref, fold_ref, first, count):
    window = pl.ds(first * 8, count * 8)
    total = (
        product_ref[1, window, :]
        + shifted(product_ref[0, window, :], 0)
        + shifted(product_ref[2, window, :], 2)
    )
    for tile in range(fold_ref.shape[0]):
        fold_ref[tile, window, :] = total[:, tile * 128 : (tile + 1) * 128]


def folded(fold_ref, rows, var):
    tiles = []
    for tile in range(fold_ref.shape[0]):
        tiles.append(
            sum(
                fold_ref[tile, pl.ds(10 * step + var, rows, stride=8), :] for step in range(3)
            )
        )
    return jnp.concatenate(tiles, axis=1)


def edges(core_ref, partner_ref, neighbour_ref):
    partner, neighbour = partner_ref[...], neighbour_ref[...]
    first = core_ref[0] == 0
    return jnp.where(first, neighbour, partner), jnp.where(first, partner, neighbour)


def fill_edges(before_ref, after_ref, var_from, wide_ref):
    for var in range(2):
        line = var_from + var
        for row in range(2):
            put_taps(wide_ref, before_ref[row, line : line + 1, :], row, var)
            put_taps(wide_ref, after_ref[row, line : line + 1, :], 2 + row, var)


def bands(tap_ref, edge_ref, frame_ref):
    half = 2 * GROUP
    last = tap_ref.shape[0] - half
    frame_ref[0:half, :] = edge_ref[0:half, :]
    frame_ref[half : 2 * half, :] = tap_ref[0:half, :]
    frame_ref[2 * half : 3 * half, :] = tap_ref[last : last + half, :]
    frame_ref[3 * half : 4 * half, :] = edge_ref[half : 2 * half, :]


def front_stack(rows_ref):
    value = rows_ref[...]
    high = value.astype(BF).astype(F32)
    low = value - high
    high = high.reshape(3, 1, 8, 128)
    low = low.reshape(3, 1, 8, 128)
    both = jnp.concatenate([high, high, low, low], axis=1).reshape(3 * GROUP, 128)
    return jnp.transpose(both).astype(BF)


def back_stack(rows_ref):
    value = rows_ref[...]
    high = value.astype(BF).astype(F32)
    both = jnp.concatenate([high, value - high], axis=0)
    return jnp.concatenate([both, both], axis=1).astype(BF)


def fetch(pairs, semaphores):
    copies = [
        pltpu.make_async_copy(source, target, semaphores.at[index])
        for index, (source, target) in enumerate(pairs)
    ]
    for copy in copies:
        copy.start()
    return copies


def prepare_kernel(
    state_far,
    cot_far,
    first_far,
    second_far,
    bias_far,
    front_ref,
    back_ref,
    state_taps,
    cot_taps,
    fold,
    cot_planes,
    wide,
    lines,
    product,
    state_ref,
    cot_ref,
    first_ref,
    second_ref,
    bias_ref,
    semaphores,
):
    rows = state_ref.shape[0]
    near = (first_ref, second_ref, bias_ref, state_ref, cot_ref)
    far = (first_far, second_far, bias_far, state_far, cot_far)
    copies = fetch(zip(far, near), semaphores)
    for copy in copies[:3]:
        copy.wait()
    for which in range(2):
        lines[...] = jnp.zeros_like(lines)
        for lon in range(3):
            for lat in range(3):
                start = 8 * lon + 2 * lat
                if which == 0:
                    lines[start : start + 2, :] = first_ref[lon, lat]
                else:
                    lines[start : start + 2, :] = second_ref[2 - lon, 2 - lat]
        if which == 0:
            lines[14:15, :] = bias_ref[...]
        front_ref[which] = front_stack(lines)
        lines[...] = jnp.zeros_like(lines)
        for lon in range(3):
            for lat in range(3):
                start = 8 * lat + 2 * lon
                if which == 0:
                    lines[start : start + 2, :] = first_ref[2 - lon, 2 - lat]
                else:
                    lines[start : start + 2, :] = second_ref[lon, lat]
        back_ref[which] = back_stack(lines)

    put_ones(wide, 1.0)
    for copy in copies[3:]:
        copy.wait()
    for main_ref, tap_ref in ((state_ref, state_taps), (cot_ref, cot_taps)):
        for var in range(2):
            plane = main_ref[:, var, :]
            if main_ref is cot_ref:
                cot_planes[var] = plane
            put_taps(wide, plane, 0, var)
        stack_taps(wide, tap_ref)

    for first in range(0, rows - 2, BATCH):
        batch = range(first, min(first + BATCH, rows - 2))
        hidden = backward_rows(
            front_ref, [(window_of(state_taps, row), window_of(cot_taps, row)) for row in batch]
        )
        fold_rows(hidden, back_ref[0], product, [row + 2 for row in batch])
    fold_lats(product, fold, 2, rows - 2)


def gradient_kernel(
    core_ref,
    cot_planes,
    partner_ref,
    neighbour_ref,
    front_ref,
    back_ref,
    state_taps,
    cot_taps,
    fold_ref,
    out_ref,
    wide,
    edge,
    state_frame,
    cot_frame,
    product,
    fold,
):
    rows = cot_planes.shape[1]
    before_ref, after_ref = edges(core_ref, partner_ref, neighbour_ref)
    put_ones(wide, 1.0)
    for var_from, tap_ref, frame_ref in ((0, state_taps, state_frame), (2, cot_taps, cot_frame)):
        fill_edges(before_ref, after_ref, var_from, wide)
        stack_taps(wide, edge)
        bands(tap_ref, edge, frame_ref)
    fold[...] = fold_ref[...]
    hidden = backward_rows(
        front_ref, [(window_of(state_frame, at), window_of(cot_frame, at)) for at in (0, 1, 4, 5)]
    )
    fold_rows(hidden, back_ref[0], product, (0, 1, rows, rows + 1))
    fold_lats(product, fold, 0, 2)
    fold_lats(product, fold, rows, 2)
    for var in range(2):
        plane = (cot_planes[var] + folded(fold, rows, var)).astype(BF)
        for pair in range(out_ref.shape[0] // 2):
            out_ref[2 * pair + var] = plane


def slopes_kernel(
    core_ref, partner_ref, neighbour_ref, front_ref, state_taps, out_ref, wide, edge, frame
):
    rows = out_ref.shape[0] - 2
    before_ref, after_ref = edges(core_ref, partner_ref, neighbour_ref)
    put_ones(wide, 1.0)
    fill_edges(before_ref, after_ref, 0, wide)
    stack_taps(wide, edge)
    bands(state_taps, edge, frame)

    windows = [window_of(frame, at) for at in (0, 1)]
    windows += [window_of(state_taps, row) for row in range(rows - 2)]
    windows += [window_of(frame, at) for at in (4, 5)]
    for first in range(0, rows + 2, BATCH):
        batch = range(first, min(first + BATCH, rows + 2))
        dots = [jnp.dot(front_ref[0], windows[row](), preferred_element_type=F32) for row in batch]
        for row, value in zip(batch, dots):
            active = jnp.tanh(value)
            out_ref[row] = 1.0 - active * active


def response_kernel(
    scale,
    copies_ref,
    slopes_far,
    front_ref,
    back_ref,
    incr_out,
    resp_out,
    wide,
    incr_taps,
    product,
    fold,
    slopes_ref,
    semaphores,
):
    rows = incr_out.shape[0]
    half = (rows + 2) // 2
    halves = [pl.ds(0, half), pl.ds(half, half)]
    copies = fetch([(slopes_far.at[part], slopes_ref.at[part]) for part in halves], semaphores)
    planes = []
    put_ones(wide, 0.0)
    for var in range(2):
        window = pl.ds(var * (rows + 4), rows + 4)
        plane = copies_ref[0, window, :].astype(F32)
        for group in range(1, copies_ref.shape[0]):
            plane = plane + copies_ref[group, window, :].astype(F32)
        plane = plane * scale
        planes.append(plane)
        put_taps(wide, plane, 0, var)
    stack_taps(wide, incr_taps)

    for part in range(2):
        batch = range(part * half, (part + 1) * half)
        hidden = [
            jnp.dot(front_ref[0], window_of(incr_taps, row)(), preferred_element_type=F32)
            for row in batch
        ]
        copies[part].wait()
        hidden = [slopes_ref[row] * value for row, value in zip(batch, hidden)]
        fold_rows(hidden, back_ref[1], product, batch)
    fold_lats(product, fold, 0, rows + 2)
    for var in range(2):
        increment = planes[var][2 : 2 + rows]
        incr_out[:, var, :] = increment
        resp_out[:, var, :] = increment + folded(fold, rows, var)


def planes_kernel(core_ref, members_far, *refs):
    *outs, near, lines, planes, in_semaphores, out_semaphores = refs
    core = core_ref[0]
    count, tiles, lines_count = near.shape[:3]
    rows = lines_count // 2
    merged = members_far.reshape(count, lines_count, tiles * 128)
    pairs = [
        (merged.at[member, :, pl.ds(tile * 128, 128)], near.at[member, tile])
        for member in range(count)
        for tile in range(tiles)
    ]
    arrivals = fetch(pairs, in_semaphores)
    departures = []
    for member in range(count):
        for tile in range(tiles):
            arrivals[member * tiles + tile].wait()
            lines[...] = near[member, tile].astype(F32)
            window = pl.ds(tile * 128, 128)
            planes[member, :, window] = lines[pl.ds(core, rows, stride=2), :].astype(BF)
            planes[count + member, :, window] = lines[pl.ds(1 - core, rows, stride=2), :].astype(BF)
        for slot in (count + member, member):
            copy = pltpu.make_async_copy(planes.at[slot], outs[slot], out_semaphores.at[slot])
            copy.start()
            departures.append(copy)
    for copy in departures:
        copy.wait()


def member_kernel(span, reaches, *refs):
    *far_refs, field_ref, lat_ref, lon_ref, out_ref, field, banded, total, held, semaphores = refs
    lons = field_ref.shape[0]
    blocks = out_ref.shape[0]
    rows = lons // blocks
    member_refs = [held.at[index] for index in range(len(far_refs))]
    copies = fetch(zip(far_refs, member_refs), semaphores)
    field[...] = field_ref[...].astype(F32)
    lats = field_ref.shape[1]
    chunk = 2 * span
    for index, member_ref in enumerate(member_refs):
        copies[index].wait()
        at = index * lats
        for start in range(0, lons, chunk):
            window = pl.ds(start, chunk)
            product = (member_ref[window, :].astype(F32) * field[window, :]).astype(BF)
            for (first, last), (low, high) in reaches:
                banded[pl.ds(HALF + start, chunk), at + first : at + last] = jnp.dot(
                    product[:, low:high], lat_ref[low:high, first:last], preferred_element_type=F32
                ).astype(BF)
    banded[pl.ds(0, HALF), :] = banded[pl.ds(lons, HALF), :]
    banded[pl.ds(HALF + lons, HALF), :] = banded[pl.ds(HALF, HALF), :]
    for start in range(0, lons, span):
        value = None
        for index, member_ref in enumerate(member_refs):
            at = index * lats
            spread = jnp.dot(
                lon_ref[...],
                banded[pl.ds(start, span + 2 * HALF), at : at + lats],
                preferred_element_type=F32,
            )
            term = member_ref[pl.ds(start, span), :].astype(F32) * spread
            value = term if value is None else value + term
        total[pl.ds(8 + start, span), :] = value
    total[pl.ds(0, 8), :] = total[pl.ds(lons, 8), :]
    total[pl.ds(lons + 8, 8), :] = total[pl.ds(8, 8), :]
    for block in range(blocks):
        out_ref[block] = total[pl.ds(6 + block * rows, rows + 4), :].astype(BF)


def sum_kernel(*refs):
    *parts_refs, out_ref = refs
    start = 0
    for parts_ref in parts_refs:
        lines, lats = parts_ref.shape[1:]
        for var in range(2):
            plane = parts_ref[var].astype(F32)
            for pair in range(1, parts_ref.shape[0] // 2):
                plane = plane + parts_ref[2 * pair + var].astype(F32)
            plane = plane.astype(BF)
            for group in range(out_ref.shape[0]):
                out_ref[group, pl.ds(var * lines, lines), pl.ds(start, lats)] = plane
        start += lats


def shape_of(*dims):
    return jax.ShapeDtypeStruct(dims, BF)


def wide_of(*dims):
    return jax.ShapeDtypeStruct(dims, F32)


FAR = pl.BlockSpec(memory_space=pltpu.HBM)
SCALAR = pl.BlockSpec(memory_space=pltpu.SMEM)
NEAR = pl.BlockSpec(memory_space=pltpu.VMEM)
PARAMS = pltpu.CompilerParams(vmem_limit_bytes=24 << 20)


def remote(value):
    return pltpu.with_memory_space_constraint(value, pltpu.HBM)


def padded_scratch(count, lats):
    return pltpu.VMEM((lats // 128, count * 8, 128), F32)


def tap_scratch(count, lats):
    return pltpu.VMEM((count * GROUP, lats), BF)


def prepare(state, cotangent, first, second, bias):
    rows, var_count, lats = state.shape
    hidden = first.shape[-1]
    operands = (state, cotangent, first, second, bias.reshape(1, hidden))
    return pl.pallas_call(
        prepare_kernel,
        out_shape=[
            shape_of(2, hidden, 3 * GROUP),
            shape_of(2, 48, 2 * hidden),
            shape_of(rows * GROUP, lats),
            shape_of(rows * GROUP, lats),
            wide_of(lats // 128, (rows + 2) * 8, 128),
            wide_of(var_count, rows, lats),
        ],
        in_specs=[FAR] * 5,
        scratch_shapes=[
            padded_scratch(rows, lats),
            pltpu.VMEM((24, hidden), F32),
            pltpu.VMEM((3, (rows + 2) * 8, lats), F32),
            pltpu.VMEM(state.shape, F32),
            pltpu.VMEM(state.shape, F32),
            pltpu.VMEM(first.shape, F32),
            pltpu.VMEM(second.shape, F32),
            pltpu.VMEM((1, hidden), F32),
            pltpu.SemaphoreType.DMA((5,)),
        ],
        compiler_params=PARAMS,
        cost_estimate=pl.CostEstimate(
            flops=2_000_000_000, bytes_accessed=3_000_000, transcendentals=1_100_000
        ),
        name="prepare",
    )(*[remote(value) for value in operands])


def gradient_planes(
    blocks, core, cot_planes, partner, neighbour, front, back, state_taps, cot_taps, partial
):
    var_count, rows, lats = cot_planes.shape
    return pl.pallas_call(
        gradient_kernel,
        out_shape=shape_of(blocks, rows, lats),
        in_specs=[SCALAR] + [NEAR] * 8,
        scratch_shapes=[
            padded_scratch(4, lats),
            tap_scratch(4, lats),
            tap_scratch(8, lats),
            tap_scratch(8, lats),
            pltpu.VMEM((3, (rows + 2) * 8, lats), F32),
            padded_scratch(rows + 2, lats),
        ],
        compiler_params=PARAMS,
        cost_estimate=pl.CostEstimate(
            flops=400_000_000, bytes_accessed=1_500_000, transcendentals=200_000
        ),
        name="gradient",
    )(core, cot_planes, partner, neighbour, front, back, state_taps, cot_taps, partial)


def member_planes(core, members):
    count, lons, var_count, lats = members.shape
    results = pl.pallas_call(
        planes_kernel,
        in_specs=[SCALAR, FAR],
        out_specs=[FAR] * (2 * count),
        out_shape=[pltpu.HBM((lons, lats), BF)] * (2 * count),
        scratch_shapes=[
            pltpu.VMEM((count, lats // 128, lons * var_count, 128), BF),
            pltpu.VMEM((lons * 2, 128), F32),
            pltpu.VMEM((2 * count, lons, lats), BF),
            pltpu.SemaphoreType.DMA((count * (lats // 128),)),
            pltpu.SemaphoreType.DMA((2 * count,)),
        ],
        compiler_params=PARAMS,
        cost_estimate=pl.CostEstimate(flops=0, bytes_accessed=10_000_000, transcendentals=0),
        name="planes",
    )(core, remote(members))
    return list(results[:count]), list(results[count:])


def hidden_slopes(core, partner, neighbour, front, state_taps):
    rows = state_taps.shape[0] // GROUP
    hidden, lats = front.shape[1], state_taps.shape[1]
    return pl.pallas_call(
        slopes_kernel,
        out_shape=pltpu.HBM((rows + 2, hidden, lats), F32),
        in_specs=[SCALAR] + [NEAR] * 4,
        out_specs=NEAR,
        scratch_shapes=[padded_scratch(4, lats), tap_scratch(4, lats), tap_scratch(8, lats)],
        compiler_params=PARAMS,
        cost_estimate=pl.CostEstimate(
            flops=1_000_000_000, bytes_accessed=6_000_000, transcendentals=1_200_000
        ),
        name="slopes",
    )(core, partner, neighbour, front, state_taps)


def member_sums(blocks, kept, taken, field):
    lons, lats = field.shape
    rows = lons // blocks
    span = 96
    count = len(kept) + len(taken)
    offsets = np.arange(lats)
    lat_loc = jnp.asarray(taps(np.abs(offsets[:, None] - offsets[None, :])))
    reaches = (((0, 256), (0, 384)), ((256, 384), (128, 384)))
    lon_loc = jnp.asarray(
        taps(np.abs(np.arange(span)[:, None] + HALF - np.arange(span + 2 * HALF)[None, :]))
    )
    return pl.pallas_call(
        functools.partial(member_kernel, span, reaches),
        in_specs=[FAR] * len(kept) + [pl.BlockSpec(memory_space=pl.ANY)] * len(taken) + [NEAR] * 3,
        out_shape=shape_of(blocks, rows + 4, lats),
        scratch_shapes=[
            pltpu.VMEM((lons, lats), F32),
            pltpu.VMEM((lons + 2 * HALF, count * lats), BF),
            pltpu.VMEM((lons + 16, lats), F32),
            pltpu.VMEM((count, lons, lats), BF),
            pltpu.SemaphoreType.DMA((count,)),
        ],
        compiler_params=PARAMS,
        cost_estimate=pl.CostEstimate(
            flops=4_000_000_000, bytes_accessed=6_000_000, transcendentals=0
        ),
        name="members",
    )(*[remote(value) for value in kept], *taken, field, lat_loc, lon_loc)


def block_sums(groups, arrived):
    lines = arrived[0].shape[1]
    lats = sum(part.shape[2] for part in arrived)
    return pl.pallas_call(
        sum_kernel,
        out_shape=shape_of(groups, 2 * lines, lats),
        compiler_params=PARAMS,
        name="block_sum",
    )(*arrived)


def responses(scale, copies, slopes, front, back):
    rows = copies.shape[1] // 2 - 4
    hidden, lats = slopes.shape[1:]
    return pl.pallas_call(
        functools.partial(response_kernel, scale),
        out_shape=[wide_of(rows, 2, lats)] * 2,
        in_specs=[NEAR, FAR, NEAR, NEAR],
        scratch_shapes=[
            padded_scratch(rows + 4, lats),
            tap_scratch(rows + 4, lats),
            pltpu.VMEM((3, (rows + 2) * 8, lats), F32),
            padded_scratch(rows + 2, lats),
            pltpu.VMEM((rows + 2, hidden, lats), F32),
            pltpu.SemaphoreType.DMA((2,)),
        ],
        compiler_params=PARAMS,
        name="response",
    )(copies, remote(slopes), front, back)


def per_device(members, state, cotangent, conv_in, conv_out, bias):
    blocks = lax.axis_size("space")
    groups = lax.axis_size("mem")
    held, lons, var_count, lats = members.shape
    core = lax.axis_index("space") % 2
    swap = [(i, i ^ 1) for i in range(blocks)]
    chain = [(i, (i + 1 if i % 2 else i - 1) % blocks) for i in range(blocks)]
    tail = jnp.concatenate([state[-2:], cotangent[-2:]], axis=1)
    head = jnp.concatenate([state[:2], cotangent[:2]], axis=1)
    neighbour = lax.ppermute(jnp.where(core == 0, head, tail), "space", chain)
    partner = lax.ppermute(jnp.where(core == 0, tail, head), "space", swap)
    core = core.reshape(1)
    first = jnp.transpose(conv_in, (0, 1, 3, 2))
    front, back, state_taps, cot_taps, partial, cot_planes = prepare(
        state, cotangent, first, conv_out, bias
    )
    outgoing = gradient_planes(
        blocks, core, cot_planes, partner, neighbour, front, back, state_taps, cot_taps, partial
    )
    members, outgoing = lax.optimization_barrier((members, outgoing))
    gathered = lax.all_to_all(outgoing, "space", 0, 0, tiled=True)
    kept, given = member_planes(core, members)
    taken = [lax.ppermute(give, "space", swap) for give in given]
    slopes = hidden_slopes(core, partner, neighbour, front, state_taps)
    gathered, slopes = lax.optimization_barrier((gathered, slopes))
    parts = member_sums(blocks, kept, taken, gathered.reshape(lons, lats))
    arrived = [lax.all_to_all(parts, "space", 0, 0, tiled=True)]
    spread = block_sums(groups, arrived)
    copies = lax.all_to_all(spread, "mem", 0, 0, tiled=True)
    member_count = held * blocks * groups
    increment, response = responses(1.0 / (member_count - 1.0), copies, slopes, front, back)
    return (increment, response)


def solution(mesh):
    in_specs = (
        P(("space", "mem"), None, None, None),
        P("space", None, None),
        P("space", None, None),
        P(),
        P(),
        P(),
    )
    out_specs = (P("space", None, None), P("space", None, None))
    return jax.shard_map(
        per_device, mesh=mesh, in_specs=in_specs, out_specs=out_specs, check_vma=False
    )
```

```python
import functools

import jax
import jax.numpy as jnp
import ml_dtypes
import numpy as np
from jax import lax
from jax.experimental import pallas as pl
from jax.experimental.pallas import tpu as pltpu
from jax.sharding import PartitionSpec as P

HALF = 16
GROUP = 32
BATCH = 11
BF = jnp.bfloat16
F32 = jnp.float32


def taps(distance):
    ratio = distance.astype(np.float32) / np.float32(HALF + 1.0)
    value = np.float32(1.0) - ratio * ratio
    return np.where(distance <= HALF, value, np.float32(0.0)).astype(ml_dtypes.bfloat16)


def shifted(value, step):
    if step == 1:
        return value
    lats = value.shape[-1]
    lane = lax.broadcasted_iota(jnp.int32, value.shape, value.ndim - 1)
    if step == 0:
        return jnp.where(lane == 0, 0.0, pltpu.roll(value, 1, value.ndim - 1))
    return jnp.where(lane == lats - 1, 0.0, pltpu.roll(value, lats - 1, value.ndim - 1))


def split_high_low(value):
    high = value.astype(BF)
    low = (value - high.astype(F32)).astype(BF)
    return high, low


def stack_taps(wide_ref, tap_ref):
    for tile in range(wide_ref.shape[0]):
        value = wide_ref[tile]
        rows = value.shape[0] // 8
        high = value.astype(BF).astype(F32)
        low = value - high
        high = high.reshape(rows, 1, 8, 128)
        low = low.reshape(rows, 1, 8, 128)
        both = jnp.concatenate([high, low, high, low], axis=1).reshape(rows * GROUP, 128)
        tap_ref[:, tile * 128 : (tile + 1) * 128] = both.astype(BF)


def put_taps(wide_ref, plane, first_row, var):
    rows = plane.shape[0]
    for step in range(3):
        moved = shifted(plane, step)
        for tile in range(wide_ref.shape[0]):
            start = first_row * 8 + 2 * step + var
            wide_ref[tile, pl.ds(start, rows, stride=8), :] = moved[:, tile * 128 : (tile + 1) * 128]


def put_ones(wide_ref, value):
    rows = wide_ref.shape[1] // 8
    for tile in range(wide_ref.shape[0]):
        wide_ref[tile, pl.ds(6, rows, stride=8), :] = jnp.full((rows, 128), value, F32)
        wide_ref[tile, pl.ds(7, rows, stride=8), :] = jnp.zeros((rows, 128), F32)


def fold_rows(hiddens, back_weight, product_ref, rows):
    lats = hiddens[0].shape[1]
    high, low = split_high_low(jnp.concatenate(hiddens, axis=1))
    product = jnp.dot(
        back_weight, jnp.concatenate([high, low], axis=0), preferred_element_type=F32
    )
    product = product[:24] + product[24:]
    for at, row in enumerate(rows):
        for step in range(3):
            product_ref[step, pl.ds(row * 8, 8), :] = product[
                8 * step : 8 * step + 8, at * lats : (at + 1) * lats
            ]


def backward_rows(front_ref, windows):
    activity = [jnp.dot(front_ref[0], state(), preferred_element_type=F32) for state, _ in windows]
    hidden = [jnp.dot(front_ref[1], cot(), preferred_element_type=F32) for _, cot in windows]
    for at in range(len(windows)):
        active = jnp.tanh(activity[at])
        hidden[at] = (1.0 - active * active) * hidden[at]
    return hidden


def window_of(ref, row):
    return lambda: ref[pl.ds(row * GROUP, 3 * GROUP), :]


def fold_lats(product_ref, fold_ref, first, count):
    window = pl.ds(first * 8, count * 8)
    total = (
        product_ref[1, window, :]
        + shifted(product_ref[0, window, :], 0)
        + shifted(product_ref[2, window, :], 2)
    )
    for tile in range(fold_ref.shape[0]):
        fold_ref[tile, window, :] = total[:, tile * 128 : (tile + 1) * 128]


def folded(fold_ref, rows, var):
    tiles = []
    for tile in range(fold_ref.shape[0]):
        tiles.append(
            sum(
                fold_ref[tile, pl.ds(10 * step + var, rows, stride=8), :] for step in range(3)
            )
        )
    return jnp.concatenate(tiles, axis=1)


def edges(core_ref, partner_ref, neighbour_ref):
    partner, neighbour = partner_ref[...], neighbour_ref[...]
    first = core_ref[0] == 0
    return jnp.where(first, neighbour, partner), jnp.where(first, partner, neighbour)


def fill_edges(before_ref, after_ref, var_from, wide_ref):
    for var in range(2):
        line = var_from + var
        for row in range(2):
            put_taps(wide_ref, before_ref[row, line : line + 1, :], row, var)
            put_taps(wide_ref, after_ref[row, line : line + 1, :], 2 + row, var)


def bands(tap_ref, edge_ref, frame_ref):
    half = 2 * GROUP
    last = tap_ref.shape[0] - half
    frame_ref[0:half, :] = edge_ref[0:half, :]
    frame_ref[half : 2 * half, :] = tap_ref[0:half, :]
    frame_ref[2 * half : 3 * half, :] = tap_ref[last : last + half, :]
    frame_ref[3 * half : 4 * half, :] = edge_ref[half : 2 * half, :]


def front_stack(rows_ref):
    value = rows_ref[...]
    high = value.astype(BF).astype(F32)
    low = value - high
    high = high.reshape(3, 1, 8, 128)
    low = low.reshape(3, 1, 8, 128)
    both = jnp.concatenate([high, high, low, low], axis=1).reshape(3 * GROUP, 128)
    return jnp.transpose(both).astype(BF)


def back_stack(rows_ref):
    value = rows_ref[...]
    high = value.astype(BF).astype(F32)
    both = jnp.concatenate([high, value - high], axis=0)
    return jnp.concatenate([both, both], axis=1).astype(BF)


def fetch(pairs, semaphores):
    copies = [
        pltpu.make_async_copy(source, target, semaphores.at[index])
        for index, (source, target) in enumerate(pairs)
    ]
    for copy in copies:
        copy.start()
    return copies


def prepare_kernel(
    state_far,
    cot_far,
    first_far,
    second_far,
    bias_far,
    front_ref,
    back_ref,
    state_taps,
    cot_taps,
    fold,
    cot_planes,
    wide,
    lines,
    product,
    state_ref,
    cot_ref,
    first_ref,
    second_ref,
    bias_ref,
    semaphores,
):
    rows = state_ref.shape[0]
    near = (first_ref, second_ref, bias_ref, state_ref, cot_ref)
    far = (first_far, second_far, bias_far, state_far, cot_far)
    copies = fetch(zip(far, near), semaphores)
    for copy in copies[:3]:
        copy.wait()
    for which in range(2):
        lines[...] = jnp.zeros_like(lines)
        for lon in range(3):
            for lat in range(3):
                start = 8 * lon + 2 * lat
                if which == 0:
                    lines[start : start + 2, :] = first_ref[lon, lat]
                else:
                    lines[start : start + 2, :] = second_ref[2 - lon, 2 - lat]
        if which == 0:
            lines[14:15, :] = bias_ref[...]
        front_ref[which] = front_stack(lines)
        lines[...] = jnp.zeros_like(lines)
        for lon in range(3):
            for lat in range(3):
                start = 8 * lat + 2 * lon
                if which == 0:
                    lines[start : start + 2, :] = first_ref[2 - lon, 2 - lat]
                else:
                    lines[start : start + 2, :] = second_ref[lon, lat]
        back_ref[which] = back_stack(lines)

    put_ones(wide, 1.0)
    for copy in copies[3:]:
        copy.wait()
    for main_ref, tap_ref in ((state_ref, state_taps), (cot_ref, cot_taps)):
        for var in range(2):
            plane = main_ref[:, var, :]
            if main_ref is cot_ref:
                cot_planes[var] = plane
            put_taps(wide, plane, 0, var)
        stack_taps(wide, tap_ref)

    for first in range(0, rows - 2, BATCH):
        batch = range(first, min(first + BATCH, rows - 2))
        hidden = backward_rows(
            front_ref, [(window_of(state_taps, row), window_of(cot_taps, row)) for row in batch]
        )
        fold_rows(hidden, back_ref[0], product, [row + 2 for row in batch])
    fold_lats(product, fold, 2, rows - 2)


def gradient_kernel(
    core_ref,
    cot_planes,
    partner_ref,
    neighbour_ref,
    front_ref,
    back_ref,
    state_taps,
    cot_taps,
    fold_ref,
    out_ref,
    wide,
    edge,
    state_frame,
    cot_frame,
    product,
    fold,
):
    rows = cot_planes.shape[1]
    before_ref, after_ref = edges(core_ref, partner_ref, neighbour_ref)
    put_ones(wide, 1.0)
    for var_from, tap_ref, frame_ref in ((0, state_taps, state_frame), (2, cot_taps, cot_frame)):
        fill_edges(before_ref, after_ref, var_from, wide)
        stack_taps(wide, edge)
        bands(tap_ref, edge, frame_ref)
    fold[...] = fold_ref[...]
    hidden = backward_rows(
        front_ref, [(window_of(state_frame, at), window_of(cot_frame, at)) for at in (0, 1, 4, 5)]
    )
    fold_rows(hidden, back_ref[0], product, (0, 1, rows, rows + 1))
    fold_lats(product, fold, 0, 2)
    fold_lats(product, fold, rows, 2)
    for var in range(2):
        plane = (cot_planes[var] + folded(fold, rows, var)).astype(BF)
        for pair in range(out_ref.shape[0] // 2):
            out_ref[2 * pair + var] = plane


def slopes_kernel(
    core_ref, partner_ref, neighbour_ref, front_ref, state_taps, out_ref, wide, edge, frame
):
    rows = out_ref.shape[0] - 2
    before_ref, after_ref = edges(core_ref, partner_ref, neighbour_ref)
    put_ones(wide, 1.0)
    fill_edges(before_ref, after_ref, 0, wide)
    stack_taps(wide, edge)
    bands(state_taps, edge, frame)

    windows = [window_of(frame, at) for at in (0, 1)]
    windows += [window_of(state_taps, row) for row in range(rows - 2)]
    windows += [window_of(frame, at) for at in (4, 5)]
    for first in range(0, rows + 2, BATCH):
        batch = range(first, min(first + BATCH, rows + 2))
        dots = [jnp.dot(front_ref[0], windows[row](), preferred_element_type=F32) for row in batch]
        for row, value in zip(batch, dots):
            active = jnp.tanh(value)
            out_ref[row] = 1.0 - active * active


def response_kernel(
    scale,
    copies_ref,
    slopes_far,
    front_ref,
    back_ref,
    incr_out,
    resp_out,
    wide,
    incr_taps,
    product,
    fold,
    slopes_ref,
    tail,
    semaphores,
):
    rows = incr_out.shape[0]
    half = (rows + 2) // 2
    halves = [pl.ds(0, half), pl.ds(half, half)]
    copies = fetch([(slopes_far.at[part], slopes_ref.at[part]) for part in halves], semaphores)
    planes = []
    put_ones(wide, 0.0)
    groups = copies_ref.shape[0]
    lane = lax.broadcasted_iota(jnp.int32, (rows + 4, 128), 1)
    for var in range(2):
        fronts, tails = [], []
        for half_of in range(2):
            window = pl.ds(var * 48, 48)
            members = [group for group in range(groups) if (group // 2) % 2 == half_of]
            value = sum(copies_ref[group, window, :].astype(F32) for group in members)
            fronts.append(value[0 : rows + 4])
            packed = value[32:46]
            tail[pl.ds(0, 14), :] = packed
            tail[pl.ds(14, 14), :] = pltpu.roll(packed, 64, 1)
            tails.append(tail[pl.ds(0, rows + 4), :])
        middle = pltpu.roll(fronts[1], 64, 1)
        plane = jnp.concatenate(
            [
                fronts[0],
                jnp.where(lane < 64, tails[0], middle),
                jnp.where(lane < 64, middle, pltpu.roll(tails[1], 64, 1)),
            ],
            axis=1,
        )
        plane = plane * scale
        planes.append(plane)
        put_taps(wide, plane, 0, var)
    stack_taps(wide, incr_taps)

    for part in range(2):
        batch = range(part * half, (part + 1) * half)
        hidden = [
            jnp.dot(front_ref[0], window_of(incr_taps, row)(), preferred_element_type=F32)
            for row in batch
        ]
        copies[part].wait()
        hidden = [slopes_ref[row] * value for row, value in zip(batch, hidden)]
        fold_rows(hidden, back_ref[1], product, batch)
    fold_lats(product, fold, 0, rows + 2)
    for var in range(2):
        increment = planes[var][2 : 2 + rows]
        incr_out[:, var, :] = increment
        resp_out[:, var, :] = increment + folded(fold, rows, var)


def planes_kernel(core_ref, members_far, *refs):
    *outs, near, lines, planes, in_semaphores, out_semaphores = refs
    core = core_ref[0]
    count, tiles, lines_count = near.shape[:3]
    rows = lines_count // 2
    merged = members_far.reshape(count, lines_count, tiles * 128)
    pairs = [
        (merged.at[member, :, pl.ds(tile * 128, 128)], near.at[member, tile])
        for member in range(count)
        for tile in range(tiles)
    ]
    arrivals = fetch(pairs, in_semaphores)
    departures = []
    for member in range(count):
        for tile in range(tiles):
            arrivals[member * tiles + tile].wait()
            lines[...] = near[member, tile].astype(F32)
            window = pl.ds(tile * 128, 128)
            planes[member, :, window] = lines[pl.ds(core, rows, stride=2), :].astype(BF)
            planes[count + member, :, window] = lines[pl.ds(1 - core, rows, stride=2), :].astype(BF)
        for slot in (count + member, member):
            copy = pltpu.make_async_copy(planes.at[slot], outs[slot], out_semaphores.at[slot])
            copy.start()
            departures.append(copy)
    for copy in departures:
        copy.wait()


def member_kernel(span, half_ref, *refs):
    *far_refs, field_ref, lat_ref, lon_ref, out_ref, field, banded, total, held, semaphores = refs
    lons = field_ref.shape[0]
    blocks = out_ref.shape[0]
    rows = lons // blocks
    wide = 2 * 128
    half = half_ref[0]
    reach = pl.ds(pl.multiple_of(half * 128, 128), wide)
    member_refs = [held.at[index] for index in range(len(far_refs))]
    copies = fetch([(far.at[:, reach], near) for far, near in zip(far_refs, member_refs)], semaphores)
    field[...] = field_ref[:, reach].astype(F32)
    lat_loc = lat_ref[half]
    chunk = 2 * span
    for index, member_ref in enumerate(member_refs):
        copies[index].wait()
        at = index * wide
        for start in range(0, lons, chunk):
            window = pl.ds(start, chunk)
            product = (member_ref[window, :].astype(F32) * field[window, :]).astype(BF)
            banded[pl.ds(HALF + start, chunk), at : at + wide] = jnp.dot(
                product, lat_loc, preferred_element_type=F32
            ).astype(BF)
    banded[pl.ds(0, HALF), :] = banded[pl.ds(lons, HALF), :]
    banded[pl.ds(HALF + lons, HALF), :] = banded[pl.ds(HALF, HALF), :]
    for start in range(0, lons, span):
        value = None
        for index, member_ref in enumerate(member_refs):
            at = index * wide
            spread = jnp.dot(
                lon_ref[...],
                banded[pl.ds(start, span + 2 * HALF), at : at + wide],
                preferred_element_type=F32,
            )
            term = member_ref[pl.ds(start, span), :].astype(F32) * spread
            value = term if value is None else value + term
        total[pl.ds(8 + start, span), :] = jnp.where(half == 0, value, pltpu.roll(value, 192, 1))
    total[pl.ds(0, 8), :] = total[pl.ds(lons, 8), :]
    total[pl.ds(lons + 8, 8), :] = total[pl.ds(8, 8), :]
    lane = lax.broadcasted_iota(jnp.int32, (16, 128), 1)
    for block in range(blocks):
        top = 6 + block * rows
        out_ref[block, 0:32, :] = total[pl.ds(top, 32), 0:128].astype(out_ref.dtype)
        near = total[pl.ds(top, 16), 128:256]
        next_rows = total[pl.ds(top + 14, 16), 128:256]
        packed = jnp.where(lane < 64, near, pltpu.roll(next_rows, 64, 1))
        out_ref[block, 32:48, :] = packed.astype(out_ref.dtype)


def add_kernel(own_ref, other_ref, out_ref):
    out_ref[...] = (own_ref[...] + other_ref[...].astype(F32)).astype(BF)


def sum_kernel(*refs):
    *parts_refs, out_ref = refs
    start = 0
    for parts_ref in parts_refs:
        lines, lats = parts_ref.shape[1:]
        for var in range(2):
            plane = parts_ref[var].astype(F32)
            for pair in range(1, parts_ref.shape[0] // 2):
                plane = plane + parts_ref[2 * pair + var].astype(F32)
            plane = plane.astype(BF)
            for group in range(out_ref.shape[0]):
                out_ref[group, pl.ds(var * lines, lines), pl.ds(start, lats)] = plane
        start += lats


def shape_of(*dims):
    return jax.ShapeDtypeStruct(dims, BF)


def wide_of(*dims):
    return jax.ShapeDtypeStruct(dims, F32)


FAR = pl.BlockSpec(memory_space=pltpu.HBM)
SCALAR = pl.BlockSpec(memory_space=pltpu.SMEM)
NEAR = pl.BlockSpec(memory_space=pltpu.VMEM)
PARAMS = pltpu.CompilerParams(vmem_limit_bytes=24 << 20)


def remote(value):
    return pltpu.with_memory_space_constraint(value, pltpu.HBM)


def padded_scratch(count, lats):
    return pltpu.VMEM((lats // 128, count * 8, 128), F32)


def tap_scratch(count, lats):
    return pltpu.VMEM((count * GROUP, lats), BF)


def prepare(state, cotangent, first, second, bias):
    rows, var_count, lats = state.shape
    hidden = first.shape[-1]
    operands = (state, cotangent, first, second, bias.reshape(1, hidden))
    return pl.pallas_call(
        prepare_kernel,
        out_shape=[
            shape_of(2, hidden, 3 * GROUP),
            shape_of(2, 48, 2 * hidden),
            shape_of(rows * GROUP, lats),
            shape_of(rows * GROUP, lats),
            wide_of(lats // 128, (rows + 2) * 8, 128),
            wide_of(var_count, rows, lats),
        ],
        in_specs=[FAR] * 5,
        scratch_shapes=[
            padded_scratch(rows, lats),
            pltpu.VMEM((24, hidden), F32),
            pltpu.VMEM((3, (rows + 2) * 8, lats), F32),
            pltpu.VMEM(state.shape, F32),
            pltpu.VMEM(state.shape, F32),
            pltpu.VMEM(first.shape, F32),
            pltpu.VMEM(second.shape, F32),
            pltpu.VMEM((1, hidden), F32),
            pltpu.SemaphoreType.DMA((5,)),
        ],
        compiler_params=PARAMS,
        cost_estimate=pl.CostEstimate(
            flops=2_000_000_000, bytes_accessed=3_000_000, transcendentals=1_100_000
        ),
        name="prepare",
    )(*[remote(value) for value in operands])


def gradient_planes(
    blocks, core, cot_planes, partner, neighbour, front, back, state_taps, cot_taps, partial
):
    var_count, rows, lats = cot_planes.shape
    return pl.pallas_call(
        gradient_kernel,
        out_shape=shape_of(blocks, rows, lats),
        in_specs=[SCALAR] + [NEAR] * 8,
        scratch_shapes=[
            padded_scratch(4, lats),
            tap_scratch(4, lats),
            tap_scratch(8, lats),
            tap_scratch(8, lats),
            pltpu.VMEM((3, (rows + 2) * 8, lats), F32),
            padded_scratch(rows + 2, lats),
        ],
        compiler_params=PARAMS,
        cost_estimate=pl.CostEstimate(
            flops=400_000_000, bytes_accessed=1_500_000, transcendentals=200_000
        ),
        name="gradient",
    )(core, cot_planes, partner, neighbour, front, back, state_taps, cot_taps, partial)


def member_planes(core, members):
    count, lons, var_count, lats = members.shape
    results = pl.pallas_call(
        planes_kernel,
        in_specs=[SCALAR, FAR],
        out_specs=[FAR] * (2 * count),
        out_shape=[pltpu.HBM((lons, lats), BF)] * (2 * count),
        scratch_shapes=[
            pltpu.VMEM((count, lats // 128, lons * var_count, 128), BF),
            pltpu.VMEM((lons * 2, 128), F32),
            pltpu.VMEM((2 * count, lons, lats), BF),
            pltpu.SemaphoreType.DMA((count * (lats // 128),)),
            pltpu.SemaphoreType.DMA((2 * count,)),
        ],
        compiler_params=PARAMS,
        cost_estimate=pl.CostEstimate(flops=0, bytes_accessed=10_000_000, transcendentals=0),
        name="planes",
    )(core, remote(members))
    return list(results[:count]), list(results[count:])


def hidden_slopes(core, partner, neighbour, front, state_taps):
    rows = state_taps.shape[0] // GROUP
    hidden, lats = front.shape[1], state_taps.shape[1]
    return pl.pallas_call(
        slopes_kernel,
        out_shape=pltpu.HBM((rows + 2, hidden, lats), F32),
        in_specs=[SCALAR] + [NEAR] * 4,
        out_specs=NEAR,
        scratch_shapes=[padded_scratch(4, lats), tap_scratch(4, lats), tap_scratch(8, lats)],
        compiler_params=PARAMS,
        cost_estimate=pl.CostEstimate(
            flops=1_000_000_000, bytes_accessed=6_000_000, transcendentals=1_200_000
        ),
        name="slopes",
    )(core, partner, neighbour, front, state_taps)


def member_sums(blocks, half, kept, taken, field, kind):
    lons = field.shape[0]
    span = 96
    count = len(kept) + len(taken)
    wide = 2 * 128
    offsets = np.arange(wide)
    lat_band = taps(np.abs(offsets[:, None] - offsets[None, :]))
    zero = np.zeros_like(lat_band)
    lat_loc = jnp.asarray(
        np.stack(
            [
                np.where(offsets[None, :] < 192, lat_band, zero),
                np.where(offsets[None, :] >= 64, lat_band, zero),
            ]
        )
    )
    lon_loc = jnp.asarray(
        taps(np.abs(np.arange(span)[:, None] + HALF - np.arange(span + 2 * HALF)[None, :]))
    )
    return pl.pallas_call(
        functools.partial(member_kernel, span),
        in_specs=[SCALAR]
        + [FAR] * len(kept)
        + [pl.BlockSpec(memory_space=pl.ANY)] * len(taken)
        + [NEAR] * 3,
        out_shape=jax.ShapeDtypeStruct((blocks, 48, 128), kind),
        scratch_shapes=[
            pltpu.VMEM((lons, wide), F32),
            pltpu.VMEM((lons + 2 * HALF, count * wide), BF),
            pltpu.VMEM((lons + 16, wide), F32),
            pltpu.VMEM((count, lons, wide), BF),
            pltpu.SemaphoreType.DMA((count,)),
        ],
        compiler_params=PARAMS,
        cost_estimate=pl.CostEstimate(
            flops=2_000_000_000, bytes_accessed=4_000_000, transcendentals=0
        ),
        name="members",
    )(half, *[remote(value) for value in kept], *taken, field, lat_loc, lon_loc)


def add_parts(own, other):
    return pl.pallas_call(
        add_kernel,
        out_shape=jax.ShapeDtypeStruct(own.shape, BF),
        compiler_params=PARAMS,
        name="add_parts",
    )(own, other)


def block_sums(groups, arrived):
    lines = arrived[0].shape[1]
    lats = sum(part.shape[2] for part in arrived)
    return pl.pallas_call(
        sum_kernel,
        out_shape=shape_of(groups, 2 * lines, lats),
        compiler_params=PARAMS,
        name="block_sum",
    )(*arrived)


def responses(scale, copies, slopes, front, back):
    rows = slopes.shape[0] - 2
    hidden, lats = slopes.shape[1:]
    return pl.pallas_call(
        functools.partial(response_kernel, scale),
        out_shape=[wide_of(rows, 2, lats)] * 2,
        in_specs=[NEAR, FAR, NEAR, NEAR],
        scratch_shapes=[
            padded_scratch(rows + 4, lats),
            tap_scratch(rows + 4, lats),
            pltpu.VMEM((3, (rows + 2) * 8, lats), F32),
            padded_scratch(rows + 2, lats),
            pltpu.VMEM((rows + 2, hidden, lats), F32),
            pltpu.VMEM((32, 128), F32),
            pltpu.SemaphoreType.DMA((2,)),
        ],
        compiler_params=PARAMS,
        name="response",
    )(copies, remote(slopes), front, back)


def per_device(members, state, cotangent, conv_in, conv_out, bias):
    blocks = lax.axis_size("space")
    groups = lax.axis_size("mem")
    held, lons, var_count, lats = members.shape
    core = lax.axis_index("space") % 2
    swap = [(i, i ^ 1) for i in range(blocks)]
    chain = [(i, (i + 1 if i % 2 else i - 1) % blocks) for i in range(blocks)]
    tail = jnp.concatenate([state[-2:], cotangent[-2:]], axis=1)
    head = jnp.concatenate([state[:2], cotangent[:2]], axis=1)
    neighbour = lax.ppermute(jnp.where(core == 0, head, tail), "space", chain)
    partner = lax.ppermute(jnp.where(core == 0, tail, head), "space", swap)
    core = core.reshape(1)
    first = jnp.transpose(conv_in, (0, 1, 3, 2))
    front, back, state_taps, cot_taps, partial, cot_planes = prepare(
        state, cotangent, first, conv_out, bias
    )
    outgoing = gradient_planes(
        blocks, core, cot_planes, partner, neighbour, front, back, state_taps, cot_taps, partial
    )
    members, outgoing = lax.optimization_barrier((members, outgoing))
    gathered = lax.all_to_all(outgoing, "space", 0, 0, tiled=True)
    kept, given = member_planes(core, members)
    taken = [lax.ppermute(give, "space", swap) for give in given]
    slopes = hidden_slopes(core, partner, neighbour, front, state_taps)
    gathered, slopes = lax.optimization_barrier((gathered, slopes))
    half = (lax.axis_index("mem") // 2) % 2
    half = half.reshape(1)
    field = gathered.reshape(lons, lats)
    theirs = member_sums(blocks, 1 - half, kept, taken, field, BF)
    theirs, field = lax.optimization_barrier((theirs, field))
    other = lax.ppermute(theirs, "mem", [(i, i ^ 2) for i in range(groups)])
    own = member_sums(blocks, half, kept, taken, field, F32)
    arrived = [lax.all_to_all(add_parts(own, other), "space", 0, 0, tiled=True)]
    spread = block_sums(groups, arrived)
    copies = lax.all_to_all(spread, "mem", 0, 0, tiled=True)
    member_count = held * blocks * groups
    increment, response = responses(1.0 / (member_count - 1.0), copies, slopes, front, back)
    return (increment, response)


def solution(mesh):
    in_specs = (
        P(("space", "mem"), None, None, None),
        P("space", None, None),
        P("space", None, None),
        P(),
        P(),
        P(),
    )
    out_specs = (P("space", None, None), P("space", None, None))
    return jax.shard_map(
        per_device, mesh=mesh, in_specs=in_specs, out_specs=out_specs, check_vma=False
    )
```

```python
import functools

import jax
import jax.numpy as jnp
import ml_dtypes
import numpy as np
from jax import lax
from jax.experimental import pallas as pl
from jax.experimental.pallas import tpu as pltpu
from jax.sharding import PartitionSpec as P

HALF = 16
GROUP = 32
BATCH = 11
BF = jnp.bfloat16
F32 = jnp.float32


def taps(distance):
    ratio = distance.astype(np.float32) / np.float32(HALF + 1.0)
    value = np.float32(1.0) - ratio * ratio
    return np.where(distance <= HALF, value, np.float32(0.0)).astype(ml_dtypes.bfloat16)


def shifted(value, step):
    if step == 1:
        return value
    lats = value.shape[-1]
    lane = lax.broadcasted_iota(jnp.int32, value.shape, value.ndim - 1)
    if step == 0:
        return jnp.where(lane == 0, 0.0, pltpu.roll(value, 1, value.ndim - 1))
    return jnp.where(lane == lats - 1, 0.0, pltpu.roll(value, lats - 1, value.ndim - 1))


def split_high_low(value):
    high = value.astype(BF)
    low = (value - high.astype(F32)).astype(BF)
    return high, low


def stack_taps(wide_ref, tap_ref):
    for tile in range(wide_ref.shape[0]):
        value = wide_ref[tile]
        rows = value.shape[0] // 8
        high = value.astype(BF).astype(F32)
        low = value - high
        high = high.reshape(rows, 1, 8, 128)
        low = low.reshape(rows, 1, 8, 128)
        both = jnp.concatenate([high, low, high, low], axis=1).reshape(rows * GROUP, 128)
        tap_ref[:, tile * 128 : (tile + 1) * 128] = both.astype(BF)


def put_taps(wide_ref, plane, first_row, var):
    rows = plane.shape[0]
    for step in range(3):
        moved = shifted(plane, step)
        for tile in range(wide_ref.shape[0]):
            start = first_row * 8 + 2 * step + var
            wide_ref[tile, pl.ds(start, rows, stride=8), :] = moved[:, tile * 128 : (tile + 1) * 128]


def put_ones(wide_ref, value):
    rows = wide_ref.shape[1] // 8
    for tile in range(wide_ref.shape[0]):
        wide_ref[tile, pl.ds(6, rows, stride=8), :] = jnp.full((rows, 128), value, F32)
        wide_ref[tile, pl.ds(7, rows, stride=8), :] = jnp.zeros((rows, 128), F32)


def fold_rows(hiddens, back_weight, product_ref, rows):
    lats = hiddens[0].shape[1]
    high, low = split_high_low(jnp.concatenate(hiddens, axis=1))
    product = jnp.dot(
        back_weight, jnp.concatenate([high, low], axis=0), preferred_element_type=F32
    )
    product = product[:24] + product[24:]
    for at, row in enumerate(rows):
        for step in range(3):
            product_ref[step, pl.ds(row * 8, 8), :] = product[
                8 * step : 8 * step + 8, at * lats : (at + 1) * lats
            ]


def backward_rows(front_ref, windows):
    activity = [jnp.dot(front_ref[0], state(), preferred_element_type=F32) for state, _ in windows]
    hidden = [jnp.dot(front_ref[1], cot(), preferred_element_type=F32) for _, cot in windows]
    for at in range(len(windows)):
        active = jnp.tanh(activity[at])
        hidden[at] = (1.0 - active * active) * hidden[at]
    return hidden


def window_of(ref, row):
    return lambda: ref[pl.ds(row * GROUP, 3 * GROUP), :]


def fold_lats(product_ref, fold_ref, first, count):
    window = pl.ds(first * 8, count * 8)
    total = (
        product_ref[1, window, :]
        + shifted(product_ref[0, window, :], 0)
        + shifted(product_ref[2, window, :], 2)
    )
    for tile in range(fold_ref.shape[0]):
        fold_ref[tile, window, :] = total[:, tile * 128 : (tile + 1) * 128]


def folded(fold_ref, rows, var):
    tiles = []
    for tile in range(fold_ref.shape[0]):
        tiles.append(
            sum(
                fold_ref[tile, pl.ds(10 * step + var, rows, stride=8), :] for step in range(3)
            )
        )
    return jnp.concatenate(tiles, axis=1)


def edges(core_ref, partner_ref, neighbour_ref):
    partner, neighbour = partner_ref[...], neighbour_ref[...]
    first = core_ref[0] == 0
    return jnp.where(first, neighbour, partner), jnp.where(first, partner, neighbour)


def fill_edges(before_ref, after_ref, var_from, wide_ref):
    for var in range(2):
        line = var_from + var
        for row in range(2):
            put_taps(wide_ref, before_ref[row, line : line + 1, :], row, var)
            put_taps(wide_ref, after_ref[row, line : line + 1, :], 2 + row, var)


def bands(tap_ref, edge_ref, frame_ref):
    half = 2 * GROUP
    last = tap_ref.shape[0] - half
    frame_ref[0:half, :] = edge_ref[0:half, :]
    frame_ref[half : 2 * half, :] = tap_ref[0:half, :]
    frame_ref[2 * half : 3 * half, :] = tap_ref[last : last + half, :]
    frame_ref[3 * half : 4 * half, :] = edge_ref[half : 2 * half, :]


def front_stack(rows_ref):
    value = rows_ref[...]
    high = value.astype(BF).astype(F32)
    low = value - high
    high = high.reshape(3, 1, 8, 128)
    low = low.reshape(3, 1, 8, 128)
    both = jnp.concatenate([high, high, low, low], axis=1).reshape(3 * GROUP, 128)
    return jnp.transpose(both).astype(BF)


def back_stack(rows_ref):
    value = rows_ref[...]
    high = value.astype(BF).astype(F32)
    both = jnp.concatenate([high, value - high], axis=0)
    return jnp.concatenate([both, both], axis=1).astype(BF)


def fetch(pairs, semaphores):
    copies = [
        pltpu.make_async_copy(source, target, semaphores.at[index])
        for index, (source, target) in enumerate(pairs)
    ]
    for copy in copies:
        copy.start()
    return copies


def prepare_kernel(
    state_far,
    cot_far,
    first_far,
    second_far,
    bias_far,
    front_ref,
    back_ref,
    state_taps,
    cot_taps,
    fold,
    cot_planes,
    wide,
    lines,
    product,
    state_ref,
    cot_ref,
    first_ref,
    second_ref,
    bias_ref,
    semaphores,
):
    rows = state_ref.shape[0]
    near = (first_ref, second_ref, bias_ref, state_ref, cot_ref)
    far = (first_far, second_far, bias_far, state_far, cot_far)
    copies = fetch(zip(far, near), semaphores)
    for copy in copies[:3]:
        copy.wait()
    for which in range(2):
        lines[...] = jnp.zeros_like(lines)
        for lon in range(3):
            for lat in range(3):
                start = 8 * lon + 2 * lat
                if which == 0:
                    lines[start : start + 2, :] = first_ref[lon, lat]
                else:
                    lines[start : start + 2, :] = second_ref[2 - lon, 2 - lat]
        if which == 0:
            lines[14:15, :] = bias_ref[...]
        front_ref[which] = front_stack(lines)
        lines[...] = jnp.zeros_like(lines)
        for lon in range(3):
            for lat in range(3):
                start = 8 * lat + 2 * lon
                if which == 0:
                    lines[start : start + 2, :] = first_ref[2 - lon, 2 - lat]
                else:
                    lines[start : start + 2, :] = second_ref[lon, lat]
        back_ref[which] = back_stack(lines)

    put_ones(wide, 1.0)
    for copy in copies[3:]:
        copy.wait()
    for main_ref, tap_ref in ((state_ref, state_taps), (cot_ref, cot_taps)):
        for var in range(2):
            plane = main_ref[:, var, :]
            if main_ref is cot_ref:
                cot_planes[var] = plane
            put_taps(wide, plane, 0, var)
        stack_taps(wide, tap_ref)

    for first in range(0, rows - 2, BATCH):
        batch = range(first, min(first + BATCH, rows - 2))
        hidden = backward_rows(
            front_ref, [(window_of(state_taps, row), window_of(cot_taps, row)) for row in batch]
        )
        fold_rows(hidden, back_ref[0], product, [row + 2 for row in batch])
    fold_lats(product, fold, 2, rows - 2)


def gradient_kernel(
    core_ref,
    cot_planes,
    partner_ref,
    neighbour_ref,
    front_ref,
    back_ref,
    state_taps,
    cot_taps,
    fold_ref,
    out_ref,
    wide,
    edge,
    state_frame,
    cot_frame,
    product,
    fold,
):
    rows = cot_planes.shape[1]
    before_ref, after_ref = edges(core_ref, partner_ref, neighbour_ref)
    put_ones(wide, 1.0)
    for var_from, tap_ref, frame_ref in ((0, state_taps, state_frame), (2, cot_taps, cot_frame)):
        fill_edges(before_ref, after_ref, var_from, wide)
        stack_taps(wide, edge)
        bands(tap_ref, edge, frame_ref)
    fold[...] = fold_ref[...]
    hidden = backward_rows(
        front_ref, [(window_of(state_frame, at), window_of(cot_frame, at)) for at in (0, 1, 4, 5)]
    )
    fold_rows(hidden, back_ref[0], product, (0, 1, rows, rows + 1))
    fold_lats(product, fold, 0, 2)
    fold_lats(product, fold, rows, 2)
    for var in range(2):
        plane = (cot_planes[var] + folded(fold, rows, var)).astype(BF)
        for pair in range(out_ref.shape[0] // 2):
            out_ref[2 * pair + var] = plane


def slopes_kernel(
    core_ref, partner_ref, neighbour_ref, front_ref, state_taps, out_ref, wide, edge, frame
):
    rows = out_ref.shape[0] - 2
    before_ref, after_ref = edges(core_ref, partner_ref, neighbour_ref)
    put_ones(wide, 1.0)
    fill_edges(before_ref, after_ref, 0, wide)
    stack_taps(wide, edge)
    bands(state_taps, edge, frame)

    windows = [window_of(frame, at) for at in (0, 1)]
    windows += [window_of(state_taps, row) for row in range(rows - 2)]
    windows += [window_of(frame, at) for at in (4, 5)]
    for first in range(0, rows + 2, BATCH):
        batch = range(first, min(first + BATCH, rows + 2))
        dots = [jnp.dot(front_ref[0], windows[row](), preferred_element_type=F32) for row in batch]
        for row, value in zip(batch, dots):
            active = jnp.tanh(value)
            out_ref[row] = 1.0 - active * active


def response_kernel(
    scale,
    copies_ref,
    slopes_far,
    front_ref,
    back_ref,
    incr_out,
    resp_out,
    wide,
    incr_taps,
    product,
    fold,
    slopes_ref,
    semaphores,
):
    rows = incr_out.shape[0]
    half = (rows + 2) // 2
    halves = [pl.ds(0, half), pl.ds(half, half)]
    copies = fetch([(slopes_far.at[part], slopes_ref.at[part]) for part in halves], semaphores)
    planes = []
    put_ones(wide, 0.0)
    groups = copies_ref.shape[0]
    lines = rows + 4
    for var in range(2):
        values = [
            copies_ref[group, pl.ds(2 * var * lines, 2 * lines), :].astype(F32)
            for group in range(groups)
        ]
        lower = sum(value for group, value in enumerate(values) if (group // 2) % 2 == 0)
        upper = sum(value for group, value in enumerate(values) if (group // 2) % 2 == 1)
        middle = (lower + upper)[lines:]
        plane = jnp.concatenate([lower[:lines], middle, upper[:lines]], axis=1)
        plane = plane * scale
        planes.append(plane)
        put_taps(wide, plane, 0, var)
    stack_taps(wide, incr_taps)

    for part in range(2):
        batch = range(part * half, (part + 1) * half)
        hidden = [
            jnp.dot(front_ref[0], window_of(incr_taps, row)(), preferred_element_type=F32)
            for row in batch
        ]
        copies[part].wait()
        hidden = [slopes_ref[row] * value for row, value in zip(batch, hidden)]
        fold_rows(hidden, back_ref[1], product, batch)
    fold_lats(product, fold, 0, rows + 2)
    for var in range(2):
        increment = planes[var][2 : 2 + rows]
        incr_out[:, var, :] = increment
        resp_out[:, var, :] = increment + folded(fold, rows, var)


def planes_kernel(core_ref, members_far, *refs):
    *outs, near, lines, planes, in_semaphores, out_semaphores = refs
    core = core_ref[0]
    count, tiles, lines_count = near.shape[:3]
    rows = lines_count // 2
    merged = members_far.reshape(count, lines_count, tiles * 128)
    pairs = [
        (merged.at[member, :, pl.ds(tile * 128, 128)], near.at[member, tile])
        for member in range(count)
        for tile in range(tiles)
    ]
    arrivals = fetch(pairs, in_semaphores)
    departures = []
    for member in range(count):
        for tile in range(tiles):
            arrivals[member * tiles + tile].wait()
            lines[...] = near[member, tile].astype(F32)
            window = pl.ds(tile * 128, 128)
            planes[member, :, window] = lines[pl.ds(core, rows, stride=2), :].astype(BF)
            planes[count + member, :, window] = lines[pl.ds(1 - core, rows, stride=2), :].astype(BF)
        for slot in (count + member, member):
            copy = pltpu.make_async_copy(planes.at[slot], outs[slot], out_semaphores.at[slot])
            copy.start()
            departures.append(copy)
    for copy in departures:
        copy.wait()


def member_kernel(span, half_ref, *refs):
    *far_refs, field_ref, lat_ref, lon_ref, out_ref, field, banded, total, held, semaphores = refs
    lons = field_ref.shape[0]
    blocks = out_ref.shape[0]
    rows = lons // blocks
    reach, wide = lat_ref.shape[1:]
    half = half_ref[0]
    offset = pl.multiple_of(half * 128, 128)
    if reach < field_ref.shape[1]:
        source = pl.ds(offset, reach)
    else:
        source = pl.ds(0, reach)
    target = pl.ds(offset, wide)
    member_refs = [held.at[index] for index in range(len(far_refs))]
    copies = fetch([(far.at[:, source], near) for far, near in zip(far_refs, member_refs)], semaphores)
    field[...] = field_ref[:, source].astype(F32)
    lat_loc = lat_ref[half]
    chunk = 2 * span
    for index, member_ref in enumerate(member_refs):
        copies[index].wait()
        at = index * wide
        for start in range(0, lons, chunk):
            window = pl.ds(start, chunk)
            product = (member_ref[window, :].astype(F32) * field[window, :]).astype(BF)
            banded[pl.ds(HALF + start, chunk), at : at + wide] = jnp.dot(
                product, lat_loc, preferred_element_type=F32
            ).astype(BF)
    banded[pl.ds(0, HALF), :] = banded[pl.ds(lons, HALF), :]
    banded[pl.ds(HALF + lons, HALF), :] = banded[pl.ds(HALF, HALF), :]
    for start in range(0, lons, span):
        value = None
        for index, member_ref in enumerate(member_refs):
            at = index * wide
            spread = jnp.dot(
                lon_ref[...],
                banded[pl.ds(start, span + 2 * HALF), at : at + wide],
                preferred_element_type=F32,
            )
            term = member_ref[pl.ds(start, span), target].astype(F32) * spread
            value = term if value is None else value + term
        if wide > 128:
            value = jnp.where(half == 0, value, pltpu.roll(value, 128, 1))
        total[pl.ds(8 + start, span), :] = value
    total[pl.ds(0, 8), :] = total[pl.ds(lons, 8), :]
    total[pl.ds(lons + 8, 8), :] = total[pl.ds(8, 8), :]
    row = lax.broadcasted_iota(jnp.int32, (32, 128), 0)
    for block in range(blocks):
        top = 6 + block * rows
        if wide > 128:
            out_ref[block, pl.ds(0, rows + 4), :] = total[pl.ds(top, rows + 4), 0:128]
            out_ref[block, pl.ds(rows + 4, rows + 4), :] = total[pl.ds(top, rows + 4), 128:256]
        else:
            value = jnp.where(row < rows + 4, total[pl.ds(top, 32), :], 0.0)
            out_ref[block] = value.astype(BF)


def add_kernel(own_ref, other_ref, out_ref):
    for block in range(own_ref.shape[0]):
        outer = own_ref[block, 0:32, :] + other_ref[block].astype(F32)
        out_ref[block] = jnp.concatenate([outer, own_ref[block, 32:, :]], axis=0).astype(BF)


def sum_kernel(*refs):
    *parts_refs, out_ref = refs
    start = 0
    for parts_ref in parts_refs:
        lines, lats = parts_ref.shape[1:]
        for var in range(2):
            plane = parts_ref[var].astype(F32)
            for pair in range(1, parts_ref.shape[0] // 2):
                plane = plane + parts_ref[2 * pair + var].astype(F32)
            plane = plane.astype(BF)
            for group in range(out_ref.shape[0]):
                out_ref[group, pl.ds(var * lines, lines), pl.ds(start, lats)] = plane
        start += lats


def shape_of(*dims):
    return jax.ShapeDtypeStruct(dims, BF)


def wide_of(*dims):
    return jax.ShapeDtypeStruct(dims, F32)


FAR = pl.BlockSpec(memory_space=pltpu.HBM)
SCALAR = pl.BlockSpec(memory_space=pltpu.SMEM)
NEAR = pl.BlockSpec(memory_space=pltpu.VMEM)
PARAMS = pltpu.CompilerParams(vmem_limit_bytes=24 << 20)


def remote(value):
    return pltpu.with_memory_space_constraint(value, pltpu.HBM)


def padded_scratch(count, lats):
    return pltpu.VMEM((lats // 128, count * 8, 128), F32)


def tap_scratch(count, lats):
    return pltpu.VMEM((count * GROUP, lats), BF)


def prepare(state, cotangent, first, second, bias):
    rows, var_count, lats = state.shape
    hidden = first.shape[-1]
    operands = (state, cotangent, first, second, bias.reshape(1, hidden))
    return pl.pallas_call(
        prepare_kernel,
        out_shape=[
            shape_of(2, hidden, 3 * GROUP),
            shape_of(2, 48, 2 * hidden),
            shape_of(rows * GROUP, lats),
            shape_of(rows * GROUP, lats),
            wide_of(lats // 128, (rows + 2) * 8, 128),
            wide_of(var_count, rows, lats),
        ],
        in_specs=[FAR] * 5,
        scratch_shapes=[
            padded_scratch(rows, lats),
            pltpu.VMEM((24, hidden), F32),
            pltpu.VMEM((3, (rows + 2) * 8, lats), F32),
            pltpu.VMEM(state.shape, F32),
            pltpu.VMEM(state.shape, F32),
            pltpu.VMEM(first.shape, F32),
            pltpu.VMEM(second.shape, F32),
            pltpu.VMEM((1, hidden), F32),
            pltpu.SemaphoreType.DMA((5,)),
        ],
        compiler_params=PARAMS,
        cost_estimate=pl.CostEstimate(
            flops=2_000_000_000, bytes_accessed=3_000_000, transcendentals=1_100_000
        ),
        name="prepare",
    )(*[remote(value) for value in operands])


def gradient_planes(
    blocks, core, cot_planes, partner, neighbour, front, back, state_taps, cot_taps, partial
):
    var_count, rows, lats = cot_planes.shape
    return pl.pallas_call(
        gradient_kernel,
        out_shape=shape_of(blocks, rows, lats),
        in_specs=[SCALAR] + [NEAR] * 8,
        scratch_shapes=[
            padded_scratch(4, lats),
            tap_scratch(4, lats),
            tap_scratch(8, lats),
            tap_scratch(8, lats),
            pltpu.VMEM((3, (rows + 2) * 8, lats), F32),
            padded_scratch(rows + 2, lats),
        ],
        compiler_params=PARAMS,
        cost_estimate=pl.CostEstimate(
            flops=400_000_000, bytes_accessed=1_500_000, transcendentals=200_000
        ),
        name="gradient",
    )(core, cot_planes, partner, neighbour, front, back, state_taps, cot_taps, partial)


def member_planes(core, members):
    count, lons, var_count, lats = members.shape
    results = pl.pallas_call(
        planes_kernel,
        in_specs=[SCALAR, FAR],
        out_specs=[FAR] * (2 * count),
        out_shape=[pltpu.HBM((lons, lats), BF)] * (2 * count),
        scratch_shapes=[
            pltpu.VMEM((count, lats // 128, lons * var_count, 128), BF),
            pltpu.VMEM((lons * 2, 128), F32),
            pltpu.VMEM((2 * count, lons, lats), BF),
            pltpu.SemaphoreType.DMA((count * (lats // 128),)),
            pltpu.SemaphoreType.DMA((2 * count,)),
        ],
        compiler_params=PARAMS,
        cost_estimate=pl.CostEstimate(flops=0, bytes_accessed=10_000_000, transcendentals=0),
        name="planes",
    )(core, remote(members))
    return list(results[:count]), list(results[count:])


def hidden_slopes(core, partner, neighbour, front, state_taps):
    rows = state_taps.shape[0] // GROUP
    hidden, lats = front.shape[1], state_taps.shape[1]
    return pl.pallas_call(
        slopes_kernel,
        out_shape=pltpu.HBM((rows + 2, hidden, lats), F32),
        in_specs=[SCALAR] + [NEAR] * 4,
        out_specs=NEAR,
        scratch_shapes=[padded_scratch(4, lats), tap_scratch(4, lats), tap_scratch(8, lats)],
        compiler_params=PARAMS,
        cost_estimate=pl.CostEstimate(
            flops=1_000_000_000, bytes_accessed=6_000_000, transcendentals=1_200_000
        ),
        name="slopes",
    )(core, partner, neighbour, front, state_taps)


def member_sums(blocks, half, kept, taken, field, wide):
    lons, lats = field.shape
    rows = lons // blocks
    span = 96
    count = len(kept) + len(taken)
    reach = 256 if wide == 128 else lats
    source, target = np.arange(reach), np.arange(wide)
    lat_loc = jnp.asarray(
        np.stack([taps(np.abs(source[:, None] - 128 * at - target[None, :])) for at in range(2)])
    )
    lon_loc = jnp.asarray(
        taps(np.abs(np.arange(span)[:, None] + HALF - np.arange(span + 2 * HALF)[None, :]))
    )
    out_shape = shape_of(blocks, 32, 128) if wide == 128 else wide_of(blocks, 2 * (rows + 4), 128)
    return pl.pallas_call(
        functools.partial(member_kernel, span),
        in_specs=[SCALAR]
        + [FAR] * len(kept)
        + [pl.BlockSpec(memory_space=pl.ANY)] * len(taken)
        + [NEAR] * 3,
        out_shape=out_shape,
        scratch_shapes=[
            pltpu.VMEM((lons, reach), F32),
            pltpu.VMEM((lons + 2 * HALF, count * wide), BF),
            pltpu.VMEM((lons + 16, wide), F32),
            pltpu.VMEM((count, lons, reach), BF),
            pltpu.SemaphoreType.DMA((count,)),
        ],
        compiler_params=PARAMS,
        cost_estimate=pl.CostEstimate(
            flops=wide * 16_000_000, bytes_accessed=4_000_000, transcendentals=0
        ),
        name="members",
    )(half, *[remote(value) for value in kept], *taken, field, lat_loc, lon_loc)


def add_parts(own, other):
    return pl.pallas_call(
        add_kernel,
        out_shape=shape_of(*own.shape),
        compiler_params=PARAMS,
        name="add_parts",
    )(own, other)


def block_sums(groups, arrived):
    lines = arrived[0].shape[1]
    lats = sum(part.shape[2] for part in arrived)
    return pl.pallas_call(
        sum_kernel,
        out_shape=shape_of(groups, 2 * lines, lats),
        compiler_params=PARAMS,
        name="block_sum",
    )(*arrived)


def responses(scale, copies, slopes, front, back):
    rows = slopes.shape[0] - 2
    hidden, lats = slopes.shape[1:]
    return pl.pallas_call(
        functools.partial(response_kernel, scale),
        out_shape=[wide_of(rows, 2, lats)] * 2,
        in_specs=[NEAR, FAR, NEAR, NEAR],
        scratch_shapes=[
            padded_scratch(rows + 4, lats),
            tap_scratch(rows + 4, lats),
            pltpu.VMEM((3, (rows + 2) * 8, lats), F32),
            padded_scratch(rows + 2, lats),
            pltpu.VMEM((rows + 2, hidden, lats), F32),
            pltpu.SemaphoreType.DMA((2,)),
        ],
        compiler_params=PARAMS,
        name="response",
    )(copies, remote(slopes), front, back)


def per_device(members, state, cotangent, conv_in, conv_out, bias):
    blocks = lax.axis_size("space")
    groups = lax.axis_size("mem")
    held, lons, var_count, lats = members.shape
    core = lax.axis_index("space") % 2
    swap = [(i, i ^ 1) for i in range(blocks)]
    chain = [(i, (i + 1 if i % 2 else i - 1) % blocks) for i in range(blocks)]
    tail = jnp.concatenate([state[-2:], cotangent[-2:]], axis=1)
    head = jnp.concatenate([state[:2], cotangent[:2]], axis=1)
    neighbour = lax.ppermute(jnp.where(core == 0, head, tail), "space", chain)
    partner = lax.ppermute(jnp.where(core == 0, tail, head), "space", swap)
    core = core.reshape(1)
    first = jnp.transpose(conv_in, (0, 1, 3, 2))
    front, back, state_taps, cot_taps, partial, cot_planes = prepare(
        state, cotangent, first, conv_out, bias
    )
    outgoing = gradient_planes(
        blocks, core, cot_planes, partner, neighbour, front, back, state_taps, cot_taps, partial
    )
    members, outgoing = lax.optimization_barrier((members, outgoing))
    gathered = lax.all_to_all(outgoing, "space", 0, 0, tiled=True)
    kept, given = member_planes(core, members)
    taken = [lax.ppermute(give, "space", swap) for give in given]
    slopes = hidden_slopes(core, partner, neighbour, front, state_taps)
    gathered, slopes = lax.optimization_barrier((gathered, slopes))
    half = (lax.axis_index("mem") // 2) % 2
    half = half.reshape(1)
    field = gathered.reshape(lons, lats)
    theirs = member_sums(blocks, 1 - half, kept, taken, field, 128)
    theirs, field = lax.optimization_barrier((theirs, field))
    other = lax.ppermute(theirs, "mem", [(i, i ^ 2) for i in range(groups)])
    own = member_sums(blocks, half, kept, taken, field, 256)
    arrived = [lax.all_to_all(add_parts(own, other), "space", 0, 0, tiled=True)]
    spread = block_sums(groups, arrived)
    copies = lax.all_to_all(spread, "mem", 0, 0, tiled=True)
    member_count = held * blocks * groups
    increment, response = responses(1.0 / (member_count - 1.0), copies, slopes, front, back)
    return (increment, response)


def solution(mesh):
    in_specs = (
        P(("space", "mem"), None, None, None),
        P("space", None, None),
        P("space", None, None),
        P(),
        P(),
        P(),
    )
    out_specs = (P("space", None, None), P("space", None, None))
    return jax.shard_map(
        per_device, mesh=mesh, in_specs=in_specs, out_specs=out_specs, check_vma=False
    )
```

```python
import functools

import jax
import jax.numpy as jnp
import ml_dtypes
import numpy as np
from jax import lax
from jax.experimental import pallas as pl
from jax.experimental.pallas import tpu as pltpu
from jax.sharding import PartitionSpec as P

HALF = 16
GROUP = 32
BATCH = 11
BF = jnp.bfloat16
F32 = jnp.float32


def taps(distance):
    ratio = distance.astype(np.float32) / np.float32(HALF + 1.0)
    value = np.float32(1.0) - ratio * ratio
    return np.where(distance <= HALF, value, np.float32(0.0)).astype(ml_dtypes.bfloat16)


def shifted(value, step):
    if step == 1:
        return value
    lats = value.shape[-1]
    lane = lax.broadcasted_iota(jnp.int32, value.shape, value.ndim - 1)
    if step == 0:
        return jnp.where(lane == 0, 0.0, pltpu.roll(value, 1, value.ndim - 1))
    return jnp.where(lane == lats - 1, 0.0, pltpu.roll(value, lats - 1, value.ndim - 1))


def split_high_low(value):
    high = value.astype(BF)
    low = (value - high.astype(F32)).astype(BF)
    return high, low


def stack_taps(wide_ref, tap_ref):
    for tile in range(wide_ref.shape[0]):
        value = wide_ref[tile]
        rows = value.shape[0] // 8
        high = value.astype(BF).astype(F32)
        low = value - high
        high = high.reshape(rows, 1, 8, 128)
        low = low.reshape(rows, 1, 8, 128)
        both = jnp.concatenate([high, low, high, low], axis=1).reshape(rows * GROUP, 128)
        tap_ref[:, tile * 128 : (tile + 1) * 128] = both.astype(BF)


def put_taps(wide_ref, plane, first_row, var):
    rows = plane.shape[0]
    for step in range(3):
        moved = shifted(plane, step)
        for tile in range(wide_ref.shape[0]):
            start = first_row * 8 + 2 * step + var
            wide_ref[tile, pl.ds(start, rows, stride=8), :] = moved[:, tile * 128 : (tile + 1) * 128]


def put_ones(wide_ref, value):
    rows = wide_ref.shape[1] // 8
    for tile in range(wide_ref.shape[0]):
        wide_ref[tile, pl.ds(6, rows, stride=8), :] = jnp.full((rows, 128), value, F32)
        wide_ref[tile, pl.ds(7, rows, stride=8), :] = jnp.zeros((rows, 128), F32)


def fold_rows(hiddens, back_weight, product_ref, rows):
    lats = hiddens[0].shape[1]
    high, low = split_high_low(jnp.concatenate(hiddens, axis=1))
    product = jnp.dot(
        back_weight, jnp.concatenate([high, low], axis=0), preferred_element_type=F32
    )
    product = product[:24] + product[24:]
    for at, row in enumerate(rows):
        for step in range(3):
            product_ref[step, pl.ds(row * 8, 8), :] = product[
                8 * step : 8 * step + 8, at * lats : (at + 1) * lats
            ]


def backward_rows(front_ref, windows):
    activity = [jnp.dot(front_ref[0], state(), preferred_element_type=F32) for state, _ in windows]
    hidden = [jnp.dot(front_ref[1], cot(), preferred_element_type=F32) for _, cot in windows]
    for at in range(len(windows)):
        active = jnp.tanh(activity[at])
        hidden[at] = (1.0 - active * active) * hidden[at]
    return hidden


def window_of(ref, row):
    return lambda: ref[pl.ds(row * GROUP, 3 * GROUP), :]


def fold_lats(product_ref, fold_ref, first, count):
    window = pl.ds(first * 8, count * 8)
    total = (
        product_ref[1, window, :]
        + shifted(product_ref[0, window, :], 0)
        + shifted(product_ref[2, window, :], 2)
    )
    for tile in range(fold_ref.shape[0]):
        fold_ref[tile, window, :] = total[:, tile * 128 : (tile + 1) * 128]


def folded(fold_ref, rows, var):
    tiles = []
    for tile in range(fold_ref.shape[0]):
        tiles.append(
            sum(
                fold_ref[tile, pl.ds(10 * step + var, rows, stride=8), :] for step in range(3)
            )
        )
    return jnp.concatenate(tiles, axis=1)


def edges(core_ref, partner_ref, neighbour_ref):
    partner, neighbour = partner_ref[...], neighbour_ref[...]
    first = core_ref[0] == 0
    return jnp.where(first, neighbour, partner), jnp.where(first, partner, neighbour)


def fill_edges(before_ref, after_ref, var_from, wide_ref):
    for var in range(2):
        line = var_from + var
        for row in range(2):
            put_taps(wide_ref, before_ref[row, line : line + 1, :], row, var)
            put_taps(wide_ref, after_ref[row, line : line + 1, :], 2 + row, var)


def bands(tap_ref, edge_ref, frame_ref):
    half = 2 * GROUP
    last = tap_ref.shape[0] - half
    frame_ref[0:half, :] = edge_ref[0:half, :]
    frame_ref[half : 2 * half, :] = tap_ref[0:half, :]
    frame_ref[2 * half : 3 * half, :] = tap_ref[last : last + half, :]
    frame_ref[3 * half : 4 * half, :] = edge_ref[half : 2 * half, :]


def front_stack(rows_ref):
    value = rows_ref[...]
    high = value.astype(BF).astype(F32)
    low = value - high
    high = high.reshape(3, 1, 8, 128)
    low = low.reshape(3, 1, 8, 128)
    both = jnp.concatenate([high, high, low, low], axis=1).reshape(3 * GROUP, 128)
    return jnp.transpose(both).astype(BF)


def back_stack(rows_ref):
    value = rows_ref[...]
    high = value.astype(BF).astype(F32)
    both = jnp.concatenate([high, value - high], axis=0)
    return jnp.concatenate([both, both], axis=1).astype(BF)


def fetch(pairs, semaphores):
    copies = [
        pltpu.make_async_copy(source, target, semaphores.at[index])
        for index, (source, target) in enumerate(pairs)
    ]
    for copy in copies:
        copy.start()
    return copies


def prepare_kernel(
    state_far,
    cot_far,
    first_far,
    second_far,
    bias_far,
    front_ref,
    back_ref,
    state_taps,
    cot_taps,
    fold,
    cot_planes,
    wide,
    lines,
    product,
    state_ref,
    cot_ref,
    first_ref,
    second_ref,
    bias_ref,
    semaphores,
):
    rows = state_ref.shape[0]
    near = (first_ref, second_ref, bias_ref, state_ref, cot_ref)
    far = (first_far, second_far, bias_far, state_far, cot_far)
    copies = fetch(zip(far, near), semaphores)
    for copy in copies[:3]:
        copy.wait()
    for which in range(2):
        lines[...] = jnp.zeros_like(lines)
        for lon in range(3):
            for lat in range(3):
                start = 8 * lon + 2 * lat
                if which == 0:
                    lines[start : start + 2, :] = first_ref[lon, lat]
                else:
                    lines[start : start + 2, :] = second_ref[2 - lon, 2 - lat]
        if which == 0:
            lines[14:15, :] = bias_ref[...]
        front_ref[which] = front_stack(lines)
        lines[...] = jnp.zeros_like(lines)
        for lon in range(3):
            for lat in range(3):
                start = 8 * lat + 2 * lon
                if which == 0:
                    lines[start : start + 2, :] = first_ref[2 - lon, 2 - lat]
                else:
                    lines[start : start + 2, :] = second_ref[lon, lat]
        back_ref[which] = back_stack(lines)

    put_ones(wide, 1.0)
    for copy in copies[3:]:
        copy.wait()
    for main_ref, tap_ref in ((state_ref, state_taps), (cot_ref, cot_taps)):
        for var in range(2):
            plane = main_ref[:, var, :]
            if main_ref is cot_ref:
                cot_planes[var] = plane
            put_taps(wide, plane, 0, var)
        stack_taps(wide, tap_ref)

    for first in range(0, rows - 2, BATCH):
        batch = range(first, min(first + BATCH, rows - 2))
        hidden = backward_rows(
            front_ref, [(window_of(state_taps, row), window_of(cot_taps, row)) for row in batch]
        )
        fold_rows(hidden, back_ref[0], product, [row + 2 for row in batch])
    fold_lats(product, fold, 2, rows - 2)


def gradient_kernel(
    core_ref,
    half_ref,
    cot_planes,
    partner_ref,
    neighbour_ref,
    front_ref,
    back_ref,
    state_taps,
    cot_taps,
    fold_ref,
    out_ref,
    wide,
    edge,
    state_frame,
    cot_frame,
    product,
    fold,
):
    rows = cot_planes.shape[1]
    before_ref, after_ref = edges(core_ref, partner_ref, neighbour_ref)
    put_ones(wide, 1.0)
    for var_from, tap_ref, frame_ref in ((0, state_taps, state_frame), (2, cot_taps, cot_frame)):
        fill_edges(before_ref, after_ref, var_from, wide)
        stack_taps(wide, edge)
        bands(tap_ref, edge, frame_ref)
    fold[...] = fold_ref[...]
    hidden = backward_rows(
        front_ref, [(window_of(state_frame, at), window_of(cot_frame, at)) for at in (0, 1, 4, 5)]
    )
    fold_rows(hidden, back_ref[0], product, (0, 1, rows, rows + 1))
    fold_lats(product, fold, 0, 2)
    fold_lats(product, fold, rows, 2)
    for var in range(2):
        plane = cot_planes[var] + folded(fold, rows, var)
        plane = jnp.where(half_ref[0] == 0, plane[:, 128:], plane[:, :256]).astype(BF)
        for pair in range(out_ref.shape[0] // 2):
            out_ref[2 * pair + var] = plane


def slopes_kernel(
    core_ref, partner_ref, neighbour_ref, front_ref, state_taps, out_ref, wide, edge, frame
):
    rows = out_ref.shape[0] - 2
    before_ref, after_ref = edges(core_ref, partner_ref, neighbour_ref)
    put_ones(wide, 1.0)
    fill_edges(before_ref, after_ref, 0, wide)
    stack_taps(wide, edge)
    bands(state_taps, edge, frame)

    windows = [window_of(frame, at) for at in (0, 1)]
    windows += [window_of(state_taps, row) for row in range(rows - 2)]
    windows += [window_of(frame, at) for at in (4, 5)]
    for first in range(0, rows + 2, BATCH):
        batch = range(first, min(first + BATCH, rows + 2))
        dots = [jnp.dot(front_ref[0], windows[row](), preferred_element_type=F32) for row in batch]
        for row, value in zip(batch, dots):
            active = jnp.tanh(value)
            out_ref[row] = 1.0 - active * active


def response_kernel(
    scale,
    copies_ref,
    slopes_ref,
    front_ref,
    back_ref,
    incr_out,
    resp_out,
    wide,
    incr_taps,
    product,
    fold,
):
    rows = incr_out.shape[0]
    half = (rows + 2) // 2
    planes = []
    put_ones(wide, 0.0)
    groups = copies_ref.shape[0]
    lines = rows + 4
    for var in range(2):
        values = [
            copies_ref[group, pl.ds(2 * var * lines, 2 * lines), :].astype(F32)
            for group in range(groups)
        ]
        lower = sum(value for group, value in enumerate(values) if (group // 2) % 2 == 0)
        upper = sum(value for group, value in enumerate(values) if (group // 2) % 2 == 1)
        middle = (lower + upper)[lines:]
        plane = jnp.concatenate([lower[:lines], middle, upper[:lines]], axis=1)
        plane = plane * scale
        planes.append(plane)
        put_taps(wide, plane, 0, var)
    stack_taps(wide, incr_taps)

    for part in range(2):
        batch = range(part * half, (part + 1) * half)
        hidden = [
            jnp.dot(front_ref[0], window_of(incr_taps, row)(), preferred_element_type=F32)
            for row in batch
        ]
        hidden = [slopes_ref[row] * value for row, value in zip(batch, hidden)]
        fold_rows(hidden, back_ref[1], product, batch)
    fold_lats(product, fold, 0, rows + 2)
    for var in range(2):
        increment = planes[var][2 : 2 + rows]
        incr_out[:, var, :] = increment
        resp_out[:, var, :] = increment + folded(fold, rows, var)


def planes_kernel(core_ref, members_far, *refs):
    *outs, near, lines, planes, in_semaphores, out_semaphores = refs
    core = core_ref[0]
    count, tiles, lines_count = near.shape[:3]
    rows = lines_count // 2
    merged = members_far.reshape(count, lines_count, tiles * 128)
    pairs = [
        (merged.at[member, :, pl.ds(tile * 128, 128)], near.at[member, tile])
        for member in range(count)
        for tile in range(tiles)
    ]
    arrivals = fetch(pairs, in_semaphores)
    departures = []
    for member in range(count):
        for tile in range(tiles):
            arrivals[member * tiles + tile].wait()
            lines[...] = near[member, tile].astype(F32)
            window = pl.ds(tile * 128, 128)
            planes[member, :, window] = lines[pl.ds(core, rows, stride=2), :].astype(BF)
            planes[count + member, :, window] = lines[pl.ds(1 - core, rows, stride=2), :].astype(BF)
        for slot in (count + member, member):
            copy = pltpu.make_async_copy(planes.at[slot], outs[slot], out_semaphores.at[slot])
            copy.start()
            departures.append(copy)
    for copy in departures:
        copy.wait()


def member_kernel(span, count, half_ref, *refs):
    far_refs = refs[:count]
    *field_refs, lat_ref, lon_ref, out_ref, field, banded, total, held, semaphores = refs[count:]
    lons = field.shape[0]
    blocks = out_ref.shape[0]
    rows = lons // blocks
    reach, wide = lat_ref.shape[1:]
    half = half_ref[0]
    offset = pl.multiple_of(half * 128, 128)
    if reach == 256:
        source = pl.ds(offset, reach)
    else:
        source = pl.ds(0, reach)
    target = pl.ds(offset, wide)
    member_refs = [held.at[index] for index in range(len(far_refs))]
    copies = fetch([(far.at[:, source], near) for far, near in zip(far_refs, member_refs)], semaphores)
    if reach == 256:
        field[...] = field_refs[0][...].astype(F32)
    else:
        field[:, pl.ds(pl.multiple_of(128 - half * 128, 128), 256)] = field_refs[0][...].astype(F32)
        field[:, pl.ds(pl.multiple_of(half * 256, 128), 128)] = field_refs[1][...].astype(F32)
    lat_loc = lat_ref[half]
    chunk = 2 * span
    for index, member_ref in enumerate(member_refs):
        copies[index].wait()
        at = index * wide
        for start in range(0, lons, chunk):
            window = pl.ds(start, chunk)
            product = (member_ref[window, :].astype(F32) * field[window, :]).astype(BF)
            banded[pl.ds(HALF + start, chunk), at : at + wide] = jnp.dot(
                product, lat_loc, preferred_element_type=F32
            ).astype(BF)
    banded[pl.ds(0, HALF), :] = banded[pl.ds(lons, HALF), :]
    banded[pl.ds(HALF + lons, HALF), :] = banded[pl.ds(HALF, HALF), :]
    for start in range(0, lons, span):
        value = None
        for index, member_ref in enumerate(member_refs):
            at = index * wide
            spread = jnp.dot(
                lon_ref[...],
                banded[pl.ds(start, span + 2 * HALF), at : at + wide],
                preferred_element_type=F32,
            )
            term = member_ref[pl.ds(start, span), target].astype(F32) * spread
            value = term if value is None else value + term
        if wide > 128:
            value = jnp.where(half == 0, value, pltpu.roll(value, 128, 1))
        total[pl.ds(8 + start, span), :] = value
    total[pl.ds(0, 8), :] = total[pl.ds(lons, 8), :]
    total[pl.ds(lons + 8, 8), :] = total[pl.ds(8, 8), :]
    row = lax.broadcasted_iota(jnp.int32, (32, 128), 0)
    for block in range(blocks):
        top = 6 + block * rows
        if wide > 128:
            out_ref[block, pl.ds(0, rows + 4), :] = total[pl.ds(top, rows + 4), 0:128]
            out_ref[block, pl.ds(rows + 4, rows + 4), :] = total[pl.ds(top, rows + 4), 128:256]
        else:
            value = jnp.where(row < rows + 4, total[pl.ds(top, 32), :], 0.0)
            out_ref[block] = value.astype(BF)


def add_kernel(own_ref, other_ref, out_ref):
    for block in range(own_ref.shape[0]):
        outer = own_ref[block, 0:32, :] + other_ref[block].astype(F32)
        out_ref[block] = jnp.concatenate([outer, own_ref[block, 32:, :]], axis=0).astype(BF)


def sum_kernel(*refs):
    *parts_refs, out_ref = refs
    start = 0
    for parts_ref in parts_refs:
        lines, lats = parts_ref.shape[1:]
        for var in range(2):
            plane = parts_ref[var].astype(F32)
            for pair in range(1, parts_ref.shape[0] // 2):
                plane = plane + parts_ref[2 * pair + var].astype(F32)
            plane = plane.astype(BF)
            for group in range(out_ref.shape[0]):
                out_ref[group, pl.ds(var * lines, lines), pl.ds(start, lats)] = plane
        start += lats


def shape_of(*dims):
    return jax.ShapeDtypeStruct(dims, BF)


def wide_of(*dims):
    return jax.ShapeDtypeStruct(dims, F32)


FAR = pl.BlockSpec(memory_space=pltpu.HBM)
SCALAR = pl.BlockSpec(memory_space=pltpu.SMEM)
NEAR = pl.BlockSpec(memory_space=pltpu.VMEM)
PARAMS = pltpu.CompilerParams(vmem_limit_bytes=24 << 20)


def remote(value):
    return pltpu.with_memory_space_constraint(value, pltpu.HBM)


def padded_scratch(count, lats):
    return pltpu.VMEM((lats // 128, count * 8, 128), F32)


def tap_scratch(count, lats):
    return pltpu.VMEM((count * GROUP, lats), BF)


def prepare(state, cotangent, first, second, bias):
    rows, var_count, lats = state.shape
    hidden = first.shape[-1]
    operands = (state, cotangent, first, second, bias.reshape(1, hidden))
    return pl.pallas_call(
        prepare_kernel,
        out_shape=[
            shape_of(2, hidden, 3 * GROUP),
            shape_of(2, 48, 2 * hidden),
            shape_of(rows * GROUP, lats),
            shape_of(rows * GROUP, lats),
            wide_of(lats // 128, (rows + 2) * 8, 128),
            wide_of(var_count, rows, lats),
        ],
        in_specs=[FAR] * 5,
        scratch_shapes=[
            padded_scratch(rows, lats),
            pltpu.VMEM((24, hidden), F32),
            pltpu.VMEM((3, (rows + 2) * 8, lats), F32),
            pltpu.VMEM(state.shape, F32),
            pltpu.VMEM(state.shape, F32),
            pltpu.VMEM(first.shape, F32),
            pltpu.VMEM(second.shape, F32),
            pltpu.VMEM((1, hidden), F32),
            pltpu.SemaphoreType.DMA((5,)),
        ],
        compiler_params=PARAMS,
        cost_estimate=pl.CostEstimate(
            flops=2_000_000_000, bytes_accessed=3_000_000, transcendentals=1_100_000
        ),
        name="prepare",
    )(*[remote(value) for value in operands])


def gradient_planes(
    blocks, core, half, cot_planes, partner, neighbour, front, back, state_taps, cot_taps, partial
):
    var_count, rows, lats = cot_planes.shape
    return pl.pallas_call(
        gradient_kernel,
        out_shape=shape_of(blocks, rows, 256),
        in_specs=[SCALAR] * 2 + [NEAR] * 8,
        scratch_shapes=[
            padded_scratch(4, lats),
            tap_scratch(4, lats),
            tap_scratch(8, lats),
            tap_scratch(8, lats),
            pltpu.VMEM((3, (rows + 2) * 8, lats), F32),
            padded_scratch(rows + 2, lats),
        ],
        compiler_params=PARAMS,
        cost_estimate=pl.CostEstimate(
            flops=400_000_000, bytes_accessed=1_500_000, transcendentals=200_000
        ),
        name="gradient",
    )(core, half, cot_planes, partner, neighbour, front, back, state_taps, cot_taps, partial)


def member_planes(core, members):
    count, lons, var_count, lats = members.shape
    results = pl.pallas_call(
        planes_kernel,
        in_specs=[SCALAR, FAR],
        out_specs=[FAR] * (2 * count),
        out_shape=[pltpu.HBM((lons, lats), BF)] * (2 * count),
        scratch_shapes=[
            pltpu.VMEM((count, lats // 128, lons * var_count, 128), BF),
            pltpu.VMEM((lons * 2, 128), F32),
            pltpu.VMEM((2 * count, lons, lats), BF),
            pltpu.SemaphoreType.DMA((count * (lats // 128),)),
            pltpu.SemaphoreType.DMA((2 * count,)),
        ],
        compiler_params=PARAMS,
        cost_estimate=pl.CostEstimate(flops=0, bytes_accessed=10_000_000, transcendentals=0),
        name="planes",
    )(core, remote(members))
    return list(results[:count]), list(results[count:])


def hidden_slopes(core, partner, neighbour, front, state_taps):
    rows = state_taps.shape[0] // GROUP
    hidden, lats = front.shape[1], state_taps.shape[1]
    return pl.pallas_call(
        slopes_kernel,
        out_shape=pltpu.HBM((rows + 2, hidden, lats), F32),
        in_specs=[SCALAR] + [NEAR] * 4,
        out_specs=NEAR,
        scratch_shapes=[padded_scratch(4, lats), tap_scratch(4, lats), tap_scratch(8, lats)],
        compiler_params=PARAMS,
        cost_estimate=pl.CostEstimate(
            flops=1_000_000_000, bytes_accessed=6_000_000, transcendentals=1_200_000
        ),
        name="slopes",
    )(core, partner, neighbour, front, state_taps)


def member_sums(blocks, half, kept, taken, fields, wide):
    lons, lats = kept[0].shape
    rows = lons // blocks
    span = 96
    count = len(kept) + len(taken)
    reach = 256 if wide == 128 else lats
    source, target = np.arange(reach), np.arange(wide)
    lat_loc = jnp.asarray(
        np.stack([taps(np.abs(source[:, None] - 128 * at - target[None, :])) for at in range(2)])
    )
    lon_loc = jnp.asarray(
        taps(np.abs(np.arange(span)[:, None] + HALF - np.arange(span + 2 * HALF)[None, :]))
    )
    out_shape = shape_of(blocks, 32, 128) if wide == 128 else wide_of(blocks, 2 * (rows + 4), 128)
    return pl.pallas_call(
        functools.partial(member_kernel, span, count),
        in_specs=[SCALAR]
        + [FAR] * len(kept)
        + [pl.BlockSpec(memory_space=pl.ANY)] * len(taken)
        + [NEAR] * (2 + len(fields)),
        out_shape=out_shape,
        scratch_shapes=[
            pltpu.VMEM((lons, reach), F32),
            pltpu.VMEM((lons + 2 * HALF, count * wide), BF),
            pltpu.VMEM((lons + 16, wide), F32),
            pltpu.VMEM((count, lons, reach), BF),
            pltpu.SemaphoreType.DMA((count,)),
        ],
        compiler_params=PARAMS,
        cost_estimate=pl.CostEstimate(
            flops=wide * 16_000_000, bytes_accessed=4_000_000, transcendentals=0
        ),
        name="members",
    )(half, *[remote(value) for value in kept], *taken, *fields, lat_loc, lon_loc)


def add_parts(own, other):
    return pl.pallas_call(
        add_kernel,
        out_shape=shape_of(*own.shape),
        compiler_params=PARAMS,
        name="add_parts",
    )(own, other)


def block_sums(groups, arrived):
    lines = arrived[0].shape[1]
    lats = sum(part.shape[2] for part in arrived)
    return pl.pallas_call(
        sum_kernel,
        out_shape=shape_of(groups, 2 * lines, lats),
        compiler_params=PARAMS,
        name="block_sum",
    )(*arrived)


def responses(scale, copies, slopes, front, back):
    rows = slopes.shape[0] - 2
    hidden, lats = slopes.shape[1:]
    return pl.pallas_call(
        functools.partial(response_kernel, scale),
        out_shape=[wide_of(rows, 2, lats)] * 2,
        in_specs=[NEAR] * 4,
        scratch_shapes=[
            padded_scratch(rows + 4, lats),
            tap_scratch(rows + 4, lats),
            pltpu.VMEM((3, (rows + 2) * 8, lats), F32),
            padded_scratch(rows + 2, lats),
        ],
        compiler_params=PARAMS,
        name="response",
    )(copies, slopes, front, back)


def per_device(members, state, cotangent, conv_in, conv_out, bias):
    blocks = lax.axis_size("space")
    groups = lax.axis_size("mem")
    held, lons, var_count, lats = members.shape
    core = lax.axis_index("space") % 2
    swap = [(i, i ^ 1) for i in range(blocks)]
    chain = [(i, (i + 1 if i % 2 else i - 1) % blocks) for i in range(blocks)]
    tail = jnp.concatenate([state[-2:], cotangent[-2:]], axis=1)
    head = jnp.concatenate([state[:2], cotangent[:2]], axis=1)
    neighbour = lax.ppermute(jnp.where(core == 0, head, tail), "space", chain)
    partner = lax.ppermute(jnp.where(core == 0, tail, head), "space", swap)
    core = core.reshape(1)
    parity = (lax.axis_index("mem") // 2) % 2
    half = parity.reshape(1)
    first = jnp.transpose(conv_in, (0, 1, 3, 2))
    front, back, state_taps, cot_taps, partial, cot_planes = prepare(
        state, cotangent, first, conv_out, bias
    )
    outgoing = gradient_planes(
        blocks, core, half, cot_planes, partner, neighbour, front, back, state_taps, cot_taps, partial
    )
    members, outgoing = lax.optimization_barrier((members, outgoing))
    gathered = lax.all_to_all(outgoing, "space", 0, 0, tiled=True)
    kept, given = member_planes(core, members)
    taken = [lax.ppermute(give, "space", swap) for give in given]
    slopes = hidden_slopes(core, partner, neighbour, front, state_taps)
    gathered, slopes = lax.optimization_barrier((gathered, slopes))
    across = [(i, i ^ 2) for i in range(groups)]
    inner = gathered.reshape(lons, 256)
    outer = lax.ppermute(jnp.where(parity == 0, inner[:, 128:], inner[:, :128]), "mem", across)
    theirs = member_sums(blocks, 1 - half, kept, taken, [inner], 128)
    theirs, inner = lax.optimization_barrier((theirs, inner))
    other = lax.ppermute(theirs, "mem", across)
    own = member_sums(blocks, half, kept, taken, [inner, outer], 256)
    arrived = [lax.all_to_all(add_parts(own, other), "space", 0, 0, tiled=True)]
    spread = block_sums(groups, arrived)
    copies = lax.all_to_all(spread, "mem", 0, 0, tiled=True)
    member_count = held * blocks * groups
    increment, response = responses(1.0 / (member_count - 1.0), copies, slopes, front, back)
    return (increment, response)


def solution(mesh):
    in_specs = (
        P(("space", "mem"), None, None, None),
        P("space", None, None),
        P("space", None, None),
        P(),
        P(),
        P(),
    )
    out_specs = (P("space", None, None), P("space", None, None))
    return jax.shard_map(
        per_device, mesh=mesh, in_specs=in_specs, out_specs=out_specs, check_vma=False
    )
```

```python
import functools

import jax
import jax.numpy as jnp
import ml_dtypes
import numpy as np
from jax import lax
from jax.experimental import pallas as pl
from jax.experimental.pallas import tpu as pltpu
from jax.sharding import PartitionSpec as P

HALF = 16
GROUP = 32
BATCH = 11
BF = jnp.bfloat16
F32 = jnp.float32


def taps(distance):
    ratio = distance.astype(np.float32) / np.float32(HALF + 1.0)
    value = np.float32(1.0) - ratio * ratio
    return np.where(distance <= HALF, value, np.float32(0.0)).astype(ml_dtypes.bfloat16)


def shifted(value, step):
    if step == 1:
        return value
    lats = value.shape[-1]
    lane = lax.broadcasted_iota(jnp.int32, value.shape, value.ndim - 1)
    if step == 0:
        return jnp.where(lane == 0, 0.0, pltpu.roll(value, 1, value.ndim - 1))
    return jnp.where(lane == lats - 1, 0.0, pltpu.roll(value, lats - 1, value.ndim - 1))


def split_high_low(value):
    high = value.astype(BF)
    low = (value - high.astype(F32)).astype(BF)
    return high, low


def stack_taps(wide_ref, tap_ref):
    for tile in range(wide_ref.shape[0]):
        value = wide_ref[tile]
        rows = value.shape[0] // 8
        high = value.astype(BF).astype(F32)
        low = value - high
        high = high.reshape(rows, 1, 8, 128)
        low = low.reshape(rows, 1, 8, 128)
        both = jnp.concatenate([high, low, high, low], axis=1).reshape(rows * GROUP, 128)
        tap_ref[:, tile * 128 : (tile + 1) * 128] = both.astype(BF)


def put_taps(wide_ref, plane, first_row, var):
    rows = plane.shape[0]
    for step in range(3):
        moved = shifted(plane, step)
        for tile in range(wide_ref.shape[0]):
            start = first_row * 8 + 2 * step + var
            wide_ref[tile, pl.ds(start, rows, stride=8), :] = moved[:, tile * 128 : (tile + 1) * 128]


def put_ones(wide_ref, value):
    rows = wide_ref.shape[1] // 8
    for tile in range(wide_ref.shape[0]):
        wide_ref[tile, pl.ds(6, rows, stride=8), :] = jnp.full((rows, 128), value, F32)
        wide_ref[tile, pl.ds(7, rows, stride=8), :] = jnp.zeros((rows, 128), F32)


def fold_rows(hiddens, back_weight, product_ref, rows):
    lats = hiddens[0].shape[1]
    high, low = split_high_low(jnp.concatenate(hiddens, axis=1))
    product = jnp.dot(
        back_weight, jnp.concatenate([high, low], axis=0), preferred_element_type=F32
    )
    product = product[:24] + product[24:]
    for at, row in enumerate(rows):
        for step in range(3):
            product_ref[step, pl.ds(row * 8, 8), :] = product[
                8 * step : 8 * step + 8, at * lats : (at + 1) * lats
            ]


def backward_rows(front_ref, windows):
    activity = [jnp.dot(front_ref[0], state(), preferred_element_type=F32) for state, _ in windows]
    hidden = [jnp.dot(front_ref[1], cot(), preferred_element_type=F32) for _, cot in windows]
    for at in range(len(windows)):
        active = jnp.tanh(activity[at])
        hidden[at] = (1.0 - active * active) * hidden[at]
    return hidden


def window_of(ref, row):
    return lambda: ref[pl.ds(row * GROUP, 3 * GROUP), :]


def fold_lats(product_ref, fold_ref, first, count):
    window = pl.ds(first * 8, count * 8)
    total = (
        product_ref[1, window, :]
        + shifted(product_ref[0, window, :], 0)
        + shifted(product_ref[2, window, :], 2)
    )
    for tile in range(fold_ref.shape[0]):
        fold_ref[tile, window, :] = total[:, tile * 128 : (tile + 1) * 128]


def folded(fold_ref, rows, var):
    tiles = []
    for tile in range(fold_ref.shape[0]):
        tiles.append(
            sum(
                fold_ref[tile, pl.ds(10 * step + var, rows, stride=8), :] for step in range(3)
            )
        )
    return jnp.concatenate(tiles, axis=1)


def edges(core_ref, partner_ref, neighbour_ref):
    partner, neighbour = partner_ref[...], neighbour_ref[...]
    first = core_ref[0] == 0
    return jnp.where(first, neighbour, partner), jnp.where(first, partner, neighbour)


def fill_edges(before_ref, after_ref, var_from, wide_ref):
    for var in range(2):
        line = var_from + var
        for row in range(2):
            put_taps(wide_ref, before_ref[row, line : line + 1, :], row, var)
            put_taps(wide_ref, after_ref[row, line : line + 1, :], 2 + row, var)


def bands(tap_ref, edge_ref, frame_ref):
    half = 2 * GROUP
    last = tap_ref.shape[0] - half
    frame_ref[0:half, :] = edge_ref[0:half, :]
    frame_ref[half : 2 * half, :] = tap_ref[0:half, :]
    frame_ref[2 * half : 3 * half, :] = tap_ref[last : last + half, :]
    frame_ref[3 * half : 4 * half, :] = edge_ref[half : 2 * half, :]


def front_stack(rows_ref):
    value = rows_ref[...]
    high = value.astype(BF).astype(F32)
    low = value - high
    high = high.reshape(3, 1, 8, 128)
    low = low.reshape(3, 1, 8, 128)
    both = jnp.concatenate([high, high, low, low], axis=1).reshape(3 * GROUP, 128)
    return jnp.transpose(both).astype(BF)


def back_stack(rows_ref):
    value = rows_ref[...]
    high = value.astype(BF).astype(F32)
    both = jnp.concatenate([high, value - high], axis=0)
    return jnp.concatenate([both, both], axis=1).astype(BF)


def fetch(pairs, semaphores):
    copies = [
        pltpu.make_async_copy(source, target, semaphores.at[index])
        for index, (source, target) in enumerate(pairs)
    ]
    for copy in copies:
        copy.start()
    return copies


def prepare_kernel(
    state_far,
    cot_far,
    first_far,
    second_far,
    bias_far,
    front_ref,
    back_ref,
    state_taps,
    cot_taps,
    fold,
    cot_planes,
    wide,
    lines,
    product,
    state_ref,
    cot_ref,
    first_ref,
    second_ref,
    bias_ref,
    semaphores,
):
    rows = state_ref.shape[0]
    near = (first_ref, second_ref, bias_ref, state_ref, cot_ref)
    far = (first_far, second_far, bias_far, state_far, cot_far)
    copies = fetch(zip(far, near), semaphores)
    for copy in copies[:3]:
        copy.wait()
    for which in range(2):
        lines[...] = jnp.zeros_like(lines)
        for lon in range(3):
            for lat in range(3):
                start = 8 * lon + 2 * lat
                if which == 0:
                    lines[start : start + 2, :] = first_ref[lon, lat]
                else:
                    lines[start : start + 2, :] = second_ref[2 - lon, 2 - lat]
        if which == 0:
            lines[14:15, :] = bias_ref[...]
        front_ref[which] = front_stack(lines)
        lines[...] = jnp.zeros_like(lines)
        for lon in range(3):
            for lat in range(3):
                start = 8 * lat + 2 * lon
                if which == 0:
                    lines[start : start + 2, :] = first_ref[2 - lon, 2 - lat]
                else:
                    lines[start : start + 2, :] = second_ref[lon, lat]
        back_ref[which] = back_stack(lines)

    put_ones(wide, 1.0)
    for copy in copies[3:]:
        copy.wait()
    for main_ref, tap_ref in ((state_ref, state_taps), (cot_ref, cot_taps)):
        for var in range(2):
            plane = main_ref[:, var, :]
            if main_ref is cot_ref:
                cot_planes[var] = plane
            put_taps(wide, plane, 0, var)
        stack_taps(wide, tap_ref)

    for first in range(0, rows - 2, BATCH):
        batch = range(first, min(first + BATCH, rows - 2))
        hidden = backward_rows(
            front_ref, [(window_of(state_taps, row), window_of(cot_taps, row)) for row in batch]
        )
        fold_rows(hidden, back_ref[0], product, [row + 2 for row in batch])
    fold_lats(product, fold, 2, rows - 2)


def gradient_kernel(
    core_ref,
    half_ref,
    cot_planes,
    partner_ref,
    neighbour_ref,
    front_ref,
    back_ref,
    state_taps,
    cot_taps,
    fold_ref,
    out_ref,
    wide,
    edge,
    state_frame,
    cot_frame,
    product,
    fold,
):
    rows = cot_planes.shape[1]
    before_ref, after_ref = edges(core_ref, partner_ref, neighbour_ref)
    put_ones(wide, 1.0)
    for var_from, tap_ref, frame_ref in ((0, state_taps, state_frame), (2, cot_taps, cot_frame)):
        fill_edges(before_ref, after_ref, var_from, wide)
        stack_taps(wide, edge)
        bands(tap_ref, edge, frame_ref)
    fold[...] = fold_ref[...]
    hidden = backward_rows(
        front_ref, [(window_of(state_frame, at), window_of(cot_frame, at)) for at in (0, 1, 4, 5)]
    )
    fold_rows(hidden, back_ref[0], product, (0, 1, rows, rows + 1))
    fold_lats(product, fold, 0, 2)
    fold_lats(product, fold, rows, 2)
    for var in range(2):
        plane = cot_planes[var] + folded(fold, rows, var)
        plane = jnp.where(half_ref[0] == 0, plane[:, 128:], plane[:, :256]).astype(BF)
        for pair in range(out_ref.shape[0] // 2):
            out_ref[2 * pair + var] = plane


def slopes_kernel(
    core_ref, partner_ref, neighbour_ref, front_ref, state_taps, out_ref, wide, edge, frame
):
    rows = out_ref.shape[0] - 2
    before_ref, after_ref = edges(core_ref, partner_ref, neighbour_ref)
    put_ones(wide, 1.0)
    fill_edges(before_ref, after_ref, 0, wide)
    stack_taps(wide, edge)
    bands(state_taps, edge, frame)

    windows = [window_of(frame, at) for at in (0, 1)]
    windows += [window_of(state_taps, row) for row in range(rows - 2)]
    windows += [window_of(frame, at) for at in (4, 5)]
    for first in range(0, rows + 2, BATCH):
        batch = range(first, min(first + BATCH, rows + 2))
        dots = [jnp.dot(front_ref[0], windows[row](), preferred_element_type=F32) for row in batch]
        for row, value in zip(batch, dots):
            active = jnp.tanh(value)
            out_ref[row] = 1.0 - active * active


def response_kernel(
    scale,
    copies_ref,
    slopes_ref,
    front_ref,
    back_ref,
    incr_out,
    resp_out,
    wide,
    incr_taps,
    product,
    fold,
):
    rows = incr_out.shape[0]
    half = (rows + 2) // 2
    planes = []
    put_ones(wide, 0.0)
    groups = copies_ref.shape[0]
    lines = rows + 4
    for var in range(2):
        values = [
            copies_ref[group, pl.ds(2 * var * lines, 2 * lines), :].astype(F32)
            for group in range(groups)
        ]
        lower = sum(value for group, value in enumerate(values) if (group // 2) % 2 == 0)
        upper = sum(value for group, value in enumerate(values) if (group // 2) % 2 == 1)
        middle = (lower + upper)[lines:]
        plane = jnp.concatenate([lower[:lines], middle, upper[:lines]], axis=1)
        plane = plane * scale
        planes.append(plane)
        put_taps(wide, plane, 0, var)
    stack_taps(wide, incr_taps)

    for part in range(2):
        batch = range(part * half, (part + 1) * half)
        hidden = [
            jnp.dot(front_ref[0], window_of(incr_taps, row)(), preferred_element_type=F32)
            for row in batch
        ]
        hidden = [slopes_ref[row] * value for row, value in zip(batch, hidden)]
        fold_rows(hidden, back_ref[1], product, batch)
    fold_lats(product, fold, 0, rows + 2)
    for var in range(2):
        increment = planes[var][2 : 2 + rows]
        incr_out[:, var, :] = increment
        resp_out[:, var, :] = increment + folded(fold, rows, var)


def planes_kernel(core_ref, members_far, *refs):
    *outs, near, lines, planes, in_semaphores, out_semaphores = refs
    core = core_ref[0]
    count, tiles, lines_count = near.shape[:3]
    rows = lines_count // 2
    merged = members_far.reshape(count, lines_count, tiles * 128)
    pairs = [
        (merged.at[member, :, pl.ds(tile * 128, 128)], near.at[member, tile])
        for member in range(count)
        for tile in range(tiles)
    ]
    arrivals = fetch(pairs, in_semaphores)
    departures = []
    for member in range(count):
        for tile in range(tiles):
            arrivals[member * tiles + tile].wait()
            lines[...] = near[member, tile].astype(F32)
            window = pl.ds(tile * 128, 128)
            planes[member, :, window] = lines[pl.ds(core, rows, stride=2), :].astype(BF)
            planes[count + member, :, window] = lines[pl.ds(1 - core, rows, stride=2), :].astype(BF)
        for slot in (count + member, member):
            copy = pltpu.make_async_copy(planes.at[slot], outs[slot], out_semaphores.at[slot])
            copy.start()
            departures.append(copy)
    for copy in departures:
        copy.wait()


def member_kernel(span, count, half_ref, *refs):
    far_refs = refs[:count]
    *field_refs, lat_far, lon_far, out_ref, field, banded, total, held, lat_ref, lon_ref, semaphores = refs[count:]
    lons = field.shape[0]
    blocks = out_ref.shape[0]
    rows = lons // blocks
    reach, wide = lat_ref.shape
    half = half_ref[0]
    offset = pl.multiple_of(half * 128, 128)
    if reach == 256:
        source = pl.ds(offset, reach)
    else:
        source = pl.ds(0, reach)
    target = pl.ds(offset, wide)
    member_refs = [held.at[index] for index in range(len(far_refs))]
    pairs = [(lat_far.at[half], lat_ref), (lon_far, lon_ref)]
    pairs += [(far.at[:, source], near) for far, near in zip(far_refs, member_refs)]
    copies = fetch(pairs, semaphores)
    bands_here, copies = copies[:2], copies[2:]
    if reach == 256:
        field[...] = field_refs[0][...].astype(F32)
    else:
        field[:, pl.ds(pl.multiple_of(128 - half * 128, 128), 256)] = field_refs[0][...].astype(F32)
        field[:, pl.ds(pl.multiple_of(half * 256, 128), 128)] = field_refs[1][...].astype(F32)
    for copy in bands_here:
        copy.wait()
    lat_loc = lat_ref[...]
    chunk = 2 * span
    for index, member_ref in enumerate(member_refs):
        copies[index].wait()
        at = index * wide
        for start in range(0, lons, chunk):
            window = pl.ds(start, chunk)
            product = (member_ref[window, :].astype(F32) * field[window, :]).astype(BF)
            banded[pl.ds(HALF + start, chunk), at : at + wide] = jnp.dot(
                product, lat_loc, preferred_element_type=F32
            ).astype(BF)
    banded[pl.ds(0, HALF), :] = banded[pl.ds(lons, HALF), :]
    banded[pl.ds(HALF + lons, HALF), :] = banded[pl.ds(HALF, HALF), :]
    for start in range(0, lons, span):
        value = None
        for index, member_ref in enumerate(member_refs):
            at = index * wide
            spread = jnp.dot(
                lon_ref[...],
                banded[pl.ds(start, span + 2 * HALF), at : at + wide],
                preferred_element_type=F32,
            )
            term = member_ref[pl.ds(start, span), target].astype(F32) * spread
            value = term if value is None else value + term
        if wide > 128:
            value = jnp.where(half == 0, value, pltpu.roll(value, 128, 1))
        total[pl.ds(8 + start, span), :] = value
    total[pl.ds(0, 8), :] = total[pl.ds(lons, 8), :]
    total[pl.ds(lons + 8, 8), :] = total[pl.ds(8, 8), :]
    row = lax.broadcasted_iota(jnp.int32, (32, 128), 0)
    for block in range(blocks):
        top = 6 + block * rows
        if wide > 128:
            out_ref[block, pl.ds(0, rows + 4), :] = total[pl.ds(top, rows + 4), 0:128]
            out_ref[block, pl.ds(rows + 4, rows + 4), :] = total[pl.ds(top, rows + 4), 128:256]
        else:
            value = jnp.where(row < rows + 4, total[pl.ds(top, 32), :], 0.0)
            out_ref[block] = value.astype(BF)


def add_kernel(own_ref, other_ref, out_ref):
    for block in range(own_ref.shape[0]):
        outer = own_ref[block, 0:32, :] + other_ref[block].astype(F32)
        out_ref[block] = jnp.concatenate([outer, own_ref[block, 32:, :]], axis=0).astype(BF)


def sum_kernel(*refs):
    *parts_refs, out_ref = refs
    start = 0
    for parts_ref in parts_refs:
        lines, lats = parts_ref.shape[1:]
        for var in range(2):
            plane = parts_ref[var].astype(F32)
            for pair in range(1, parts_ref.shape[0] // 2):
                plane = plane + parts_ref[2 * pair + var].astype(F32)
            plane = plane.astype(BF)
            for group in range(out_ref.shape[0]):
                out_ref[group, pl.ds(var * lines, lines), pl.ds(start, lats)] = plane
        start += lats


def shape_of(*dims):
    return jax.ShapeDtypeStruct(dims, BF)


def wide_of(*dims):
    return jax.ShapeDtypeStruct(dims, F32)


FAR = pl.BlockSpec(memory_space=pltpu.HBM)
SCALAR = pl.BlockSpec(memory_space=pltpu.SMEM)
NEAR = pl.BlockSpec(memory_space=pltpu.VMEM)
PARAMS = pltpu.CompilerParams(vmem_limit_bytes=24 << 20)


def remote(value):
    return pltpu.with_memory_space_constraint(value, pltpu.HBM)


def padded_scratch(count, lats):
    return pltpu.VMEM((lats // 128, count * 8, 128), F32)


def tap_scratch(count, lats):
    return pltpu.VMEM((count * GROUP, lats), BF)


def prepare(state, cotangent, first, second, bias):
    rows, var_count, lats = state.shape
    hidden = first.shape[-1]
    operands = (state, cotangent, first, second, bias.reshape(1, hidden))
    return pl.pallas_call(
        prepare_kernel,
        out_shape=[
            shape_of(2, hidden, 3 * GROUP),
            shape_of(2, 48, 2 * hidden),
            shape_of(rows * GROUP, lats),
            shape_of(rows * GROUP, lats),
            wide_of(lats // 128, (rows + 2) * 8, 128),
            wide_of(var_count, rows, lats),
        ],
        in_specs=[FAR] * 5,
        scratch_shapes=[
            padded_scratch(rows, lats),
            pltpu.VMEM((24, hidden), F32),
            pltpu.VMEM((3, (rows + 2) * 8, lats), F32),
            pltpu.VMEM(state.shape, F32),
            pltpu.VMEM(state.shape, F32),
            pltpu.VMEM(first.shape, F32),
            pltpu.VMEM(second.shape, F32),
            pltpu.VMEM((1, hidden), F32),
            pltpu.SemaphoreType.DMA((5,)),
        ],
        compiler_params=PARAMS,
        cost_estimate=pl.CostEstimate(
            flops=2_000_000_000, bytes_accessed=3_000_000, transcendentals=1_100_000
        ),
        name="prepare",
    )(*[remote(value) for value in operands])


def gradient_planes(
    blocks, core, half, cot_planes, partner, neighbour, front, back, state_taps, cot_taps, partial
):
    var_count, rows, lats = cot_planes.shape
    return pl.pallas_call(
        gradient_kernel,
        out_shape=shape_of(blocks, rows, 256),
        in_specs=[SCALAR] * 2 + [NEAR] * 8,
        scratch_shapes=[
            padded_scratch(4, lats),
            tap_scratch(4, lats),
            tap_scratch(8, lats),
            tap_scratch(8, lats),
            pltpu.VMEM((3, (rows + 2) * 8, lats), F32),
            padded_scratch(rows + 2, lats),
        ],
        compiler_params=PARAMS,
        cost_estimate=pl.CostEstimate(
            flops=400_000_000, bytes_accessed=1_500_000, transcendentals=200_000
        ),
        name="gradient",
    )(core, half, cot_planes, partner, neighbour, front, back, state_taps, cot_taps, partial)


def member_planes(core, members):
    count, lons, var_count, lats = members.shape
    results = pl.pallas_call(
        planes_kernel,
        in_specs=[SCALAR, FAR],
        out_specs=[FAR] * (2 * count),
        out_shape=[pltpu.HBM((lons, lats), BF)] * (2 * count),
        scratch_shapes=[
            pltpu.VMEM((count, lats // 128, lons * var_count, 128), BF),
            pltpu.VMEM((lons * 2, 128), F32),
            pltpu.VMEM((2 * count, lons, lats), BF),
            pltpu.SemaphoreType.DMA((count * (lats // 128),)),
            pltpu.SemaphoreType.DMA((2 * count,)),
        ],
        compiler_params=PARAMS,
        cost_estimate=pl.CostEstimate(flops=0, bytes_accessed=10_000_000, transcendentals=0),
        name="planes",
    )(core, remote(members))
    return list(results[:count]), list(results[count:])


def hidden_slopes(core, partner, neighbour, front, state_taps):
    rows = state_taps.shape[0] // GROUP
    hidden, lats = front.shape[1], state_taps.shape[1]
    return pl.pallas_call(
        slopes_kernel,
        out_shape=pltpu.HBM((rows + 2, hidden, lats), F32),
        in_specs=[SCALAR] + [NEAR] * 4,
        out_specs=NEAR,
        scratch_shapes=[padded_scratch(4, lats), tap_scratch(4, lats), tap_scratch(8, lats)],
        compiler_params=PARAMS,
        cost_estimate=pl.CostEstimate(
            flops=1_000_000_000, bytes_accessed=6_000_000, transcendentals=1_200_000
        ),
        name="slopes",
    )(core, partner, neighbour, front, state_taps)


def member_sums(blocks, half, kept, taken, fields, wide):
    lons, lats = kept[0].shape
    rows = lons // blocks
    span = 96
    count = len(kept) + len(taken)
    reach = 256 if wide == 128 else lats
    source, target = np.arange(reach), np.arange(wide)
    lat_loc = jnp.asarray(
        np.stack([taps(np.abs(source[:, None] - 128 * at - target[None, :])) for at in range(2)])
    )
    lon_loc = jnp.asarray(
        taps(np.abs(np.arange(span)[:, None] + HALF - np.arange(span + 2 * HALF)[None, :]))
    )
    out_shape = shape_of(blocks, 32, 128) if wide == 128 else wide_of(blocks, 2 * (rows + 4), 128)
    return pl.pallas_call(
        functools.partial(member_kernel, span, count),
        in_specs=[SCALAR]
        + [FAR] * len(kept)
        + [pl.BlockSpec(memory_space=pl.ANY)] * len(taken)
        + [NEAR] * len(fields)
        + [FAR] * 2,
        out_shape=out_shape,
        scratch_shapes=[
            pltpu.VMEM((lons, reach), F32),
            pltpu.VMEM((lons + 2 * HALF, count * wide), BF),
            pltpu.VMEM((lons + 16, wide), F32),
            pltpu.VMEM((count, lons, reach), BF),
            pltpu.VMEM((reach, wide), BF),
            pltpu.VMEM((span, span + 2 * HALF), BF),
            pltpu.SemaphoreType.DMA((count + 2,)),
        ],
        compiler_params=PARAMS,
        cost_estimate=pl.CostEstimate(
            flops=wide * 16_000_000, bytes_accessed=4_000_000, transcendentals=0
        ),
        name="members",
    )(half, *[remote(value) for value in kept], *taken, *fields, remote(lat_loc), remote(lon_loc))


def add_parts(own, other):
    return pl.pallas_call(
        add_kernel,
        out_shape=shape_of(*own.shape),
        compiler_params=PARAMS,
        name="add_parts",
    )(own, other)


def block_sums(groups, arrived):
    lines = arrived[0].shape[1]
    lats = sum(part.shape[2] for part in arrived)
    return pl.pallas_call(
        sum_kernel,
        out_shape=shape_of(groups, 2 * lines, lats),
        compiler_params=PARAMS,
        name="block_sum",
    )(*arrived)


def responses(scale, copies, slopes, front, back):
    rows = slopes.shape[0] - 2
    hidden, lats = slopes.shape[1:]
    return pl.pallas_call(
        functools.partial(response_kernel, scale),
        out_shape=[wide_of(rows, 2, lats)] * 2,
        in_specs=[NEAR] * 4,
        scratch_shapes=[
            padded_scratch(rows + 4, lats),
            tap_scratch(rows + 4, lats),
            pltpu.VMEM((3, (rows + 2) * 8, lats), F32),
            padded_scratch(rows + 2, lats),
        ],
        compiler_params=PARAMS,
        name="response",
    )(copies, slopes, front, back)


def per_device(members, state, cotangent, conv_in, conv_out, bias):
    blocks = lax.axis_size("space")
    groups = lax.axis_size("mem")
    held, lons, var_count, lats = members.shape
    core = lax.axis_index("space") % 2
    swap = [(i, i ^ 1) for i in range(blocks)]
    chain = [(i, (i + 1 if i % 2 else i - 1) % blocks) for i in range(blocks)]
    tail = jnp.concatenate([state[-2:], cotangent[-2:]], axis=1)
    head = jnp.concatenate([state[:2], cotangent[:2]], axis=1)
    neighbour = lax.ppermute(jnp.where(core == 0, head, tail), "space", chain)
    partner = lax.ppermute(jnp.where(core == 0, tail, head), "space", swap)
    core = core.reshape(1)
    parity = (lax.axis_index("mem") // 2) % 2
    half = parity.reshape(1)
    first = jnp.transpose(conv_in, (0, 1, 3, 2))
    front, back, state_taps, cot_taps, partial, cot_planes = prepare(
        state, cotangent, first, conv_out, bias
    )
    outgoing = gradient_planes(
        blocks, core, half, cot_planes, partner, neighbour, front, back, state_taps, cot_taps, partial
    )
    members, outgoing = lax.optimization_barrier((members, outgoing))
    gathered = lax.all_to_all(outgoing, "space", 0, 0, tiled=True)
    kept, given = member_planes(core, members)
    taken = [lax.ppermute(give, "space", swap) for give in given]
    slopes = hidden_slopes(core, partner, neighbour, front, state_taps)
    gathered, slopes = lax.optimization_barrier((gathered, slopes))
    across = [(i, i ^ 2) for i in range(groups)]
    inner = gathered.reshape(lons, 256)
    outer = lax.ppermute(jnp.where(parity == 0, inner[:, 128:], inner[:, :128]), "mem", across)
    theirs = member_sums(blocks, 1 - half, kept, taken, [inner], 128)
    theirs, inner = lax.optimization_barrier((theirs, inner))
    other = lax.ppermute(theirs, "mem", across)
    own = member_sums(blocks, half, kept, taken, [inner, outer], 256)
    arrived = [lax.all_to_all(add_parts(own, other), "space", 0, 0, tiled=True)]
    spread = block_sums(groups, arrived)
    copies = lax.all_to_all(spread, "mem", 0, 0, tiled=True)
    member_count = held * blocks * groups
    increment, response = responses(1.0 / (member_count - 1.0), copies, slopes, front, back)
    return (increment, response)


def solution(mesh):
    in_specs = (
        P(("space", "mem"), None, None, None),
        P("space", None, None),
        P("space", None, None),
        P(),
        P(),
        P(),
    )
    out_specs = (P("space", None, None), P("space", None, None))
    return jax.shard_map(
        per_device, mesh=mesh, in_specs=in_specs, out_specs=out_specs, check_vma=False
    )
```

```python
import functools

import jax
import jax.numpy as jnp
import ml_dtypes
import numpy as np
from jax import lax
from jax.experimental import pallas as pl
from jax.experimental.pallas import tpu as pltpu
from jax.sharding import PartitionSpec as P

HALF = 16
GROUP = 32
BATCH = 6
BF = jnp.bfloat16
F32 = jnp.float32


def taps(distance):
    ratio = distance.astype(np.float32) / np.float32(HALF + 1.0)
    value = np.float32(1.0) - ratio * ratio
    return np.where(distance <= HALF, value, np.float32(0.0)).astype(ml_dtypes.bfloat16)


def shifted(value, step):
    if step == 1:
        return value
    lats = value.shape[-1]
    lane = lax.broadcasted_iota(jnp.int32, value.shape, value.ndim - 1)
    if step == 0:
        return jnp.where(lane == 0, 0.0, pltpu.roll(value, 1, value.ndim - 1))
    return jnp.where(lane == lats - 1, 0.0, pltpu.roll(value, lats - 1, value.ndim - 1))


def split_high_low(value):
    high = value.astype(BF)
    low = (value - high.astype(F32)).astype(BF)
    return high, low


def stack_taps(wide_ref, tap_ref):
    for tile in range(wide_ref.shape[0]):
        value = wide_ref[tile]
        rows = value.shape[0] // 8
        high = value.astype(BF).astype(F32)
        low = value - high
        high = high.reshape(rows, 1, 8, 128)
        low = low.reshape(rows, 1, 8, 128)
        both = jnp.concatenate([high, low, high, low], axis=1).reshape(rows * GROUP, 128)
        tap_ref[:, tile * 128 : (tile + 1) * 128] = both.astype(BF)


def put_taps(wide_ref, plane, first_row, var):
    rows = plane.shape[0]
    for step in range(3):
        moved = shifted(plane, step)
        for tile in range(wide_ref.shape[0]):
            start = first_row * 8 + 2 * step + var
            wide_ref[tile, pl.ds(start, rows, stride=8), :] = moved[:, tile * 128 : (tile + 1) * 128]


def put_ones(wide_ref, value):
    rows = wide_ref.shape[1] // 8
    for tile in range(wide_ref.shape[0]):
        wide_ref[tile, pl.ds(6, rows, stride=8), :] = jnp.full((rows, 128), value, F32)
        wide_ref[tile, pl.ds(7, rows, stride=8), :] = jnp.zeros((rows, 128), F32)


def fold_rows(hiddens, back_weight, product_ref, rows):
    lats = hiddens[0].shape[1]
    high, low = split_high_low(jnp.concatenate(hiddens, axis=1))
    product = jnp.dot(
        back_weight, jnp.concatenate([high, low], axis=0), preferred_element_type=F32
    )
    product = product[:24] + product[24:]
    for at, row in enumerate(rows):
        for step in range(3):
            product_ref[step, pl.ds(row * 8, 8), :] = product[
                8 * step : 8 * step + 8, at * lats : (at + 1) * lats
            ]


def backward_rows(front_ref, windows):
    activity = [jnp.dot(front_ref[0], state(), preferred_element_type=F32) for state, _ in windows]
    hidden = [jnp.dot(front_ref[1], cot(), preferred_element_type=F32) for _, cot in windows]
    for at in range(len(windows)):
        active = jnp.tanh(activity[at])
        hidden[at] = (1.0 - active * active) * hidden[at]
    return hidden


def window_of(ref, row):
    return lambda: ref[pl.ds(row * GROUP, 3 * GROUP), :]


def fold_lats(product_ref, fold_ref, first, count):
    window = pl.ds(first * 8, count * 8)
    total = (
        product_ref[1, window, :]
        + shifted(product_ref[0, window, :], 0)
        + shifted(product_ref[2, window, :], 2)
    )
    for tile in range(fold_ref.shape[0]):
        fold_ref[tile, window, :] = total[:, tile * 128 : (tile + 1) * 128]


def folded(fold_ref, rows, var):
    tiles = []
    for tile in range(fold_ref.shape[0]):
        tiles.append(
            sum(
                fold_ref[tile, pl.ds(10 * step + var, rows, stride=8), :] for step in range(3)
            )
        )
    return jnp.concatenate(tiles, axis=1)


def edges(core_ref, partner_ref, neighbour_ref):
    partner, neighbour = partner_ref[...], neighbour_ref[...]
    first = core_ref[0] == 0
    return jnp.where(first, neighbour, partner), jnp.where(first, partner, neighbour)


def fill_edges(before_ref, after_ref, var_from, wide_ref):
    for var in range(2):
        line = var_from + var
        for row in range(2):
            put_taps(wide_ref, before_ref[row, line : line + 1, :], row, var)
            put_taps(wide_ref, after_ref[row, line : line + 1, :], 2 + row, var)


def bands(tap_ref, edge_ref, frame_ref):
    half = 2 * GROUP
    last = tap_ref.shape[0] - half
    frame_ref[0:half, :] = edge_ref[0:half, :]
    frame_ref[half : 2 * half, :] = tap_ref[0:half, :]
    frame_ref[2 * half : 3 * half, :] = tap_ref[last : last + half, :]
    frame_ref[3 * half : 4 * half, :] = edge_ref[half : 2 * half, :]


def front_stack(rows_ref):
    value = rows_ref[...]
    high = value.astype(BF).astype(F32)
    low = value - high
    high = high.reshape(3, 1, 8, 128)
    low = low.reshape(3, 1, 8, 128)
    both = jnp.concatenate([high, high, low, low], axis=1).reshape(3 * GROUP, 128)
    return jnp.transpose(both).astype(BF)


def back_stack(rows_ref):
    value = rows_ref[...]
    high = value.astype(BF).astype(F32)
    both = jnp.concatenate([high, value - high], axis=0)
    return jnp.concatenate([both, both], axis=1).astype(BF)


def fetch(pairs, semaphores):
    copies = [
        pltpu.make_async_copy(source, target, semaphores.at[index])
        for index, (source, target) in enumerate(pairs)
    ]
    for copy in copies:
        copy.start()
    return copies


def prepare_kernel(
    state_far,
    cot_far,
    first_far,
    second_far,
    bias_far,
    front_ref,
    back_ref,
    state_taps,
    cot_taps,
    fold,
    cot_planes,
    wide,
    lines,
    product,
    state_ref,
    cot_ref,
    first_ref,
    second_ref,
    bias_ref,
    semaphores,
):
    rows = state_ref.shape[0]
    near = (first_ref, second_ref, bias_ref, state_ref, cot_ref)
    far = (first_far, second_far, bias_far, state_far, cot_far)
    copies = fetch(zip(far, near), semaphores)
    for copy in copies[:3]:
        copy.wait()
    for which in range(2):
        lines[...] = jnp.zeros_like(lines)
        for lon in range(3):
            for lat in range(3):
                start = 8 * lon + 2 * lat
                if which == 0:
                    lines[start : start + 2, :] = first_ref[lon, lat]
                else:
                    lines[start : start + 2, :] = second_ref[2 - lon, 2 - lat]
        if which == 0:
            lines[14:15, :] = bias_ref[...]
        front_ref[which] = front_stack(lines)
        lines[...] = jnp.zeros_like(lines)
        for lon in range(3):
            for lat in range(3):
                start = 8 * lat + 2 * lon
                if which == 0:
                    lines[start : start + 2, :] = first_ref[2 - lon, 2 - lat]
                else:
                    lines[start : start + 2, :] = second_ref[lon, lat]
        back_ref[which] = back_stack(lines)

    put_ones(wide, 1.0)
    for copy in copies[3:]:
        copy.wait()
    for main_ref, tap_ref in ((state_ref, state_taps), (cot_ref, cot_taps)):
        for var in range(2):
            plane = main_ref[:, var, :]
            if main_ref is cot_ref:
                cot_planes[var] = plane
            put_taps(wide, plane, 0, var)
        stack_taps(wide, tap_ref)

    for first in range(0, rows - 2, BATCH):
        batch = range(first, min(first + BATCH, rows - 2))
        hidden = backward_rows(
            front_ref, [(window_of(state_taps, row), window_of(cot_taps, row)) for row in batch]
        )
        fold_rows(hidden, back_ref[0], product, [row + 2 for row in batch])
    fold_lats(product, fold, 2, rows - 2)


def gradient_kernel(
    core_ref,
    half_ref,
    cot_planes,
    partner_ref,
    neighbour_ref,
    front_ref,
    back_ref,
    state_taps,
    cot_taps,
    fold_ref,
    out_ref,
    wide,
    edge,
    state_frame,
    cot_frame,
    product,
    fold,
):
    rows = cot_planes.shape[1]
    before_ref, after_ref = edges(core_ref, partner_ref, neighbour_ref)
    put_ones(wide, 1.0)
    for var_from, tap_ref, frame_ref in ((0, state_taps, state_frame), (2, cot_taps, cot_frame)):
        fill_edges(before_ref, after_ref, var_from, wide)
        stack_taps(wide, edge)
        bands(tap_ref, edge, frame_ref)
    fold[...] = fold_ref[...]
    hidden = backward_rows(
        front_ref, [(window_of(state_frame, at), window_of(cot_frame, at)) for at in (0, 1, 4, 5)]
    )
    fold_rows(hidden, back_ref[0], product, (0, 1, rows, rows + 1))
    fold_lats(product, fold, 0, 2)
    fold_lats(product, fold, rows, 2)
    for var in range(2):
        plane = cot_planes[var] + folded(fold, rows, var)
        plane = jnp.where(half_ref[0] == 0, plane[:, 128:], plane[:, :256]).astype(BF)
        for pair in range(out_ref.shape[0] // 2):
            out_ref[2 * pair + var] = plane


def slopes_kernel(
    core_ref, partner_ref, neighbour_ref, front_ref, state_taps, out_ref, wide, edge, frame
):
    rows = out_ref.shape[0] - 2
    before_ref, after_ref = edges(core_ref, partner_ref, neighbour_ref)
    put_ones(wide, 1.0)
    fill_edges(before_ref, after_ref, 0, wide)
    stack_taps(wide, edge)
    bands(state_taps, edge, frame)

    windows = [window_of(frame, at) for at in (0, 1)]
    windows += [window_of(state_taps, row) for row in range(rows - 2)]
    windows += [window_of(frame, at) for at in (4, 5)]
    for first in range(0, rows + 2, BATCH):
        batch = range(first, min(first + BATCH, rows + 2))
        dots = [jnp.dot(front_ref[0], windows[row](), preferred_element_type=F32) for row in batch]
        for row, value in zip(batch, dots):
            active = jnp.tanh(value)
            out_ref[row] = 1.0 - active * active


def response_kernel(
    scale,
    copies_ref,
    slopes_ref,
    front_ref,
    back_ref,
    incr_out,
    resp_out,
    wide,
    incr_taps,
    product,
    fold,
):
    rows = incr_out.shape[0]
    half = (rows + 2) // 2
    planes = []
    put_ones(wide, 0.0)
    groups = copies_ref.shape[0]
    lines = rows + 4
    for var in range(2):
        values = [
            copies_ref[group, pl.ds(2 * var * lines, 2 * lines), :].astype(F32)
            for group in range(groups)
        ]
        lower = sum(value for group, value in enumerate(values) if (group // 2) % 2 == 0)
        upper = sum(value for group, value in enumerate(values) if (group // 2) % 2 == 1)
        middle = (lower + upper)[lines:]
        plane = jnp.concatenate([lower[:lines], middle, upper[:lines]], axis=1)
        plane = plane * scale
        planes.append(plane)
        put_taps(wide, plane, 0, var)
    stack_taps(wide, incr_taps)

    for part in range(2):
        batch = range(part * half, (part + 1) * half)
        hidden = [
            jnp.dot(front_ref[0], window_of(incr_taps, row)(), preferred_element_type=F32)
            for row in batch
        ]
        hidden = [slopes_ref[row] * value for row, value in zip(batch, hidden)]
        fold_rows(hidden, back_ref[1], product, batch)
    fold_lats(product, fold, 0, rows + 2)
    for var in range(2):
        increment = planes[var][2 : 2 + rows]
        incr_out[:, var, :] = increment
        resp_out[:, var, :] = increment + folded(fold, rows, var)


def planes_kernel(core_ref, members_far, *refs):
    *outs, near, lines, planes, in_semaphores, out_semaphores = refs
    core = core_ref[0]
    count, tiles, lines_count = near.shape[:3]
    rows = lines_count // 2
    merged = members_far.reshape(count, lines_count, tiles * 128)
    pairs = [
        (merged.at[member, :, pl.ds(tile * 128, 128)], near.at[member, tile])
        for member in range(count)
        for tile in range(tiles)
    ]
    arrivals = fetch(pairs, in_semaphores)
    departures = []
    for member in range(count):
        for tile in range(tiles):
            arrivals[member * tiles + tile].wait()
            lines[...] = near[member, tile].astype(F32)
            window = pl.ds(tile * 128, 128)
            planes[member, :, window] = lines[pl.ds(core, rows, stride=2), :].astype(BF)
            planes[count + member, :, window] = lines[pl.ds(1 - core, rows, stride=2), :].astype(BF)
        for slot in (count + member, member):
            copy = pltpu.make_async_copy(planes.at[slot], outs[slot], out_semaphores.at[slot])
            copy.start()
            departures.append(copy)
    for copy in departures:
        copy.wait()


def member_kernel(span, count, half_ref, *refs):
    far_refs = refs[:count]
    *field_refs, lat_far, lon_far, out_ref, field, banded, total, held, lat_ref, lon_ref, semaphores = refs[count:]
    lons = field.shape[0]
    blocks = out_ref.shape[0]
    rows = lons // blocks
    reach, wide = lat_ref.shape
    half = half_ref[0]
    offset = pl.multiple_of(half * 128, 128)
    if reach == 256:
        source = pl.ds(offset, reach)
    else:
        source = pl.ds(0, reach)
    target = pl.ds(offset, wide)
    member_refs = [held.at[index] for index in range(len(far_refs))]
    pairs = [(lat_far.at[half], lat_ref), (lon_far, lon_ref)]
    pairs += [(far.at[:, source], near) for far, near in zip(far_refs, member_refs)]
    copies = fetch(pairs, semaphores)
    bands_here, copies = copies[:2], copies[2:]
    if reach == 256:
        field[...] = field_refs[0][...].astype(F32)
    else:
        field[:, pl.ds(pl.multiple_of(128 - half * 128, 128), 256)] = field_refs[0][...].astype(F32)
        field[:, pl.ds(pl.multiple_of(half * 256, 128), 128)] = field_refs[1][...].astype(F32)
    for copy in bands_here:
        copy.wait()
    lat_loc = lat_ref[...]
    chunk = 2 * span
    for index, member_ref in enumerate(member_refs):
        copies[index].wait()
        at = index * wide
        for start in range(0, lons, chunk):
            window = pl.ds(start, chunk)
            product = (member_ref[window, :].astype(F32) * field[window, :]).astype(BF)
            banded[pl.ds(HALF + start, chunk), at : at + wide] = jnp.dot(
                product, lat_loc, preferred_element_type=F32
            ).astype(BF)
    banded[pl.ds(0, HALF), :] = banded[pl.ds(lons, HALF), :]
    banded[pl.ds(HALF + lons, HALF), :] = banded[pl.ds(HALF, HALF), :]
    for start in range(0, lons, span):
        value = None
        for index, member_ref in enumerate(member_refs):
            at = index * wide
            spread = jnp.dot(
                lon_ref[...],
                banded[pl.ds(start, span + 2 * HALF), at : at + wide],
                preferred_element_type=F32,
            )
            term = member_ref[pl.ds(start, span), target].astype(F32) * spread
            value = term if value is None else value + term
        if wide > 128:
            value = jnp.where(half == 0, value, pltpu.roll(value, 128, 1))
        total[pl.ds(8 + start, span), :] = value
    total[pl.ds(0, 8), :] = total[pl.ds(lons, 8), :]
    total[pl.ds(lons + 8, 8), :] = total[pl.ds(8, 8), :]
    row = lax.broadcasted_iota(jnp.int32, (32, 128), 0)
    for block in range(blocks):
        top = 6 + block * rows
        if wide > 128:
            out_ref[block, pl.ds(0, rows + 4), :] = total[pl.ds(top, rows + 4), 0:128]
            out_ref[block, pl.ds(rows + 4, rows + 4), :] = total[pl.ds(top, rows + 4), 128:256]
        else:
            value = jnp.where(row < rows + 4, total[pl.ds(top, 32), :], 0.0)
            out_ref[block] = value.astype(BF)


def add_kernel(own_ref, other_ref, out_ref):
    for block in range(own_ref.shape[0]):
        outer = own_ref[block, 0:32, :] + other_ref[block].astype(F32)
        out_ref[block] = jnp.concatenate([outer, own_ref[block, 32:, :]], axis=0).astype(BF)


def sum_kernel(*refs):
    *parts_refs, out_ref = refs
    start = 0
    for parts_ref in parts_refs:
        lines, lats = parts_ref.shape[1:]
        for var in range(2):
            plane = parts_ref[var].astype(F32)
            for pair in range(1, parts_ref.shape[0] // 2):
                plane = plane + parts_ref[2 * pair + var].astype(F32)
            plane = plane.astype(BF)
            for group in range(out_ref.shape[0]):
                out_ref[group, pl.ds(var * lines, lines), pl.ds(start, lats)] = plane
        start += lats


def shape_of(*dims):
    return jax.ShapeDtypeStruct(dims, BF)


def wide_of(*dims):
    return jax.ShapeDtypeStruct(dims, F32)


FAR = pl.BlockSpec(memory_space=pltpu.HBM)
SCALAR = pl.BlockSpec(memory_space=pltpu.SMEM)
NEAR = pl.BlockSpec(memory_space=pltpu.VMEM)
PARAMS = pltpu.CompilerParams(vmem_limit_bytes=24 << 20)


def remote(value):
    return pltpu.with_memory_space_constraint(value, pltpu.HBM)


def padded_scratch(count, lats):
    return pltpu.VMEM((lats // 128, count * 8, 128), F32)


def tap_scratch(count, lats):
    return pltpu.VMEM((count * GROUP, lats), BF)


def prepare(state, cotangent, first, second, bias):
    rows, var_count, lats = state.shape
    hidden = first.shape[-1]
    operands = (state, cotangent, first, second, bias.reshape(1, hidden))
    return pl.pallas_call(
        prepare_kernel,
        out_shape=[
            shape_of(2, hidden, 3 * GROUP),
            shape_of(2, 48, 2 * hidden),
            shape_of(rows * GROUP, lats),
            shape_of(rows * GROUP, lats),
            wide_of(lats // 128, (rows + 2) * 8, 128),
            wide_of(var_count, rows, lats),
        ],
        in_specs=[FAR] * 5,
        scratch_shapes=[
            padded_scratch(rows, lats),
            pltpu.VMEM((24, hidden), F32),
            pltpu.VMEM((3, (rows + 2) * 8, lats), F32),
            pltpu.VMEM(state.shape, F32),
            pltpu.VMEM(state.shape, F32),
            pltpu.VMEM(first.shape, F32),
            pltpu.VMEM(second.shape, F32),
            pltpu.VMEM((1, hidden), F32),
            pltpu.SemaphoreType.DMA((5,)),
        ],
        compiler_params=PARAMS,
        cost_estimate=pl.CostEstimate(
            flops=2_000_000_000, bytes_accessed=3_000_000, transcendentals=1_100_000
        ),
        name="prepare",
    )(*[remote(value) for value in operands])


def gradient_planes(
    blocks, core, half, cot_planes, partner, neighbour, front, back, state_taps, cot_taps, partial
):
    var_count, rows, lats = cot_planes.shape
    return pl.pallas_call(
        gradient_kernel,
        out_shape=shape_of(blocks, rows, 256),
        in_specs=[SCALAR] * 2 + [NEAR] * 8,
        scratch_shapes=[
            padded_scratch(4, lats),
            tap_scratch(4, lats),
            tap_scratch(8, lats),
            tap_scratch(8, lats),
            pltpu.VMEM((3, (rows + 2) * 8, lats), F32),
            padded_scratch(rows + 2, lats),
        ],
        compiler_params=PARAMS,
        cost_estimate=pl.CostEstimate(
            flops=400_000_000, bytes_accessed=1_500_000, transcendentals=200_000
        ),
        name="gradient",
    )(core, half, cot_planes, partner, neighbour, front, back, state_taps, cot_taps, partial)


def member_planes(core, members):
    count, lons, var_count, lats = members.shape
    results = pl.pallas_call(
        planes_kernel,
        in_specs=[SCALAR, FAR],
        out_specs=[FAR] * (2 * count),
        out_shape=[pltpu.HBM((lons, lats), BF)] * (2 * count),
        scratch_shapes=[
            pltpu.VMEM((count, lats // 128, lons * var_count, 128), BF),
            pltpu.VMEM((lons * 2, 128), F32),
            pltpu.VMEM((2 * count, lons, lats), BF),
            pltpu.SemaphoreType.DMA((count * (lats // 128),)),
            pltpu.SemaphoreType.DMA((2 * count,)),
        ],
        compiler_params=PARAMS,
        cost_estimate=pl.CostEstimate(flops=0, bytes_accessed=10_000_000, transcendentals=0),
        name="planes",
    )(core, remote(members))
    return list(results[:count]), list(results[count:])


def hidden_slopes(core, partner, neighbour, front, state_taps):
    rows = state_taps.shape[0] // GROUP
    hidden, lats = front.shape[1], state_taps.shape[1]
    return pl.pallas_call(
        slopes_kernel,
        out_shape=pltpu.HBM((rows + 2, hidden, lats), F32),
        in_specs=[SCALAR] + [NEAR] * 4,
        out_specs=NEAR,
        scratch_shapes=[padded_scratch(4, lats), tap_scratch(4, lats), tap_scratch(8, lats)],
        compiler_params=PARAMS,
        cost_estimate=pl.CostEstimate(
            flops=1_000_000_000, bytes_accessed=6_000_000, transcendentals=1_200_000
        ),
        name="slopes",
    )(core, partner, neighbour, front, state_taps)


def member_sums(blocks, half, kept, taken, fields, wide):
    lons, lats = kept[0].shape
    rows = lons // blocks
    span = 96
    count = len(kept) + len(taken)
    reach = 256 if wide == 128 else lats
    source, target = np.arange(reach), np.arange(wide)
    lat_loc = jnp.asarray(
        np.stack([taps(np.abs(source[:, None] - 128 * at - target[None, :])) for at in range(2)])
    )
    lon_loc = jnp.asarray(
        taps(np.abs(np.arange(span)[:, None] + HALF - np.arange(span + 2 * HALF)[None, :]))
    )
    out_shape = shape_of(blocks, 32, 128) if wide == 128 else wide_of(blocks, 2 * (rows + 4), 128)
    return pl.pallas_call(
        functools.partial(member_kernel, span, count),
        in_specs=[SCALAR]
        + [FAR] * len(kept)
        + [pl.BlockSpec(memory_space=pl.ANY)] * len(taken)
        + [NEAR] * len(fields)
        + [FAR] * 2,
        out_shape=out_shape,
        scratch_shapes=[
            pltpu.VMEM((lons, reach), F32),
            pltpu.VMEM((lons + 2 * HALF, count * wide), BF),
            pltpu.VMEM((lons + 16, wide), F32),
            pltpu.VMEM((count, lons, reach), BF),
            pltpu.VMEM((reach, wide), BF),
            pltpu.VMEM((span, span + 2 * HALF), BF),
            pltpu.SemaphoreType.DMA((count + 2,)),
        ],
        compiler_params=PARAMS,
        cost_estimate=pl.CostEstimate(
            flops=wide * 16_000_000, bytes_accessed=4_000_000, transcendentals=0
        ),
        name="members",
    )(half, *[remote(value) for value in kept], *taken, *fields, remote(lat_loc), remote(lon_loc))


def add_parts(own, other):
    return pl.pallas_call(
        add_kernel,
        out_shape=shape_of(*own.shape),
        compiler_params=PARAMS,
        name="add_parts",
    )(own, other)


def block_sums(groups, arrived):
    lines = arrived[0].shape[1]
    lats = sum(part.shape[2] for part in arrived)
    return pl.pallas_call(
        sum_kernel,
        out_shape=shape_of(groups, 2 * lines, lats),
        compiler_params=PARAMS,
        name="block_sum",
    )(*arrived)


def responses(scale, copies, slopes, front, back):
    rows = slopes.shape[0] - 2
    hidden, lats = slopes.shape[1:]
    return pl.pallas_call(
        functools.partial(response_kernel, scale),
        out_shape=[wide_of(rows, 2, lats)] * 2,
        in_specs=[NEAR] * 4,
        scratch_shapes=[
            padded_scratch(rows + 4, lats),
            tap_scratch(rows + 4, lats),
            pltpu.VMEM((3, (rows + 2) * 8, lats), F32),
            padded_scratch(rows + 2, lats),
        ],
        compiler_params=PARAMS,
        name="response",
    )(copies, slopes, front, back)


def per_device(members, state, cotangent, conv_in, conv_out, bias):
    blocks = lax.axis_size("space")
    groups = lax.axis_size("mem")
    held, lons, var_count, lats = members.shape
    core = lax.axis_index("space") % 2
    swap = [(i, i ^ 1) for i in range(blocks)]
    chain = [(i, (i + 1 if i % 2 else i - 1) % blocks) for i in range(blocks)]
    tail = jnp.concatenate([state[-2:], cotangent[-2:]], axis=1)
    head = jnp.concatenate([state[:2], cotangent[:2]], axis=1)
    neighbour = lax.ppermute(jnp.where(core == 0, head, tail), "space", chain)
    partner = lax.ppermute(jnp.where(core == 0, tail, head), "space", swap)
    core = core.reshape(1)
    parity = (lax.axis_index("mem") // 2) % 2
    half = parity.reshape(1)
    first = jnp.transpose(conv_in, (0, 1, 3, 2))
    front, back, state_taps, cot_taps, partial, cot_planes = prepare(
        state, cotangent, first, conv_out, bias
    )
    outgoing = gradient_planes(
        blocks, core, half, cot_planes, partner, neighbour, front, back, state_taps, cot_taps, partial
    )
    members, outgoing = lax.optimization_barrier((members, outgoing))
    gathered = lax.all_to_all(outgoing, "space", 0, 0, tiled=True)
    kept, given = member_planes(core, members)
    taken = [lax.ppermute(give, "space", swap) for give in given]
    slopes = hidden_slopes(core, partner, neighbour, front, state_taps)
    gathered, slopes = lax.optimization_barrier((gathered, slopes))
    across = [(i, i ^ 2) for i in range(groups)]
    inner = gathered.reshape(lons, 256)
    outer = lax.ppermute(jnp.where(parity == 0, inner[:, 128:], inner[:, :128]), "mem", across)
    theirs = member_sums(blocks, 1 - half, kept, taken, [inner], 128)
    theirs, inner = lax.optimization_barrier((theirs, inner))
    other = lax.ppermute(theirs, "mem", across)
    own = member_sums(blocks, half, kept, taken, [inner, outer], 256)
    arrived = [lax.all_to_all(add_parts(own, other), "space", 0, 0, tiled=True)]
    spread = block_sums(groups, arrived)
    copies = lax.all_to_all(spread, "mem", 0, 0, tiled=True)
    member_count = held * blocks * groups
    increment, response = responses(1.0 / (member_count - 1.0), copies, slopes, front, back)
    return (increment, response)


def solution(mesh):
    in_specs = (
        P(("space", "mem"), None, None, None),
        P("space", None, None),
        P("space", None, None),
        P(),
        P(),
        P(),
    )
    out_specs = (P("space", None, None), P("space", None, None))
    return jax.shard_map(
        per_device, mesh=mesh, in_specs=in_specs, out_specs=out_specs, check_vma=False
    )
```
